128 devices in a mesh: ctx: 8 (over x_lo, z), tp: 16 (over x_hi, y, core).
Axes of the slice: x: 4 (x_hi: 2, x_lo: 2; x = x_hi * 2 + x_lo), y: 4, z: 4, core: 2. Of those that a mesh axis runs over, the one named last changes fastest.
Arguments:
- token_ids: int32 [16384], P('ctx'), may hold values from 0 to 15
- embedding: bfloat16 [16, 2048], P(None, 'tp'), may hold values from -64 to 64
- norm_gain: float32 [2048], P('tp'), may hold values from 0.25 to 1.75
- proj_blocks: bfloat16 [16, 128, 384], P('tp'), may hold values from -0.5 to 0.5
- proj_mixers: bfloat16 [3, 128, 16, 16], P(None, 'tp'), may hold values from -1.5 to 1.5
- out_blocks: bfloat16 [16, 128, 128], P('tp'), may hold values from -0.5 to 0.5
- out_mixers: bfloat16 [128, 16, 16], P('tp'), may hold values from -1.5 to 1.5
- filters: bfloat16 [2048, 16384], P('tp', 'ctx'), may hold values from -2 to 2
- cotangent: bfloat16 [2048, 16384], P('tp', 'ctx'), may hold values from -1 to 1
Outputs:
- layer_out: bfloat16 [2048, 16384], P('tp', 'ctx')
- filter_grad: float32 [2048, 16384], P('tp', 'ctx')
- embed_grad: float32 [16, 2048], P(None, 'tp')
- gain_grad: float32 [2048], P('tp')
The draws below stay inside these ranges and needn't reach their ends.
All inputs are finite; a program needn't handle non-finite values.
Results may differ from the reference program's by a relative error of at most 0.0097.
Values may be sent and summed in bfloat16 or wider, within the bound.
A program may use at most 64 MiB of HBM per device.

```python
import math
import jax
import jax.numpy as jnp
import numpy as np
from jax import lax

MODEL_WIDTH = 2048
BS = 128
VOCAB = 16
NB = 16
SEQUENCE_LENGTH = 16384


def draw_filters(key, part):
    random_splits = jax.random.split(key, 4)
    decay_length = jnp.exp(jax.random.uniform(random_splits[0], (MODEL_WIDTH, 1), minval=math.log(16.0), maxval=math.log(SEQUENCE_LENGTH * SEQUENCE_LENGTH / 64.0 + 32.0)))
    lag_float = jnp.arange(SEQUENCE_LENGTH, dtype=jnp.float32)[None, :]
    delay_index = jnp.arange(SEQUENCE_LENGTH, dtype=jnp.int32)[None, :]
    envelope = jnp.exp(-lag_float / decay_length)
    spike_start = jax.random.randint(random_splits[1], (MODEL_WIDTH, 3), 1, SEQUENCE_LENGTH)
    spike_mask = jax.random.uniform(random_splits[2], (MODEL_WIDTH, 3), minval=0.5, maxval=0.8)
    kept_values = jnp.ones((MODEL_WIDTH, SEQUENCE_LENGTH), jnp.float32)
    for spike_position in range(3):
        kept_values = kept_values * jnp.where(delay_index >= spike_start[:, spike_position:spike_position + 1], spike_mask[:, spike_position:spike_position + 1], 1.0)
    amplitude = 1.0 / jnp.sqrt(1.0 + jnp.minimum(decay_length / 2.0, SEQUENCE_LENGTH * 1.0))
    jitter = jnp.clip(jax.random.normal(random_splits[3], (MODEL_WIDTH, SEQUENCE_LENGTH)), -4.0, 4.0)
    kernel = amplitude * envelope * kept_values * jitter
    return jnp.clip(kernel, -2.0, 2.0).astype(jnp.bfloat16)


def draw_embedding(key, part):
    random_splits = jax.random.split(key, 4)
    column_place = jnp.arange(MODEL_WIDTH, dtype=jnp.float32)[None, :] / MODEL_WIDTH
    column_scale = jnp.exp(jax.random.uniform(random_splits[0], (1, MODEL_WIDTH), minval=math.log(0.3), maxval=math.log(3.0)))
    column_scale = column_scale * jnp.exp(math.log(3.0) * (column_place - 0.5))
    row_scale = jnp.exp(jax.random.uniform(random_splits[1], (VOCAB, 1), minval=math.log(0.3), maxval=math.log(3.0)))
    jitter = jnp.clip(jax.random.normal(random_splits[3], (VOCAB, MODEL_WIDTH)), -4.0, 4.0)
    return (row_scale * column_scale * jitter).astype(jnp.bfloat16)


def draw_cotangent(key, part):
    random_splits = jax.random.split(key, 1)
    position = jnp.arange(SEQUENCE_LENGTH, dtype=jnp.float32)[None, :] / SEQUENCE_LENGTH
    growth = jnp.exp(math.log(3.0) * position) * (0.5 / math.sqrt(SEQUENCE_LENGTH))
    jitter = jnp.clip(jax.random.normal(random_splits[0], (MODEL_WIDTH, SEQUENCE_LENGTH)), -4.0, 4.0)
    return (growth * jitter).astype(jnp.bfloat16)


def place_ends(values, own_key, smallest, high):
    dims = values.shape
    spot = [jax.random.randint(jax.random.fold_in(own_key, axis), (), 0, dims[axis]) for axis in range(len(dims))]
    values = values.at[tuple(spot)].set(smallest)
    longest = dims.index(max(dims))
    spot[longest] = (spot[longest] + 1) % dims[longest]
    return values.at[tuple(spot)].set(high)


def block_levels(stream_key, dims, cuts, least, top_value):
    def one(axis_at, blocks):
        draws = jax.random.uniform(jax.random.fold_in(jax.random.fold_in(stream_key, 6), axis_at), (blocks,), jnp.float32, least / len(cuts), top_value / len(cuts))
        return jnp.repeat(jnp.exp(draws), dims[axis_at] // blocks).reshape((-1,) + (1,) * (len(dims) - axis_at - 1))

    level = one(*cuts[0])
    for cut in cuts[1:]:
        level = level * one(*cut)
    return level


def rank_table(number_of, slope):
    weights = [(1 << 20) // math.isqrt(rank ** slope) + 1 for rank in range(1, number_of + 1)]
    width = 1 + sum(weights) // (1 << 30)
    return np.cumsum(np.array([max(1, weight // width) for weight in weights]))


def ranked_ids(own_key, extent, number_of, skew):
    listing = rank_table(number_of, skew)
    pick = jax.random.randint(jax.random.fold_in(own_key, 1), extent, 0, int(listing[number_of - 1]))
    rank = jnp.searchsorted(jnp.asarray(listing, jnp.int32), pick, side="right")
    return jax.random.permutation(jax.random.fold_in(own_key, 2), number_of)[rank].astype(jnp.int32)


def gaussian(rng, extent, deviation, most, cuts=(), held_as=jnp.bfloat16):
    loudness = block_levels(rng, extent, cuts, -0.22, 0.18) if cuts else 1.0
    values = jax.random.normal(rng, extent, jnp.float32) * deviation * loudness
    return jnp.minimum(jnp.maximum(values, -most), most).astype(held_as)


def setup_inputs(seed: int = 0) -> dict:
    arg_keys = jax.random.split(jax.random.key(seed), 10)
    token_ids = place_ends(ranked_ids(arg_keys[0], (SEQUENCE_LENGTH,), VOCAB, 2), jax.random.fold_in(arg_keys[0], 3), 0, VOCAB - 1).astype(jnp.int32)
    embedding = draw_embedding(jax.random.fold_in(arg_keys[9], 71), 0)
    norm_gain = jnp.clip(1.0 + 0.15 * jax.random.normal(arg_keys[2], (MODEL_WIDTH,), jnp.float32), 0.25, 1.75)
    proj_blocks = gaussian(arg_keys[3], (NB, BS, 3 * BS), BS ** -0.5, 0.5, ((0, 16),))
    proj_mixers = gaussian(arg_keys[4], (3, BS, NB, NB), NB ** -0.5, 1.5, ((1, 16),))
    out_blocks = gaussian(arg_keys[5], (NB, BS, BS), BS ** -0.5, 0.5, ((0, 16),))
    out_mixers = gaussian(arg_keys[6], (BS, NB, NB), NB ** -0.5, 1.5, ((0, 16),))
    filters = draw_filters(jax.random.fold_in(arg_keys[9], 71), 0)
    cotangent = draw_cotangent(jax.random.fold_in(arg_keys[9], 71), 0)
    return dict(token_ids=token_ids, embedding=embedding, norm_gain=norm_gain, proj_blocks=proj_blocks, proj_mixers=proj_mixers, out_blocks=out_blocks, out_mixers=out_mixers, filters=filters, cotangent=cotangent)


epsilon = 1e-06
precise = lax.Precision.HIGHEST

def even_spectrum(kernel_rows, full_span):
    return 2.0 * jnp.real(jnp.fft.rfft(kernel_rows.astype(jnp.float32), n=full_span, axis=1))

def forward_block(operands):
    gated_rows, kernel_rows = operands
    length = gated_rows.shape[1]
    full_span = 2 * length
    spectrum = even_spectrum(kernel_rows, full_span)
    gated_spectrum = jnp.fft.rfft(gated_rows.astype(jnp.float32), n=full_span, axis=1)
    result = jnp.fft.irfft(gated_spectrum * spectrum, n=full_span, axis=1)
    return result[:, :length].astype(jnp.bfloat16)

def backward_block(operands):
    gated_rows, kernel_rows, grad_rows = operands
    length = gated_rows.shape[1]
    full_span = 2 * length
    spectrum = even_spectrum(kernel_rows, full_span)
    gated_spectrum = jnp.fft.rfft(gated_rows.astype(jnp.float32), n=full_span, axis=1)
    grad_spectrum = jnp.fft.rfft(grad_rows.astype(jnp.float32), n=full_span, axis=1)
    grad_gated = jnp.fft.irfft(grad_spectrum * spectrum, n=full_span, axis=1)[:, :length].astype(jnp.bfloat16)
    cross_spectrum = 2.0 * jnp.real(grad_spectrum * jnp.conj(gated_spectrum))
    kernel_grad = jnp.fft.irfft(cross_spectrum, n=full_span, axis=1)[:, :length]
    return (grad_gated, kernel_grad.astype(jnp.float32))

def reference(token_ids, embedding, norm_gain, proj_blocks, proj_mixers, out_blocks, out_mixers, filters, cotangent):
    embedded = embedding.astype(jnp.float32)[token_ids].T
    scaling = lax.rsqrt(lax.optimization_barrier(jnp.sum(embedded * embedded, axis=0)) / MODEL_WIDTH + epsilon)
    normed = (embedded * scaling[None, :] * norm_gain[:, None]).astype(jnp.bfloat16)
    section_one = jnp.einsum('gjt,gjk->kgt', normed.reshape(NB, BS, SEQUENCE_LENGTH).astype(jnp.float32), proj_blocks.astype(jnp.float32), precision=precise)
    section_one = section_one.astype(jnp.bfloat16).reshape(3, BS, NB, SEQUENCE_LENGTH)
    projected = jnp.einsum('pigt,pigm->pimt', section_one.astype(jnp.float32), proj_mixers.astype(jnp.float32), precision=precise).reshape(3, MODEL_WIDTH, SEQUENCE_LENGTH)
    gate_inner = projected[0]
    values = projected[1]
    gate_outer = projected[2]
    gated_tokens = (gate_inner * values).astype(jnp.bfloat16)
    filtered = lax.map(forward_block, (gated_tokens.reshape(NB, BS, SEQUENCE_LENGTH), filters.reshape(NB, BS, SEQUENCE_LENGTH))).reshape(MODEL_WIDTH, SEQUENCE_LENGTH)
    branch = (gate_outer * filtered.astype(jnp.float32)).astype(jnp.bfloat16)
    out_section = jnp.einsum('gjt,gji->igt', branch.reshape(NB, BS, SEQUENCE_LENGTH).astype(jnp.float32), out_blocks.astype(jnp.float32), precision=precise).astype(jnp.bfloat16)
    mixture = jnp.einsum('igt,igm->imt', out_section.astype(jnp.float32), out_mixers.astype(jnp.float32), precision=precise).reshape(MODEL_WIDTH, SEQUENCE_LENGTH)
    layer_out = (embedded + mixture).astype(jnp.bfloat16)
    back_pieces = jnp.einsum('igm,imt->igt', out_mixers.astype(jnp.float32), cotangent.reshape(BS, NB, SEQUENCE_LENGTH).astype(jnp.float32), precision=precise).astype(jnp.bfloat16)
    grad_branch = jnp.einsum('gji,igt->gjt', out_blocks.astype(jnp.float32), back_pieces.astype(jnp.float32), precision=precise).reshape(MODEL_WIDTH, SEQUENCE_LENGTH)
    grad_filtered = (grad_branch * gate_outer).astype(jnp.bfloat16)
    grad_outer = grad_branch * filtered.astype(jnp.float32)
    grad_gated, filter_grad = lax.map(backward_block, (gated_tokens.reshape(NB, BS, SEQUENCE_LENGTH), filters.reshape(NB, BS, SEQUENCE_LENGTH), grad_filtered.reshape(NB, BS, SEQUENCE_LENGTH)))
    grad_gated = grad_gated.reshape(MODEL_WIDTH, SEQUENCE_LENGTH)
    filter_grad = filter_grad.reshape(MODEL_WIDTH, SEQUENCE_LENGTH)
    grad_inner = grad_gated.astype(jnp.float32) * values
    grad_values = grad_gated.astype(jnp.float32) * gate_inner
    gradients = jnp.stack([grad_inner, grad_values, grad_outer]).reshape(3, BS, NB, SEQUENCE_LENGTH)
    grad_pieces = jnp.einsum('pigm,pimt->pigt', proj_mixers.astype(jnp.float32), gradients, precision=precise).astype(jnp.bfloat16)
    grad_normed = jnp.einsum('gjk,kgt->gjt', proj_blocks.astype(jnp.float32), grad_pieces.reshape(3 * BS, NB, SEQUENCE_LENGTH).astype(jnp.float32), precision=precise).reshape(MODEL_WIDTH, SEQUENCE_LENGTH)
    gain_grad = lax.optimization_barrier(jnp.sum(grad_normed * embedded * scaling[None, :], axis=1))
    cross_total = lax.optimization_barrier(jnp.sum(grad_normed * norm_gain[:, None] * embedded, axis=0))
    grad_embedded = cotangent.astype(jnp.float32) + scaling[None, :] * norm_gain[:, None] * grad_normed - embedded * (scaling * scaling * scaling * cross_total / MODEL_WIDTH)[None, :]
    embed_grad = jax.ops.segment_sum(grad_embedded.T, token_ids, num_segments=VOCAB)
    return (layer_out, filter_grad, embed_grad, gain_grad)
```

```python
import math

import jax
import jax.numpy as jnp
import numpy as np
from jax import lax
from jax.sharding import PartitionSpec as P

WIDTH = 2048
EPS = 1e-06
HI = lax.Precision.HIGHEST
SPAN = 32768
BF = jnp.bfloat16
F32 = jnp.float32


def tables():
    idx = np.arange(128)
    half = idx + 0.5
    first = 2 * np.pi * np.outer(half, idx) / 256.0
    c1 = np.concatenate([np.cos(first), -np.sin(first)], 0)
    twist = 2 * np.pi * np.outer(half, idx) / SPAN
    second = 2 * np.pi * (np.outer(idx, idx) % 128) / 128.0
    co, si = np.cos(second), np.sin(second)
    c2 = np.block([[co, -si], [si, co]])
    i1 = np.block([[co, si], [-si, co]])
    i2 = np.concatenate([np.cos(first.T), -np.sin(first.T)], 1) * (2.0 / SPAN)
    to = lambda a, d: jnp.asarray(a, F32).astype(d)
    return to(c1, BF), to(np.cos(twist), F32), to(np.sin(twist), F32), to(c2, BF), to(i1, BF), to(i2, BF)


def dot(formula, a, b):
    return jnp.einsum(formula, a.astype(BF), b.astype(BF), preferred_element_type=F32)


def forward(signal, consts, real_only=False):
    c1, tc, ts, c2, _, _ = consts
    a = dot("kq,cqr->ckr", c1, signal)
    re, im = a[:, :128], a[:, 128:]
    b = jnp.concatenate([re * tc + im * ts, im * tc - re * ts], axis=2)
    return dot("cks,sj->ckj", b, c2[:, :128] if real_only else c2)


def inverse(spectrum, consts):
    _, tc, ts, _, i1, i2 = consts
    u = dot("ckj,js->cks", spectrum, i1[: spectrum.shape[2]])
    re, im = u[:, :, :128], u[:, :, 128:]
    v = jnp.concatenate([re * tc - im * ts, im * tc + re * ts], axis=1)
    return dot("qk,ckr->cqr", i2, v)


def everyone(x, axis, count):
    return lax.all_to_all(jnp.broadcast_to(x[None], (count,) + x.shape), axis, 0, 0, tiled=True)


def local(token_ids, embedding, norm_gain, proj_blocks, proj_mixers, out_blocks, out_mixers, filters, cotangent):
    consts = tables()
    tokens = token_ids.shape[0]
    nctx, ntp = lax.axis_size("ctx"), lax.axis_size("tp")
    back_pieces = jnp.einsum(
        "igm,imt->igt", out_mixers, cotangent.reshape(8, 16, tokens), preferred_element_type=F32
    ).astype(BF)
    filter_parts = lax.all_to_all(filters.reshape(nctx, 16, 16, 128), "ctx", 0, 0, tiled=True)
    filter_whole = filter_parts.transpose(1, 0, 2, 3).reshape(16, 128, 128)
    back_section = lax.all_to_all(back_pieces, "tp", split_axis=1, concat_axis=0, tiled=True)
    grad_branch = jnp.einsum(
        "ji,it->jt", out_blocks[0], back_section.reshape(128, tokens), preferred_element_type=F32
    )
    all_ids = everyone(token_ids, "ctx", nctx).reshape(nctx * tokens)
    ids16 = lax.broadcasted_iota(jnp.int32, (16, tokens), 0)
    one_hot = (token_ids[None, :] == ids16).astype(F32)
    emb = embedding.astype(F32)
    squares = jnp.sum(everyone(jnp.sum(emb * emb, axis=1), "tp", ntp).reshape(ntp, 16), axis=0)
    scaling = lax.rsqrt(squares / WIDTH + EPS)
    normed = (emb * scaling[:, None] * norm_gain[None, :]).astype(BF)
    first = jnp.einsum("vj,jk->kv", normed, proj_blocks[0], preferred_element_type=F32).astype(BF)
    pieces = lax.all_to_all(first.reshape(3, 128, 1, 16), "tp", split_axis=1, concat_axis=2, tiled=True)
    table = jnp.einsum("pigv,pigm->pimv", pieces, proj_mixers, preferred_element_type=F32).reshape(3, 128, 16)
    gated_table = (table[0] * table[1]).astype(BF)
    here = lax.axis_index("ctx")
    mine = lax.dynamic_slice_in_dim(gated_table, here * 16, 16, 0)
    all_hot = (all_ids[None, :] == lax.broadcasted_iota(jnp.int32, (16, nctx * tokens), 0)).astype(BF)
    gated = dot("cv,vt->ct", mine, all_hot).astype(BF).reshape(16, 128, 128)
    gate_outer = jnp.einsum("cv,vt->ct", table[2], one_hot, precision=HI)
    grad_filtered = (grad_branch * gate_outer).astype(BF)
    grad_parts = lax.all_to_all(grad_filtered.reshape(nctx, 16, 16, 128), "ctx", 0, 0, tiled=True)
    grad_whole = grad_parts.transpose(1, 0, 2, 3).reshape(16, 128, 128)
    even = 2.0 * forward(filter_whole, consts, True)
    even2 = jnp.concatenate([even, even], axis=2)
    spec_x = forward(gated, consts)
    filtered_whole = inverse(spec_x * even2, consts).astype(BF)
    filtered = lax.all_to_all(
        filtered_whole.reshape(16, nctx, 16, 128).transpose(1, 0, 2, 3), "ctx", 0, 0, tiled=True
    ).reshape(128, tokens)
    branch = (gate_outer * filtered).astype(BF)
    out_section = jnp.einsum("jt,ji->it", branch, out_blocks[0], preferred_element_type=F32).astype(BF)
    out_pieces = lax.all_to_all(out_section.reshape(128, 1, tokens), "tp", 0, 1, tiled=True)
    mixture = jnp.einsum("igt,igm->imt", out_pieces, out_mixers, preferred_element_type=F32).reshape(128, tokens)
    embedded = jnp.einsum("vc,vt->ct", embedding, one_hot.astype(BF), preferred_element_type=F32)
    layer_out = (embedded + mixture).astype(BF)
    spec_g = forward(grad_whole, consts)
    grad_gated = inverse(spec_g * even2, consts)
    cross = 2.0 * (spec_g[:, :, :128] * spec_x[:, :, :128] + spec_g[:, :, 128:] * spec_x[:, :, 128:])
    kernel_whole = inverse(cross, consts).astype(BF)
    filter_grad = (
        lax.all_to_all(kernel_whole.reshape(16, nctx, 16, 128).transpose(1, 0, 2, 3), "ctx", 0, 0, tiled=True)
        .reshape(128, tokens)
        .astype(F32)
    )
    gg = dot("ct,vt->cv", grad_gated.reshape(16, nctx * tokens), all_hot)
    gp2 = dot("ct,vt->cv", grad_branch * filtered, one_hot)
    ct = dot("ct,vt->cv", cotangent, one_hot)
    gg_all = everyone(gg, "ctx", nctx).reshape(128, 16)
    sums = jnp.sum(everyone(jnp.stack([gp2, ct]), "ctx", nctx).reshape(nctx, 2, 128, 16), axis=0)
    grads = jnp.stack([gg_all * table[1], gg_all * table[0], sums[0]]).reshape(3, 8, 16, 16)
    grad_first = jnp.einsum("pigm,pimv->pigv", proj_mixers.astype(F32), grads, precision=HI)
    grad_first = lax.all_to_all(grad_first, "tp", split_axis=2, concat_axis=1, tiled=True)
    grad_normed = jnp.einsum(
        "jk,kv->vj", proj_blocks[0].astype(F32), grad_first.reshape(384, 16), precision=HI
    )
    gain_grad = jnp.sum(grad_normed * emb * scaling[:, None], axis=0)
    cross_part = jnp.sum(grad_normed * norm_gain[None, :] * emb, axis=1)
    cross_total = jnp.sum(everyone(cross_part, "tp", ntp).reshape(ntp, 16), axis=0)
    embed_grad = (
        sums[1].T
        + scaling[:, None] * norm_gain[None, :] * grad_normed
        - emb * (scaling**3 * cross_total / WIDTH)[:, None]
    )
    return (layer_out, filter_grad, embed_grad, gain_grad)


def solution(mesh):
    in_specs = (
        P("ctx"),
        P(None, "tp"),
        P("tp"),
        P("tp", None, None),
        P(None, "tp", None, None),
        P("tp", None, None),
        P("tp", None, None),
        P("tp", "ctx"),
        P("tp", "ctx"),
    )
    out_specs = (P("tp", "ctx"), P("tp", "ctx"), P(None, "tp"), P("tp"))
    return jax.shard_map(local, mesh=mesh, in_specs=in_specs, out_specs=out_specs, check_vma=False)
```

```python
import jax
import jax.numpy as jnp
import numpy as np
from jax import lax
from jax.experimental import pallas as pl
from jax.experimental.pallas import tpu as pltpu
from jax.sharding import PartitionSpec as P

WIDTH = 2048
EPS = 1e-06
SPAN = 32768
NC = 8
NT = 16
BF = jnp.bfloat16
F32 = jnp.float32
MESH = pl.DeviceIdType.MESH

FILT_IN, TOK, GF, FILT, FG, GG, SEG = range(7)
BACK, SS, TAB, OUT, GT, CR = range(6)


def dft_tables():
    idx = np.arange(128)
    half = idx + 0.5
    first = 2 * np.pi * np.outer(half, idx) / 256.0
    c1 = np.concatenate([np.cos(first), -np.sin(first)], 0)
    twist = 2 * np.pi * np.outer(half, idx) / SPAN
    second = 2 * np.pi * (np.outer(idx, idx) % 128) / 128.0
    co, si = np.cos(second), np.sin(second)
    c2 = np.block([[co, -si], [si, co]])
    i1 = np.block([[co, si], [-si, co]])
    i2 = np.concatenate([np.cos(first.T), -np.sin(first.T)], 1) * (2.0 / SPAN)
    cast = lambda a, d: jnp.asarray(a, F32).astype(d)
    return (
        cast(c1, BF),
        cast(np.cos(twist), F32),
        cast(np.sin(twist), F32),
        cast(c2, BF),
        cast(i1, BF),
        cast(i2, BF),
    )


def mm(a, b):
    return jnp.dot(a, b, preferred_element_type=F32)


def mm_tn(a, b):
    return lax.dot_general(a, b, (((0,), (0,)), ((), ())), preferred_element_type=F32)


def mm_nt(a, b):
    return lax.dot_general(a, b, (((1,), (1,)), ((), ())), preferred_element_type=F32)


def iota2(rows, lanes):
    return (
        lax.broadcasted_iota(jnp.int32, (rows, lanes), 0),
        lax.broadcasted_iota(jnp.int32, (rows, lanes), 1),
    )


def ones_at(cond):
    return jnp.where(cond, 1.0, 0.0).astype(F32)


def split(x):
    hi = x.astype(BF)
    return hi, (x - hi.astype(F32)).astype(BF)


def kernel(
    tok_ref, emb_ref, gain_ref, blk_ref, mix_ref, oblk_ref, omix_ref, filt_ref, cot_ref,
    c1_ref, tc_ref, ts_ref, c2_ref, i1_ref, i2_ref,
    lay_ref, fgrad_ref, egrad_ref, ggrad_ref,
    r_filt, r_tok, s_gf, r_gf, s_fl, r_fl, s_fg, r_fg, s_gg, r_gg, s_seg, r_seg,
    s_back, r_back, s_ss, r_ss, s_tab, r_tab, s_out, r_out, s_gt, r_gt, s_cr, r_cr,
    w_back, w_two, r_mix, hot, tall, gated_t, grid_a, grid_b, spec_x, spec_s, outer, gbranch,
    ssem_c, rsem_c, ssem_t, rsem_t,
):
    a = lax.axis_index("ctx")
    b = lax.axis_index("tp")

    class Exchange:
        def __init__(self, axis, msg, src, dst):
            self.me, self.n = (a, NC) if axis == "ctx" else (b, NT)
            sends, recvs = (ssem_c, rsem_c) if axis == "ctx" else (ssem_t, rsem_t)

            def copy(k):
                peer = lax.rem(self.me + k, self.n)
                return pltpu.make_async_remote_copy(
                    src_ref=src(peer),
                    dst_ref=dst(self.me),
                    send_sem=sends.at[msg, k],
                    recv_sem=recvs.at[msg, k],
                    device_id={axis: peer},
                    device_id_type=MESH,
                )

            self.copy = copy

        def each(self, act):
            def body(k, carry):
                act(self.copy(k))
                return carry

            lax.fori_loop(1, self.n, body, 0)

        def start(self):
            self.each(lambda c: c.start())

        def recv(self):
            self.each(lambda c: c.wait_recv())

        def drain(self):
            self.each(lambda c: c.wait_send())

    rows16 = lambda ref: (lambda p: ref.at[pl.ds(pl.multiple_of(p * 16, 16), 16), :])
    slot = lambda ref: (lambda p: ref.at[p])
    whole = lambda ref: (lambda p: ref)

    x_filt = Exchange("ctx", FILT_IN, rows16(filt_ref), slot(r_filt))
    x_tok = Exchange("ctx", TOK, whole(tok_ref), slot(r_tok))
    x_gf = Exchange("ctx", GF, slot(s_gf), slot(r_gf))
    x_fl = Exchange("ctx", FILT, slot(s_fl), slot(r_fl))
    x_fg = Exchange("ctx", FG, slot(s_fg), slot(r_fg))
    x_gg = Exchange("ctx", GG, whole(s_gg), slot(r_gg))
    x_seg = Exchange("ctx", SEG, whole(s_seg), slot(r_seg))
    x_back = Exchange("tp", BACK, slot(s_back), slot(r_back))
    x_ss = Exchange("tp", SS, whole(s_ss), slot(r_ss))
    x_tab = Exchange("tp", TAB, slot(s_tab), slot(r_tab))
    x_out = Exchange("tp", OUT, slot(s_out), slot(r_out))
    x_gt = Exchange("tp", GT, slot(s_gt), slot(r_gt))
    x_cr = Exchange("tp", CR, whole(s_cr), slot(r_cr))

    barrier = pltpu.get_barrier_semaphore()

    def greet(axis, me, n):
        def body(k, carry):
            pl.semaphore_signal(
                barrier, inc=1, device_id={axis: lax.rem(me + k, n)}, device_id_type=MESH
            )
            return carry

        lax.fori_loop(1, n, body, 0)

    greet("ctx", a, NC)
    greet("tp", b, NT)

    row128, lane128 = iota2(128, 128)
    p_lane = lane128 >> 4

    row16, lane16 = iota2(16, 128)
    spread = ones_at(((lane16 & 15) == row16) & (lane16 < 48)).astype(BF)
    emb_t = mm_tn(emb_ref[...], spread)
    s_ss[...] = jnp.broadcast_to(jnp.sum(emb_t * emb_t, axis=0, keepdims=True), (8, 128))

    pl.semaphore_wait(barrier, NC - 1 + NT - 1)
    x_ss.start()
    x_tok.start()
    x_filt.start()
    r_ss[b] = s_ss[...]
    r_tok[a] = tok_ref[...]

    tile_m = ones_at((lane16 & 15) == row16).astype(BF)
    row, lane = iota2(256, 128)
    sel_row = ones_at(((row & 7) == (lane >> 4)) & ((row >> 4) == (lane & 15))).astype(BF)
    wide = mm(sel_row, mm(omix_ref[...], tile_m).astype(BF))
    row, lane = iota2(256, 256)
    keep = ((row & 7) == ((lane >> 4) & 7)) & (((row >> 3) & 1) == (lane >> 7))
    w_back[...] = jnp.where(keep, jnp.concatenate([wide, wide], axis=1), 0.0).astype(BF)
    cot2 = jnp.concatenate([cot_ref[:, :1024], cot_ref[:, 1024:]], axis=0)
    s_back[...] = mm(w_back[...], cot2).astype(BF).reshape(NT, 16, 1024)
    x_back.start()
    r_back[b] = s_back[b]
    r_filt[a] = filt_ref[pl.ds(pl.multiple_of(a * 16, 16), 16), :]

    sel_p = ones_at(((row128 & 7) == p_lane) & ((row128 >> 3) == (lane128 & 15))).astype(BF)
    for p in range(3):
        wide = mm(sel_p, mm(mix_ref[p * 128 : (p + 1) * 128, :], tile_m).astype(BF))
        r_mix[p] = jnp.where((row128 & 7) == p_lane, wide, 0.0).astype(BF)
    gain_row = gain_ref[...]
    gain_col = jnp.sum(jnp.where(row128 == lane128, gain_row, 0.0), axis=1, keepdims=True)

    x_ss.recv()
    total = jnp.sum(r_ss[...], axis=0)[0:1, :]
    scal_row = lax.rsqrt(total * (1.0 / WIDTH) + EPS)
    normed = emb_t * scal_row * gain_col
    first = jnp.zeros((128, 128), F32)
    for p in range(3):
        first += mm_tn(
            blk_ref[:, p * 128 : (p + 1) * 128], jnp.where(p_lane == p, normed, 0.0).astype(BF)
        )
    s_tab[...] = first.astype(BF).astype(F32).reshape(NT, 8, 128)
    x_tab.start()
    r_tab[b] = s_tab[b]

    row, lane = iota2(128, 256)
    sel_col = ones_at(((lane >> 4) * 8 + (lane & 7)) == row).astype(BF)
    wide = mm(oblk_ref[...], sel_col)
    low = ((lane >> 3) & 1) == 0
    w_two[...] = jnp.concatenate(
        [jnp.where(low, wide, 0.0), jnp.where(low, 0.0, wide)], axis=0
    ).astype(BF)

    x_tok.recv()
    for src in range(NC):
        ids = r_tok[src]
        for q in range(16):
            hot[src, :, q * 128 : (q + 1) * 128] = ones_at(
                jnp.broadcast_to(ids[q : q + 1, :], (16, 128)) == row16
            ).astype(BF)

    x_tab.recv()
    pieces = r_tab[...].reshape(128, 128)
    table = jnp.zeros((128, 128), F32)
    for p in range(3):
        table += mm_tn(r_mix[p], jnp.where(p_lane == p, pieces, 0.0).astype(BF))
    tall[...] = table
    gated_t[...] = table * pltpu.roll(table, 112, 1)
    outer_hi, outer_lo = split(pltpu.roll(table, 96, 1)[:, :16])
    outer_w = jnp.concatenate([outer_hi, outer_lo], axis=1)
    for h in range(2):
        hot_h = hot[a, :, h * 1024 : (h + 1) * 1024]
        outer[h * 128 : (h + 1) * 128, :] = mm(outer_w, jnp.concatenate([hot_h, hot_h], axis=0))

    x_back.recv()
    gbranch[...] = mm(w_two[...], r_back[...].reshape(256, 1024))
    for h in range(2):
        for s in range(8):
            part = slice(s * 128, (s + 1) * 128)
            hrow = slice(h * 128, (h + 1) * 128)
            grid_a[pl.ds(h * 8 + s, 128, stride=16), :] = gbranch[hrow, part] * outer[hrow, part]
    s_gf[...] = grid_a[...].astype(BF).reshape(NC, 16, 16, 128)
    x_gf.start()
    r_gf[a] = s_gf[a]

    mine = gated_t[pl.ds(pl.multiple_of(a * 16, 16), 16), :][:, :16].astype(BF)
    for src in range(NC):
        vals = mm(mine, hot[src])
        for q in range(16):
            grid_a[pl.ds(src * 16 + q, 16, stride=128), :] = vals[:, q * 128 : (q + 1) * 128]

    tc = tc_ref[...]
    ts = ts_ref[...]

    def forward(signal, second):
        first_stage = mm(c1_ref[...], signal)
        re, im = first_stage[:128], first_stage[128:]
        turned = jnp.concatenate([re * tc + im * ts, im * tc - re * ts], axis=1)
        return mm(turned.astype(BF), second)

    def inverse(spectrum, weights):
        back = mm(spectrum.astype(BF), weights)
        re, im = back[:, :128], back[:, 128:]
        turned = jnp.concatenate([re * tc - im * ts, im * tc + re * ts], axis=0)
        return mm(i2_ref[...], turned.astype(BF))

    def channels(step, body):
        def block(n, carry):
            for u in range(step):
                body(n * step + u)
            return carry

        lax.fori_loop(0, 16 // step, block, 0)

    def at_rows(ref, c):
        return ref.at[pl.ds(pl.multiple_of(c * 128, 128), 128), :]

    def gated_spectrum(c):
        spec_x[c] = forward(at_rows(grid_a, c)[...].astype(BF), c2_ref[...])

    channels(4, gated_spectrum)

    x_filt.recv()
    for src in range(NC):
        for q in range(16):
            grid_b[pl.ds(src * 16 + q, 16, stride=128), :] = r_filt[
                src, :, q * 128 : (q + 1) * 128
            ].astype(F32)

    def filtered_channel(c):
        even = 2.0 * forward(at_rows(grid_b, c)[...].astype(BF), c2_ref[:, :128])
        spec_s[c] = even
        spectrum = spec_x[c] * jnp.concatenate([even, even], axis=1)
        s_fl[:, c] = inverse(spectrum, i1_ref[...]).astype(BF).reshape(NC, 16, 128)

    channels(4, filtered_channel)
    x_fl.start()
    r_fl[a] = s_fl[a]

    x_gf.recv()

    def grad_channel(c):
        spec_g = forward(r_gf[:, c].reshape(128, 128), c2_ref[...])
        even = spec_s[c]
        prod = spec_g * spec_x[c]
        cross = 2.0 * (prod[:, :128] + prod[:, 128:])
        s_fg[:, c] = inverse(cross, i1_ref[:128, :]).astype(BF).reshape(NC, 16, 128)
        at_rows(grid_b, c)[...] = inverse(
            spec_g * jnp.concatenate([even, even], axis=1), i1_ref[...]
        )

    channels(2, grad_channel)
    x_fg.start()
    r_fg[a] = s_fg[a]

    sums = jnp.zeros((16, 32), F32)
    for src in range(NC):
        vals = jnp.concatenate(
            [grid_b[pl.ds(src * 16 + q, 16, stride=128), :] for q in range(16)], axis=1
        ).astype(BF)
        hot_s = hot[src]
        sums += mm_nt(vals, jnp.concatenate([hot_s, hot_s], axis=0))
    s_gg[...] = jnp.concatenate([sums, jnp.zeros((16, 96), F32)], axis=1)
    x_gg.start()
    r_gg[a] = s_gg[...]

    x_fl.recv()
    grid_a[...] = r_fl[...].reshape(2048, 128).astype(F32)
    gp2 = jnp.zeros((16, 128), F32)
    ctt = jnp.zeros((16, 128), F32)
    branch = []
    for h in range(2):
        hrow = slice(h * 128, (h + 1) * 128)
        filtered = jnp.concatenate(
            [grid_a[pl.ds(h * 8 + s, 128, stride=16), :] for s in range(8)], axis=1
        )
        branch.append((outer[hrow, :] * filtered).astype(BF))
        hot_h = hot[a, :, h * 1024 : (h + 1) * 1024]
        hi, lo = split(gbranch[hrow, :] * filtered)
        gp2 += mm_nt(hot_h, hi) + mm_nt(hot_h, lo)
        ctt += mm_nt(hot_h, cot_ref[:, h * 1024 : (h + 1) * 1024])
    s_out[...] = (
        mm_tn(w_two[...], jnp.concatenate(branch, axis=0)).astype(BF).reshape(NT, 16, 1024)
    )
    x_out.start()
    r_out[b] = s_out[b]
    s_seg[0] = gp2
    s_seg[1] = ctt
    x_seg.start()
    r_seg[a] = s_seg[...]

    x_gg.recv()
    x_seg.recv()
    seg = jnp.sum(r_seg[...], axis=0)
    ctt = seg[1]
    hi, rest = seg[0].astype(BF), seg[0] - seg[0].astype(BF).astype(F32)
    mid, low_part = split(rest)
    row48, lane48 = iota2(48, 128)
    place = ones_at(((row48 & 15) + 32) == lane48).astype(BF)
    gp2_t = mm_tn(jnp.concatenate([hi, mid, low_part], axis=0), place)
    table = tall[...]
    swapped = jnp.where(lane128 < 16, pltpu.roll(table, 112, 1), pltpu.roll(table, 16, 1))
    grads = jnp.where(lane128 < 32, r_gg[...].reshape(128, 128) * swapped, gp2_t)
    gfirst = jnp.zeros((128, 128), F32)
    for p in range(3):
        hi, lo = split(jnp.where(p_lane == p, grads, 0.0))
        gfirst += mm(r_mix[p], hi) + mm(r_mix[p], lo)
    s_gt[...] = gfirst.reshape(NT, 8, 128)
    x_gt.start()
    r_gt[b] = s_gt[b]

    x_out.recv()
    mixture = mm_tn(w_back[...], r_out[...].reshape(256, 1024))
    for h in range(2):
        cols = slice(h * 1024, (h + 1) * 1024)
        embedded = mm_tn(emb_ref[...], hot[a, :, cols])
        lay_ref[:, cols] = (embedded + mixture[h * 128 : (h + 1) * 128]).astype(BF)

    x_gt.recv()
    gt = r_gt[...].reshape(128, 128).T
    gnt = jnp.zeros((16, 128), F32)
    for p in range(3):
        hi, lo = split(gt[p * 16 : (p + 1) * 16, :])
        block = blk_ref[:, p * 128 : (p + 1) * 128]
        gnt += mm_nt(hi, block) + mm_nt(lo, block)
    emb = emb_ref[...].astype(F32)
    scal_col = jnp.sum(jnp.where(lane16 == row16, scal_row, 0.0), axis=1, keepdims=True)
    ggrad_ref[...] = jnp.sum(gnt * emb * scal_col, axis=0, keepdims=True)
    s_cr[...] = jnp.broadcast_to(jnp.sum(gnt * gain_row * emb, axis=1, keepdims=True), (16, 128))
    x_cr.start()
    r_cr[b] = s_cr[...]

    x_fg.recv()
    grid_a[...] = r_fg[...].reshape(2048, 128).astype(F32)
    for q in range(16):
        fgrad_ref[:, q * 128 : (q + 1) * 128] = grid_a[pl.ds(q, 128, stride=16), :]

    x_cr.recv()
    cross = jnp.sum(r_cr[...], axis=0)
    egrad_ref[...] = (
        ctt
        + scal_col * gain_row * gnt
        - emb * (scal_col * scal_col * scal_col * cross * (1.0 / WIDTH))
    )

    for exchange in (
        x_filt, x_tok, x_gf, x_fl, x_fg, x_gg, x_seg, x_back, x_ss, x_tab, x_out, x_gt, x_cr
    ):
        exchange.drain()


def local(token_ids, embedding, norm_gain, proj_blocks, proj_mixers, out_blocks, out_mixers, filters, cotangent):
    vmem = pl.BlockSpec(memory_space=pltpu.VMEM)
    V = pltpu.VMEM
    scratch = [
        V((NC, 16, 2048), BF),
        V((NC, 16, 128), jnp.int32),
        V((NC, 16, 16, 128), BF), V((NC, 16, 16, 128), BF),
        V((NC, 16, 16, 128), BF), V((NC, 16, 16, 128), BF),
        V((NC, 16, 16, 128), BF), V((NC, 16, 16, 128), BF),
        V((16, 128), F32), V((NC, 16, 128), F32),
        V((2, 16, 128), F32), V((NC, 2, 16, 128), F32),
        V((NT, 16, 1024), BF), V((NT, 16, 1024), BF),
        V((8, 128), F32), V((NT, 8, 128), F32),
        V((NT, 8, 128), F32), V((NT, 8, 128), F32),
        V((NT, 16, 1024), BF), V((NT, 16, 1024), BF),
        V((NT, 8, 128), F32), V((NT, 8, 128), F32),
        V((16, 128), F32), V((NT, 16, 128), F32),
        V((256, 256), BF), V((256, 256), BF), V((3, 128, 128), BF),
        V((NC, 16, 2048), BF),
        V((128, 128), F32), V((128, 128), F32),
        V((2048, 128), F32), V((2048, 128), F32),
        V((16, 128, 256), F32), V((16, 128, 128), F32),
        V((256, 1024), F32), V((256, 1024), F32),
        pltpu.SemaphoreType.DMA((7, NC)), pltpu.SemaphoreType.DMA((7, NC)),
        pltpu.SemaphoreType.DMA((6, NT)), pltpu.SemaphoreType.DMA((6, NT)),
    ]
    layer_out, filter_grad, embed_grad, gain_grad = pl.pallas_call(
        kernel,
        out_shape=(
            jax.ShapeDtypeStruct((128, 2048), BF),
            jax.ShapeDtypeStruct((128, 2048), F32),
            jax.ShapeDtypeStruct((16, 128), F32),
            jax.ShapeDtypeStruct((1, 128), F32),
        ),
        in_specs=[vmem] * 15,
        out_specs=(vmem,) * 4,
        scratch_shapes=scratch,
        compiler_params=pltpu.CompilerParams(
            collective_id=0, has_side_effects=True, vmem_limit_bytes=56 * 1024 * 1024
        ),
    )(
        token_ids.reshape(16, 128),
        embedding,
        norm_gain.reshape(1, 128),
        proj_blocks.reshape(128, 384),
        proj_mixers.reshape(384, 16),
        out_blocks.reshape(128, 128),
        out_mixers.reshape(128, 16),
        filters,
        cotangent,
        *dft_tables(),
    )
    return layer_out, filter_grad, embed_grad, gain_grad.reshape(128)


def solution(mesh):
    in_specs = (
        P("ctx"),
        P(None, "tp"),
        P("tp"),
        P("tp", None, None),
        P(None, "tp", None, None),
        P("tp", None, None),
        P("tp", None, None),
        P("tp", "ctx"),
        P("tp", "ctx"),
    )
    out_specs = (P("tp", "ctx"), P("tp", "ctx"), P(None, "tp"), P("tp"))
    return jax.shard_map(local, mesh=mesh, in_specs=in_specs, out_specs=out_specs, check_vma=False)
```

```python
import jax
import jax.numpy as jnp
import numpy as np
from jax import lax
from jax.experimental import pallas as pl
from jax.experimental.pallas import tpu as pltpu
from jax.sharding import PartitionSpec as P

WIDTH = 2048
EPS = 1e-06
SPAN = 32768
NC = 8
NT = 16
BF = jnp.bfloat16
F32 = jnp.float32
MESH = pl.DeviceIdType.MESH

FILT_IN, TOK, GF, GG, SEG, FILT, FG = 0, 1, 2, 3, 4, 5, 9
BACK, SS, TAB, OUT, GT = range(5)


def dft_tables():
    idx = np.arange(128)
    half = idx + 0.5
    first = 2 * np.pi * np.outer(half, idx) / 256.0
    c1 = np.concatenate([np.cos(first), -np.sin(first)], 0)
    twist = 2 * np.pi * np.outer(half, idx) / SPAN
    second = 2 * np.pi * (np.outer(idx, idx) % 128) / 128.0
    co, si = np.cos(second), np.sin(second)
    c2 = np.block([[co, -si], [si, co]])
    i1 = np.block([[co, si], [-si, co]])
    i2 = np.concatenate([np.cos(first.T), -np.sin(first.T)], 1) * (2.0 / SPAN)
    cast = lambda a, d: jnp.asarray(a, F32).astype(d)
    return (
        cast(c1, BF),
        cast(np.concatenate([np.cos(twist), np.sin(twist)], 1), F32),
        cast(np.concatenate([c2, i1, i2], 0), BF),
    )


def mm(a, b):
    return jnp.dot(a, b, preferred_element_type=F32)


def mm_tn(a, b):
    return lax.dot_general(a, b, (((0,), (0,)), ((), ())), preferred_element_type=F32)


def mm_nt(a, b):
    return lax.dot_general(a, b, (((1,), (1,)), ((), ())), preferred_element_type=F32)


def iota2(rows, lanes):
    return (
        lax.broadcasted_iota(jnp.int32, (rows, lanes), 0),
        lax.broadcasted_iota(jnp.int32, (rows, lanes), 1),
    )


def ones_at(cond):
    return jnp.where(cond, 1.0, 0.0).astype(F32)


def split(x):
    hi = x.astype(BF)
    return hi, (x - hi.astype(F32)).astype(BF)


def kernel(
    tok_hbm, emb_hbm, gain_hbm, blk_hbm, mix_hbm, oblk_hbm, omix_hbm, filt_hbm, cot_hbm,
    c1_hbm, turn_hbm, dft_hbm,
    r_out, r_fg, w_back, embedded, small,
    tok_ref, emb_ref, gain_ref, blk_ref, mix_ref, oblk_ref, omix_ref, cot_ref, c1_ref, turn_ref, dft_ref,
    r_filt, r_tok, s_gf, r_gf, s_fl, r_fl, s_fg, s_gg, r_gg, s_seg, r_seg,
    s_back, r_back, s_ss, r_ss, s_tab, r_tab, s_out, s_gt, r_gt,
    w_two, r_mix, hot, tall, gated_t, grid_a, grid_b, spec_x, spec_g, spec_s, outer, gbranch,
    ssem_c, rsem_c, ssem_t, rsem_t, lsem,
):
    a = lax.axis_index("ctx")
    b = lax.axis_index("tp")

    class Exchange:
        def __init__(self, axis, msg, src, dst):
            self.me, self.n = (a, NC) if axis == "ctx" else (b, NT)
            sends, recvs = (ssem_c, rsem_c) if axis == "ctx" else (ssem_t, rsem_t)

            def copy(k):
                peer = lax.rem(self.me + k, self.n)
                return pltpu.make_async_remote_copy(
                    src_ref=src(peer),
                    dst_ref=dst(self.me),
                    send_sem=sends.at[msg, k],
                    recv_sem=recvs.at[msg, k],
                    device_id={axis: peer},
                    device_id_type=MESH,
                )

            self.copy = copy

        def each(self, act):
            def body(k, carry):
                act(self.copy(k))
                return carry

            lax.fori_loop(1, self.n, body, 0)

        def start(self):
            self.each(lambda c: c.start())

        def recv(self):
            self.each(lambda c: c.wait_recv())

        def drain(self):
            self.each(lambda c: c.wait_send())

    rows16 = lambda ref: (lambda p: ref.at[pl.ds(pl.multiple_of(p * 16, 16), 16), :])
    slot = lambda ref: (lambda p: ref.at[p])
    whole = lambda ref: (lambda p: ref)

    x_filt = Exchange("ctx", FILT_IN, rows16(filt_hbm), slot(r_filt))
    x_tok = Exchange("ctx", TOK, whole(tok_ref), slot(r_tok))
    x_gf = Exchange("ctx", GF, slot(s_gf), slot(r_gf))
    quarter = lambda ref, n: (lambda p: ref.at[p, pl.ds(n * 4, 4)])
    x_fl = lambda n: Exchange("ctx", FILT + n, quarter(s_fl, n), quarter(r_fl, n))
    x_fg = lambda n: Exchange("ctx", FG + n, quarter(s_fg, n), quarter(r_fg, n))
    x_gg = Exchange("ctx", GG, whole(s_gg), slot(r_gg))
    x_seg = Exchange("ctx", SEG, whole(s_seg), slot(r_seg))
    x_back = Exchange("tp", BACK, slot(s_back), slot(r_back))
    x_ss = Exchange("tp", SS, whole(s_ss), slot(r_ss))
    x_tab = Exchange("tp", TAB, slot(s_tab), slot(r_tab))
    x_out = Exchange("tp", OUT, slot(s_out), slot(r_out))
    x_gt = Exchange("tp", GT, slot(s_gt), slot(r_gt))

    barrier = pltpu.get_barrier_semaphore()

    def greet(axis, me, n):
        def body(k, carry):
            pl.semaphore_signal(
                barrier, inc=1, device_id={axis: lax.rem(me + k, n)}, device_id_type=MESH
            )
            return carry

        lax.fori_loop(1, n, body, 0)

    greet("ctx", a, NC)
    greet("tp", b, NT)

    own = pl.ds(pl.multiple_of(a * 16, 16), 16)
    loads = {}
    for n, (name, src, dst) in enumerate(
        (
            ("omix", omix_hbm, omix_ref),
            ("cot", cot_hbm, cot_ref),
            ("emb", emb_hbm, emb_ref),
            ("tok", tok_hbm, tok_ref),
            ("filt", filt_hbm.at[own, :], r_filt.at[a]),
            ("mix", mix_hbm, mix_ref),
            ("gain", gain_hbm, gain_ref),
            ("blk", blk_hbm, blk_ref),
            ("oblk", oblk_hbm, oblk_ref),
            ("c1", c1_hbm, c1_ref),
            ("turn", turn_hbm, turn_ref),
            ("dft", dft_hbm, dft_ref),
        )
    ):
        loads[name] = pltpu.make_async_copy(src, dst, lsem.at[n])
        loads[name].start()

    row128, lane128 = iota2(128, 128)
    p_lane = lane128 >> 4

    row16, lane16 = iota2(16, 128)
    spread = ones_at(((lane16 & 15) == row16) & (lane16 < 48)).astype(BF)
    loads["emb"].wait()
    loads["tok"].wait()
    emb_t = mm_tn(emb_ref[...], spread)
    s_ss[...] = jnp.broadcast_to(jnp.sum(emb_t * emb_t, axis=0, keepdims=True), (8, 128))

    loads["omix"].wait()
    tile_m = ones_at((lane16 & 15) == row16).astype(BF)
    row, lane = iota2(256, 128)
    sel_row = ones_at(((row & 7) == (lane >> 4)) & ((row >> 4) == (lane & 15))).astype(BF)
    wide = mm(sel_row, mm(omix_ref[...], tile_m).astype(BF))
    row, lane = iota2(256, 256)
    keep = ((row & 7) == ((lane >> 4) & 7)) & (((row >> 3) & 1) == (lane >> 7))
    w_back[...] = jnp.where(keep, jnp.concatenate([wide, wide], axis=1), 0.0).astype(BF)
    loads["cot"].wait()
    cot2 = jnp.concatenate([cot_ref[:, :1024], cot_ref[:, 1024:]], axis=0)
    s_back[...] = mm(w_back[...], cot2).astype(BF).reshape(NT, 16, 1024)
    pl.semaphore_wait(barrier, NC - 1 + NT - 1)
    x_ss.start()
    x_tok.start()
    x_back.start()
    x_filt.start()
    r_ss[b] = s_ss[...]
    r_tok[a] = tok_ref[...]

    r_back[b] = s_back[b]

    sel_p = ones_at(((row128 & 7) == p_lane) & ((row128 >> 3) == (lane128 & 15))).astype(BF)
    loads["mix"].wait()
    for p in range(3):
        wide = mm(sel_p, mm(mix_ref[p * 128 : (p + 1) * 128, :], tile_m).astype(BF))
        r_mix[p] = jnp.where((row128 & 7) == p_lane, wide, 0.0).astype(BF)
    for name in ("gain", "blk", "oblk", "c1", "turn", "dft", "filt"):
        loads[name].wait()
    gain_row = gain_ref[...]
    gain_col = jnp.sum(jnp.where(row128 == lane128, gain_row, 0.0), axis=1, keepdims=True)

    x_ss.recv()
    total = jnp.sum(r_ss[...], axis=0)[0:1, :]
    scal_row = lax.rsqrt(total * (1.0 / WIDTH) + EPS)
    normed = emb_t * scal_row * gain_col
    first = jnp.zeros((128, 128), F32)
    for p in range(3):
        first += mm_tn(
            blk_ref[:, p * 128 : (p + 1) * 128], jnp.where(p_lane == p, normed, 0.0).astype(BF)
        )
    s_tab[...] = first.reshape(NT, 8, 128)
    x_tab.start()
    r_tab[b] = s_tab[b]

    row, lane = iota2(128, 256)
    sel_col = ones_at(((lane >> 4) * 8 + (lane & 7)) == row).astype(BF)
    wide = mm(oblk_ref[...], sel_col)
    low = ((lane >> 3) & 1) == 0
    w_two[...] = jnp.concatenate(
        [jnp.where(low, wide, 0.0), jnp.where(low, 0.0, wide)], axis=0
    ).astype(BF)

    x_tok.recv()
    for src in range(NC):
        ids = r_tok[src]
        for q in range(16):
            hot[src, :, q * 128 : (q + 1) * 128] = ones_at(
                jnp.broadcast_to(ids[q : q + 1, :], (16, 128)) == row16
            ).astype(BF)

    x_tab.recv()
    pieces = r_tab[...].reshape(128, 128)
    table = jnp.zeros((128, 128), F32)
    for p in range(3):
        table += mm_tn(r_mix[p], jnp.where(p_lane == p, pieces, 0.0).astype(BF))
    tall[...] = table
    gated_t[...] = table * pltpu.roll(table, 112, 1)
    outer_hi, outer_lo = split(pltpu.roll(table, 96, 1)[:, :16])
    outer_w = jnp.concatenate([outer_hi, outer_lo], axis=1)
    for h in range(2):
        hot_h = hot[a, :, h * 1024 : (h + 1) * 1024]
        outer[h * 128 : (h + 1) * 128, :] = mm(outer_w, jnp.concatenate([hot_h, hot_h], axis=0))
        embedded[h * 128 : (h + 1) * 128, :] = mm_tn(emb_ref[...], hot_h).astype(BF)

    x_back.recv()
    gbranch[...] = mm(w_two[...], r_back[...].reshape(256, 1024))
    for h in range(2):
        for s in range(8):
            part = slice(s * 128, (s + 1) * 128)
            hrow = slice(h * 128, (h + 1) * 128)
            grid_a[pl.ds(h * 8 + s, 128, stride=16), :] = gbranch[hrow, part] * outer[hrow, part]
    s_gf[...] = grid_a[...].astype(BF).reshape(NC, 16, 16, 128)
    x_gf.start()
    r_gf[a] = s_gf[a]

    mine = gated_t[pl.ds(pl.multiple_of(a * 16, 16), 16), :][:, :16].astype(BF)
    for src in range(NC):
        vals = mm(mine, hot[src])
        for q in range(16):
            grid_a[pl.ds(src * 16 + q, 16, stride=128), :] = vals[:, q * 128 : (q + 1) * 128]

    tc = turn_ref[:, :128]
    ts = turn_ref[:, 128:]
    c2_ref = dft_ref.at[0:256, :]
    i1_ref = dft_ref.at[256:512, :]
    i2_ref = dft_ref.at[512:640, :]
    tc2 = jnp.concatenate([tc, tc], axis=1)
    ts2 = jnp.concatenate([ts, ts], axis=1)

    def forward(signals, second):
        turned = []
        for u in range(0, len(signals), 2):
            stage = mm(c1_ref[...], jnp.concatenate(signals[u : u + 2], axis=1))
            re, im = stage[:128], stage[128:]
            tr = re * tc2 + im * ts2
            ti = im * tc2 - re * ts2
            for v in range(2):
                cols = slice(v * 128, (v + 1) * 128)
                turned.append(jnp.concatenate([tr[:, cols], ti[:, cols]], axis=1).astype(BF))
        return mm(jnp.concatenate(turned, axis=0), second)

    def inverse(spectrum, weights):
        back = mm(spectrum.astype(BF), weights)
        results = []
        for u in range(0, spectrum.shape[0], 256):
            both = [
                jnp.concatenate(
                    [back[u + v : u + v + 128, :128], back[u + v : u + v + 128, 128:]], axis=0
                )
                for v in (0, 128)
            ]
            both = jnp.concatenate(both, axis=1)
            re, im = both[:128], both[128:]
            turned = jnp.concatenate([re * tc2 - im * ts2, im * tc2 + re * ts2], axis=0)
            pair = mm(i2_ref[...], turned.astype(BF))
            results += [pair[:, :128], pair[:, 128:]]
        return results

    def groups(body):
        def step(n, carry):
            body(n)
            return carry

        lax.fori_loop(0, 4, step, 0)

    def rows_of(n):
        return pl.ds(pl.multiple_of(n * 512, 512), 512)

    def signals(ref, n):
        block = ref[rows_of(n), :].astype(BF)
        return [block[u * 128 : (u + 1) * 128] for u in range(4)]

    def gated_spectrum(n):
        spec_x[rows_of(n), :] = forward(signals(grid_a, n), c2_ref[...])

    groups(gated_spectrum)

    x_filt.recv()
    for src in range(NC):
        for q in range(16):
            grid_b[pl.ds(src * 16 + q, 16, stride=128), :] = r_filt[
                src, :, q * 128 : (q + 1) * 128
            ].astype(F32)

    def filtered_group(n):
        even = 2.0 * forward(signals(grid_b, n), c2_ref[:, :128])
        spec_s[rows_of(n), :] = even
        spectrum = spec_x[rows_of(n), :] * jnp.concatenate([even, even], axis=1)
        for u, result in enumerate(inverse(spectrum, i1_ref[...])):
            s_fl[:, n * 4 + u] = result.astype(BF).reshape(NC, 16, 128)
        x_fl(n).start()

    groups(filtered_group)
    r_fl[a] = s_fl[a]

    x_gf.recv()

    def grad_group(n):
        spectrum = forward([r_gf[:, n * 4 + u].reshape(128, 128) for u in range(4)], c2_ref[...])
        spec_g[rows_of(n), :] = spectrum
        prod = spectrum * spec_x[rows_of(n), :]
        cross = 2.0 * (prod[:, :128] + prod[:, 128:])
        for u, result in enumerate(inverse(cross, i1_ref[:128, :])):
            s_fg[:, n * 4 + u] = result.astype(BF).reshape(NC, 16, 128)
        x_fg(n).start()

    groups(grad_group)
    r_fg[a] = s_fg[a]

    for n in range(4):
        x_fl(n).recv()
    grid_a[...] = r_fl[...].reshape(2048, 128).astype(F32)
    gp2 = jnp.zeros((16, 128), F32)
    ctt = jnp.zeros((16, 128), F32)
    branch = []
    for h in range(2):
        hrow = slice(h * 128, (h + 1) * 128)
        filtered = jnp.concatenate(
            [grid_a[pl.ds(h * 8 + s, 128, stride=16), :] for s in range(8)], axis=1
        )
        branch.append((outer[hrow, :] * filtered).astype(BF))
        hot_h = hot[a, :, h * 1024 : (h + 1) * 1024]
        hi, lo = split(gbranch[hrow, :] * filtered)
        gp2 += mm_nt(hot_h, hi) + mm_nt(hot_h, lo)
        ctt += mm_nt(hot_h, cot_ref[:, h * 1024 : (h + 1) * 1024])
    s_seg[0] = gp2
    s_seg[1] = ctt
    x_seg.start()
    r_seg[a] = s_seg[...]
    s_out[...] = (
        mm_tn(w_two[...], jnp.concatenate(branch, axis=0)).astype(BF).reshape(NT, 16, 1024)
    )
    x_out.start()
    r_out[b] = s_out[b]

    def gated_group(n):
        even = spec_s[rows_of(n), :]
        spectrum = spec_g[rows_of(n), :] * jnp.concatenate([even, even], axis=1)
        for u, result in enumerate(inverse(spectrum, i1_ref[...])):
            start = pl.multiple_of(n * 512 + u * 128, 128)
            grid_b[pl.ds(start, 128), :] = result

    groups(gated_group)
    sums = jnp.zeros((16, 32), F32)
    for src in range(NC):
        vals = jnp.concatenate(
            [grid_b[pl.ds(src * 16 + q, 16, stride=128), :] for q in range(16)], axis=1
        ).astype(BF)
        hot_s = hot[src]
        sums += mm_nt(vals, jnp.concatenate([hot_s, hot_s], axis=0))
    s_gg[...] = jnp.concatenate([sums, jnp.zeros((16, 96), F32)], axis=1)
    x_gg.start()
    r_gg[a] = s_gg[...]

    x_gg.recv()
    x_seg.recv()
    seg = jnp.sum(r_seg[...], axis=0)
    ctt = seg[1]
    hi, rest = seg[0].astype(BF), seg[0] - seg[0].astype(BF).astype(F32)
    mid, low_part = split(rest)
    row48, lane48 = iota2(48, 128)
    place = ones_at(((row48 & 15) + 32) == lane48).astype(BF)
    gp2_t = mm_tn(jnp.concatenate([hi, mid, low_part], axis=0), place)
    table = tall[...]
    swapped = jnp.where(lane128 < 16, pltpu.roll(table, 112, 1), pltpu.roll(table, 16, 1))
    grads = jnp.where(lane128 < 32, r_gg[...].reshape(128, 128) * swapped, gp2_t)
    gfirst = jnp.zeros((128, 128), F32)
    for p in range(3):
        hi, lo = split(jnp.where(p_lane == p, grads, 0.0))
        gfirst += mm(r_mix[p], hi) + mm(r_mix[p], lo)
    share = jnp.sum(gfirst * r_tab[...].reshape(128, 128), axis=0, keepdims=True) / scal_row
    share = jnp.broadcast_to(share, (128, 128))
    share = pltpu.roll(share, 48, 1) + pltpu.roll(share, 32, 1) + pltpu.roll(share, 16, 1)
    s_gt[...] = jnp.where(
        lane128 < 48, gfirst, jnp.where(lane128 < 64, share, 0.0)
    ).reshape(NT, 8, 128)
    x_gt.start()
    r_gt[b] = s_gt[b]

    x_gt.recv()
    gt = r_gt[...].reshape(128, 128).T
    gnt = jnp.zeros((16, 128), F32)
    for p in range(3):
        hi, lo = split(gt[p * 16 : (p + 1) * 16, :])
        block = blk_ref[:, p * 128 : (p + 1) * 128]
        gnt += mm_nt(hi, block) + mm_nt(lo, block)
    cross = jnp.sum(gt[48:64, :], axis=1, keepdims=True) * 0.125
    emb = emb_ref[...].astype(F32)
    scal_col = jnp.sum(jnp.where(lane16 == row16, scal_row, 0.0), axis=1, keepdims=True)
    small[16:24, :] = jnp.broadcast_to(
        jnp.sum(gnt * emb * scal_col, axis=0, keepdims=True), (8, 128)
    )
    small[0:16, :] = (
        ctt
        + scal_col * gain_row * gnt
        - emb * (scal_col * scal_col * scal_col * cross * (1.0 / WIDTH))
    )

    x_out.recv()
    for n in range(4):
        x_fg(n).recv()

    for exchange in (
        x_filt, x_tok, x_gf, x_gg, x_seg, x_back, x_ss, x_tab, x_out, x_gt,
        *[x_fl(n) for n in range(4)], *[x_fg(n) for n in range(4)],
    ):
        exchange.drain()


def finish(
    out_hbm, fg_hbm, w_hbm, emb_hbm, small_hbm,
    lay_ref, fgrad_ref, egrad_ref, ggrad_ref,
    out_ref, fg_ref, w_ref, emb_ref, small_ref, grid, sem,
):
    pairs = (
        (fg_hbm, fg_ref), (out_hbm, out_ref), (w_hbm, w_ref), (emb_hbm, emb_ref),
        (small_hbm, small_ref),
    )
    copies = [pltpu.make_async_copy(src, dst, sem.at[n]) for n, (src, dst) in enumerate(pairs)]
    for copy in copies:
        copy.start()
    copies[0].wait()
    grid[...] = fg_ref[...].reshape(2048, 128).astype(F32)
    for q in range(16):
        fgrad_ref[:, q * 128 : (q + 1) * 128] = grid[pl.ds(q, 128, stride=16), :]
    for copy in copies[1:]:
        copy.wait()
    mixture = mm_tn(w_ref[...], out_ref[...].reshape(256, 1024))
    for h in range(2):
        hrow = slice(h * 128, (h + 1) * 128)
        lay_ref[:, h * 1024 : (h + 1) * 1024] = (emb_ref[hrow].astype(F32) + mixture[hrow]).astype(BF)
    egrad_ref[...] = small_ref[0:16, :]
    ggrad_ref[...] = small_ref[16:17, :]


def local(token_ids, embedding, norm_gain, proj_blocks, proj_mixers, out_blocks, out_mixers, filters, cotangent):
    vmem = pl.BlockSpec(memory_space=pltpu.VMEM)
    V = pltpu.VMEM
    scratch = [
        V((16, 128), jnp.int32), V((16, 128), BF), V((1, 128), F32), V((128, 384), BF),
        V((384, 16), BF), V((128, 128), BF), V((128, 16), BF), V((128, 2048), BF),
        V((256, 128), BF), V((128, 256), F32), V((640, 256), BF),
        V((NC, 16, 2048), BF),
        V((NC, 16, 128), jnp.int32),
        V((NC, 16, 16, 128), BF), V((NC, 16, 16, 128), BF),
        V((NC, 16, 16, 128), BF), V((NC, 16, 16, 128), BF),
        V((NC, 16, 16, 128), BF),
        V((16, 128), F32), V((NC, 16, 128), F32),
        V((2, 16, 128), F32), V((NC, 2, 16, 128), F32),
        V((NT, 16, 1024), BF), V((NT, 16, 1024), BF),
        V((8, 128), F32), V((NT, 8, 128), F32),
        V((NT, 8, 128), F32), V((NT, 8, 128), F32),
        V((NT, 16, 1024), BF),
        V((NT, 8, 128), F32), V((NT, 8, 128), F32),
        V((256, 256), BF), V((3, 128, 128), BF),
        V((NC, 16, 2048), BF),
        V((128, 128), F32), V((128, 128), F32),
        V((2048, 128), F32), V((2048, 128), F32),
        V((2048, 256), F32), V((2048, 256), F32), V((2048, 128), F32),
        V((256, 1024), F32), V((256, 1024), F32),
        pltpu.SemaphoreType.DMA((13, NC)), pltpu.SemaphoreType.DMA((13, NC)),
        pltpu.SemaphoreType.DMA((5, NT)), pltpu.SemaphoreType.DMA((5, NT)), pltpu.SemaphoreType.DMA((12,)),
    ]
    received = pl.pallas_call(
        kernel,
        out_shape=(
            jax.ShapeDtypeStruct((NT, 16, 1024), BF),
            jax.ShapeDtypeStruct((NC, 16, 16, 128), BF),
            jax.ShapeDtypeStruct((256, 256), BF),
            jax.ShapeDtypeStruct((256, 1024), BF),
            jax.ShapeDtypeStruct((24, 128), F32),
        ),
        in_specs=[pl.BlockSpec(memory_space=pltpu.HBM)] * 12,
        out_specs=(vmem,) * 5,
        scratch_shapes=scratch,
        compiler_params=pltpu.CompilerParams(
            collective_id=0, has_side_effects=True, vmem_limit_bytes=56 * 1024 * 1024
        ),
    )(
        token_ids.reshape(16, 128),
        embedding,
        norm_gain.reshape(1, 128),
        proj_blocks.reshape(128, 384),
        proj_mixers.reshape(384, 16),
        out_blocks.reshape(128, 128),
        out_mixers.reshape(128, 16),
        filters,
        cotangent,
        *dft_tables(),
    )
    layer_out, filter_grad, embed_grad, gain_grad = pl.pallas_call(
        finish,
        out_shape=(
            jax.ShapeDtypeStruct((128, 2048), BF),
            jax.ShapeDtypeStruct((128, 2048), F32),
            jax.ShapeDtypeStruct((16, 128), F32),
            jax.ShapeDtypeStruct((1, 128), F32),
        ),
        in_specs=[pl.BlockSpec(memory_space=pltpu.HBM)] * 5,
        out_specs=(vmem,) * 4,
        scratch_shapes=[
            V((NT, 16, 1024), BF), V((NC, 16, 16, 128), BF), V((256, 256), BF), V((256, 1024), BF),
            V((24, 128), F32), V((2048, 128), F32), pltpu.SemaphoreType.DMA((5,)),
        ],
        compiler_params=pltpu.CompilerParams(vmem_limit_bytes=56 * 1024 * 1024),
    )(*received)
    return layer_out, filter_grad, embed_grad, gain_grad.reshape(128)


def solution(mesh):
    in_specs = (
        P("ctx"),
        P(None, "tp"),
        P("tp"),
        P("tp", None, None),
        P(None, "tp", None, None),
        P("tp", None, None),
        P("tp", None, None),
        P("tp", "ctx"),
        P("tp", "ctx"),
    )
    out_specs = (P("tp", "ctx"), P("tp", "ctx"), P(None, "tp"), P("tp"))
    return jax.shard_map(local, mesh=mesh, in_specs=in_specs, out_specs=out_specs, check_vma=False)
```

```python
import jax
import jax.numpy as jnp
import numpy as np
from jax import lax
from jax.experimental import pallas as pl
from jax.experimental.pallas import tpu as pltpu
from jax.sharding import PartitionSpec as P

WIDTH = 2048
EPS = 1e-06
SPAN = 32768
NC = 8
NT = 16
BF = jnp.bfloat16
F32 = jnp.float32
MESH = pl.DeviceIdType.MESH

FILT_IN, TOK, GF, GG, SEG, FILT, FG = 0, 1, 2, 3, 4, 5, 9
BACK, TAB, OUT, GT = range(4)


def dft_tables():
    idx = np.arange(128)
    half = idx + 0.5
    first = 2 * np.pi * np.outer(half, idx) / 256.0
    c1 = np.concatenate([np.cos(first), -np.sin(first)], 0)
    twist = 2 * np.pi * np.outer(half, idx) / SPAN
    second = 2 * np.pi * (np.outer(idx, idx) % 128) / 128.0
    co, si = np.cos(second), np.sin(second)
    c2 = np.block([[co, -si], [si, co]])
    i1 = np.block([[co, si], [-si, co]])
    i2 = np.concatenate([np.cos(first.T), -np.sin(first.T)], 1) * (2.0 / SPAN)
    cast = lambda a, d: jnp.asarray(a, F32).astype(d)
    return (
        cast(c1, BF),
        cast(np.concatenate([np.cos(twist), np.sin(twist)], 1), F32),
        cast(np.concatenate([c2, i1, i2], 0), BF),
    )


def mm(a, b):
    return jnp.dot(a, b, preferred_element_type=F32)


def mm_tn(a, b):
    return lax.dot_general(a, b, (((0,), (0,)), ((), ())), preferred_element_type=F32)


def mm_nt(a, b):
    return lax.dot_general(a, b, (((1,), (1,)), ((), ())), preferred_element_type=F32)


def iota2(rows, lanes):
    return (
        lax.broadcasted_iota(jnp.int32, (rows, lanes), 0),
        lax.broadcasted_iota(jnp.int32, (rows, lanes), 1),
    )


def ones_at(cond):
    return jnp.where(cond, 1.0, 0.0).astype(F32)


def split(x):
    hi = x.astype(BF)
    return hi, (x - hi.astype(F32)).astype(BF)


def kernel(
    tok_hbm, emb_hbm, gain_hbm, blk_hbm, mix_hbm, oblk_hbm, omix_hbm, filt_hbm, cot_hbm,
    c1_hbm, turn_hbm, dft_hbm,
    r_out, r_fg, w_back, embedded, small,
    tok_ref, emb_ref, gain_ref, blk_ref, mix_ref, oblk_ref, omix_ref, cot_ref, c1_ref, turn_ref, dft_ref,
    r_filt, r_tok, s_gf, r_gf, s_fl, r_fl, s_fg, s_gg, r_gg, s_seg, r_seg,
    s_back, r_back, s_tab, r_tab, s_out, s_gt, r_gt,
    w_two, r_mix, hot, tall, gated_t, grid_a, grid_b, spec_x, spec_g, spec_s, outer, gbranch,
    ssem_c, rsem_c, ssem_t, rsem_t, lsem,
):
    a = lax.axis_index("ctx")
    b = lax.axis_index("tp")

    def peer_of(axis, k):
        if axis == "tp":
            return lax.rem(b + k, NT)
        return lax.rem(a // 4 + k // 4, 2) * 4 + lax.rem(a % 4 + k % 4, 4)

    class Exchange:
        def __init__(self, axis, msg, src, dst):
            self.me, self.n = (a, NC) if axis == "ctx" else (b, NT)
            sends, recvs = (ssem_c, rsem_c) if axis == "ctx" else (ssem_t, rsem_t)

            def copy(k):
                peer = peer_of(axis, k)
                return pltpu.make_async_remote_copy(
                    src_ref=src(peer),
                    dst_ref=dst(self.me),
                    send_sem=sends.at[msg, k],
                    recv_sem=recvs.at[msg, k],
                    device_id={axis: peer},
                    device_id_type=MESH,
                )

            self.copy = copy

        def each(self, act, low=1, high=None):
            def body(k, carry):
                act(self.copy(k))
                return carry

            lax.fori_loop(low, high or self.n, body, 0)

        def start(self, low=1, high=None):
            self.each(lambda c: c.start(), low, high)

        def recv(self):
            self.each(lambda c: c.wait_recv())

        def drain(self):
            self.each(lambda c: c.wait_send())

    rows16 = lambda ref: (lambda p: ref.at[pl.ds(pl.multiple_of(p * 16, 16), 16), :])
    slot = lambda ref: (lambda p: ref.at[p])
    whole = lambda ref: (lambda p: ref)

    x_filt = Exchange("ctx", FILT_IN, rows16(filt_hbm), slot(r_filt))
    x_tok = Exchange("ctx", TOK, whole(tok_ref), slot(r_tok))
    x_gf = Exchange("ctx", GF, slot(s_gf), slot(r_gf))
    quarter = lambda ref, n: (lambda p: ref.at[p, pl.ds(n * 4, 4)])
    x_fl = lambda n: Exchange("ctx", FILT + n, quarter(s_fl, n), quarter(r_fl, n))
    x_fg = lambda n: Exchange("ctx", FG + n, quarter(s_fg, n), quarter(r_fg, n))
    x_gg = Exchange("ctx", GG, whole(s_gg), slot(r_gg))
    x_seg = Exchange("ctx", SEG, whole(s_seg), slot(r_seg))
    x_back = Exchange("tp", BACK, slot(s_back), slot(r_back))
    x_tab = Exchange("tp", TAB, slot(s_tab), slot(r_tab))
    x_out = Exchange("tp", OUT, slot(s_out), slot(r_out))
    x_gt = Exchange("tp", GT, slot(s_gt), slot(r_gt))

    barrier = pltpu.get_barrier_semaphore()

    def greet(axis, n):
        def body(k, carry):
            pl.semaphore_signal(
                barrier, inc=1, device_id={axis: peer_of(axis, k)}, device_id_type=MESH
            )
            return carry

        lax.fori_loop(1, n, body, 0)

    greet("ctx", NC)
    greet("tp", NT)

    own = pl.ds(pl.multiple_of(a * 16, 16), 16)
    loads = {}
    for n, (name, src, dst) in enumerate(
        (
            ("emb", emb_hbm, emb_ref),
            ("gain", gain_hbm, gain_ref),
            ("blk", blk_hbm, blk_ref),
            ("omix", omix_hbm, omix_ref),
            ("cot", cot_hbm, cot_ref),
            ("tok", tok_hbm, tok_ref),
            ("mix", mix_hbm, mix_ref),
            ("oblk", oblk_hbm, oblk_ref),
            ("c1", c1_hbm, c1_ref),
            ("turn", turn_hbm, turn_ref),
            ("dft", dft_hbm, dft_ref),
            ("filt", filt_hbm.at[own, :], r_filt.at[a]),
        )
    ):
        loads[name] = pltpu.make_async_copy(src, dst, lsem.at[n])
        loads[name].start()

    row128, lane128 = iota2(128, 128)
    p_lane = lane128 >> 4
    row16, lane16 = iota2(16, 128)

    spread = ones_at(((lane16 & 15) == row16) & (lane16 < 48)).astype(BF)
    for name in ("emb", "gain", "blk"):
        loads[name].wait()
    gain_row = gain_ref[...]
    gain_col = jnp.sum(jnp.where(row128 == lane128, gain_row, 0.0), axis=1, keepdims=True)
    emb_t = mm_tn(emb_ref[...], spread)
    squares = jnp.broadcast_to(jnp.sum(emb_t * emb_t, axis=0, keepdims=True), (128, 128))
    first = jnp.where(
        (lane128 >= 48) & (lane128 < 64), pltpu.roll(squares, 48, 1), 0.0
    )
    for p in range(3):
        block = blk_ref[:, p * 128 : (p + 1) * 128]
        hi, lo = split(jnp.where(p_lane == p, emb_t * gain_col, 0.0))
        first += mm_tn(block, hi) + mm_tn(block, lo)
    s_tab[...] = first.reshape(NT, 8, 128)

    tile_m = ones_at((lane16 & 15) == row16).astype(BF)
    row, lane = iota2(256, 128)
    sel_row = ones_at(((row & 7) == (lane >> 4)) & ((row >> 4) == (lane & 15))).astype(BF)
    loads["omix"].wait()
    wide = mm(sel_row, mm(omix_ref[...], tile_m).astype(BF))
    row, lane = iota2(256, 256)
    keep = ((row & 7) == ((lane >> 4) & 7)) & (((row >> 3) & 1) == (lane >> 7))
    w_back[...] = jnp.where(keep, jnp.concatenate([wide, wide], axis=1), 0.0).astype(BF)
    loads["cot"].wait()
    cot2 = jnp.concatenate([cot_ref[:, :1024], cot_ref[:, 1024:]], axis=0)
    s_back[...] = mm(w_back[...], cot2).astype(BF).reshape(NT, 16, 1024)

    loads["tok"].wait()
    pl.semaphore_wait(barrier, NC - 1 + NT - 1)
    x_tab.start()
    x_tok.start()
    x_back.start()
    x_filt.start(1, 4)
    r_tab[b] = s_tab[b]
    r_tok[a] = tok_ref[...]
    r_back[b] = s_back[b]

    sel_p = ones_at(((row128 & 7) == p_lane) & ((row128 >> 3) == (lane128 & 15))).astype(BF)
    for name in ("mix", "oblk", "c1", "turn", "dft", "filt"):
        loads[name].wait()
    for p in range(3):
        wide = mm(sel_p, mm(mix_ref[p * 128 : (p + 1) * 128, :], tile_m).astype(BF))
        r_mix[p] = jnp.where((row128 & 7) == p_lane, wide, 0.0).astype(BF)

    row, lane = iota2(128, 256)
    sel_col = ones_at(((lane >> 4) * 8 + (lane & 7)) == row).astype(BF)
    wide = mm(oblk_ref[...], sel_col)
    low = ((lane >> 3) & 1) == 0
    w_two[...] = jnp.concatenate(
        [jnp.where(low, wide, 0.0), jnp.where(low, 0.0, wide)], axis=0
    ).astype(BF)

    x_tok.recv()
    for src in range(NC):
        ids = r_tok[src]
        for q in range(16):
            hot[src, :, q * 128 : (q + 1) * 128] = ones_at(
                jnp.broadcast_to(ids[q : q + 1, :], (16, 128)) == row16
            ).astype(BF)

    x_tab.recv()
    pieces = r_tab[...].reshape(128, 128)
    squares = jnp.sum(pieces, axis=0, keepdims=True) * 0.125
    squares = jnp.where((lane128 >= 48) & (lane128 < 64), squares, 0.0)[:8]
    squares = pltpu.roll(squares, 80, 1) + pltpu.roll(squares, 96, 1) + pltpu.roll(squares, 112, 1)
    scal_row = lax.rsqrt(squares[0:1, :] * (1.0 / WIDTH) + EPS)
    pieces = pieces * scal_row
    table = jnp.zeros((128, 128), F32)
    for p in range(3):
        table += mm_tn(r_mix[p], jnp.where(p_lane == p, pieces, 0.0).astype(BF))
    tall[...] = table
    gated_t[...] = table * pltpu.roll(table, 112, 1)
    outer_hi, outer_lo = split(pltpu.roll(table, 96, 1)[:, :16])
    outer_w = jnp.concatenate([outer_hi, outer_lo], axis=1)
    for h in range(2):
        hot_h = hot[a, :, h * 1024 : (h + 1) * 1024]
        outer[h * 128 : (h + 1) * 128, :] = mm(outer_w, jnp.concatenate([hot_h, hot_h], axis=0))
        embedded[h * 128 : (h + 1) * 128, :] = mm_tn(emb_ref[...], hot_h).astype(BF)

    mine = gated_t[pl.ds(pl.multiple_of(a * 16, 16), 16), :][:, :16].astype(BF)
    for src in range(NC):
        vals = mm(mine, hot[src])
        for q in range(16):
            grid_a[pl.ds(src * 16 + q, 16, stride=128), :] = vals[:, q * 128 : (q + 1) * 128]

    tc = turn_ref[:, :128]
    ts = turn_ref[:, 128:]
    c2_ref = dft_ref.at[0:256, :]
    i1_ref = dft_ref.at[256:512, :]
    i2_ref = dft_ref.at[512:640, :]
    tc2 = jnp.concatenate([tc, tc], axis=1)
    ts2 = jnp.concatenate([ts, ts], axis=1)

    def forward(signals, second):
        turned = []
        for u in range(0, len(signals), 2):
            stage = mm(c1_ref[...], jnp.concatenate(signals[u : u + 2], axis=1))
            re, im = stage[:128], stage[128:]
            tr = re * tc2 + im * ts2
            ti = im * tc2 - re * ts2
            for v in range(2):
                cols = slice(v * 128, (v + 1) * 128)
                turned.append(jnp.concatenate([tr[:, cols], ti[:, cols]], axis=1).astype(BF))
        return mm(jnp.concatenate(turned, axis=0), second)

    def inverse(spectrum, weights):
        back = mm(spectrum.astype(BF), weights)
        results = []
        for u in range(0, spectrum.shape[0], 256):
            both = [
                jnp.concatenate(
                    [back[u + v : u + v + 128, :128], back[u + v : u + v + 128, 128:]], axis=0
                )
                for v in (0, 128)
            ]
            both = jnp.concatenate(both, axis=1)
            re, im = both[:128], both[128:]
            turned = jnp.concatenate([re * tc2 - im * ts2, im * tc2 + re * ts2], axis=0)
            pair = mm(i2_ref[...], turned.astype(BF))
            results += [pair[:, :128], pair[:, 128:]]
        return results

    def groups(body):
        def step(n, carry):
            body(n)
            return carry

        lax.fori_loop(0, 4, step, 0)

    def rows_of(n):
        return pl.ds(pl.multiple_of(n * 512, 512), 512)

    def signals(ref, n):
        block = ref[rows_of(n), :].astype(BF)
        return [block[u * 128 : (u + 1) * 128] for u in range(4)]

    def gated_spectrum(n):
        spec_x[rows_of(n), :] = forward(signals(grid_a, n), c2_ref[...])

    groups(gated_spectrum)

    x_filt.start(4, 8)
    x_back.recv()
    gbranch[...] = mm(w_two[...], r_back[...].reshape(256, 1024))
    for h in range(2):
        for s in range(8):
            part = slice(s * 128, (s + 1) * 128)
            hrow = slice(h * 128, (h + 1) * 128)
            grid_a[pl.ds(h * 8 + s, 128, stride=16), :] = gbranch[hrow, part] * outer[hrow, part]
    s_gf[...] = grid_a[...].astype(BF).reshape(NC, 16, 16, 128)
    x_gf.start()
    r_gf[a] = s_gf[a]

    x_filt.recv()
    for src in range(NC):
        for q in range(16):
            grid_b[pl.ds(src * 16 + q, 16, stride=128), :] = r_filt[
                src, :, q * 128 : (q + 1) * 128
            ].astype(F32)

    def filtered_group(n):
        even = 2.0 * forward(signals(grid_b, n), c2_ref[:, :128])
        spec_s[rows_of(n), :] = even
        spectrum = spec_x[rows_of(n), :] * jnp.concatenate([even, even], axis=1)
        for u, result in enumerate(inverse(spectrum, i1_ref[...])):
            s_fl[:, n * 4 + u] = result.astype(BF).reshape(NC, 16, 128)
        x_fl(n).start()

    groups(filtered_group)
    r_fl[a] = s_fl[a]

    x_gf.recv()

    def grad_group(n):
        spectrum = forward([r_gf[:, n * 4 + u].reshape(128, 128) for u in range(4)], c2_ref[...])
        spec_g[rows_of(n), :] = spectrum
        prod = spectrum * spec_x[rows_of(n), :]
        cross = 2.0 * (prod[:, :128] + prod[:, 128:])
        for u, result in enumerate(inverse(cross, i1_ref[:128, :])):
            s_fg[:, n * 4 + u] = result.astype(BF).reshape(NC, 16, 128)
        x_fg(n).start()

    groups(grad_group)
    r_fg[a] = s_fg[a]

    def gated_group(n):
        even = spec_s[rows_of(n), :]
        spectrum = spec_g[rows_of(n), :] * jnp.concatenate([even, even], axis=1)
        for u, result in enumerate(inverse(spectrum, i1_ref[...])):
            start = pl.multiple_of(n * 512 + u * 128, 128)
            grid_b[pl.ds(start, 128), :] = result

    groups(gated_group)
    sums = jnp.zeros((16, 32), F32)
    for src in range(NC):
        vals = jnp.concatenate(
            [grid_b[pl.ds(src * 16 + q, 16, stride=128), :] for q in range(16)], axis=1
        ).astype(BF)
        hot_s = hot[src]
        sums += mm_nt(vals, jnp.concatenate([hot_s, hot_s], axis=0))
    s_gg[...] = jnp.concatenate([sums, jnp.zeros((16, 96), F32)], axis=1)
    x_gg.start()
    r_gg[a] = s_gg[...]

    for n in range(4):
        x_fl(n).recv()
    grid_a[...] = r_fl[...].reshape(2048, 128).astype(F32)
    gp2 = jnp.zeros((16, 128), F32)
    ctt = jnp.zeros((16, 128), F32)
    branch = []
    for h in range(2):
        hrow = slice(h * 128, (h + 1) * 128)
        filtered = jnp.concatenate(
            [grid_a[pl.ds(h * 8 + s, 128, stride=16), :] for s in range(8)], axis=1
        )
        branch.append((outer[hrow, :] * filtered).astype(BF))
        hot_h = hot[a, :, h * 1024 : (h + 1) * 1024]
        hi, lo = split(gbranch[hrow, :] * filtered)
        gp2 += mm_nt(hot_h, hi) + mm_nt(hot_h, lo)
        ctt += mm_nt(hot_h, cot_ref[:, h * 1024 : (h + 1) * 1024])
    s_seg[0] = gp2
    s_seg[1] = ctt
    x_seg.start()
    r_seg[a] = s_seg[...]
    s_out[...] = (
        mm_tn(w_two[...], jnp.concatenate(branch, axis=0)).astype(BF).reshape(NT, 16, 1024)
    )
    x_out.start()
    r_out[b] = s_out[b]

    x_gg.recv()
    x_seg.recv()
    seg = jnp.sum(r_seg[...], axis=0)
    ctt = seg[1]
    hi, rest = seg[0].astype(BF), seg[0] - seg[0].astype(BF).astype(F32)
    mid, low_part = split(rest)
    row48, lane48 = iota2(48, 128)
    place = ones_at(((row48 & 15) + 32) == lane48).astype(BF)
    gp2_t = mm_tn(jnp.concatenate([hi, mid, low_part], axis=0), place)
    table = tall[...]
    swapped = jnp.where(lane128 < 16, pltpu.roll(table, 112, 1), pltpu.roll(table, 16, 1))
    grads = jnp.where(lane128 < 32, r_gg[...].reshape(128, 128) * swapped, gp2_t)
    gfirst = jnp.zeros((128, 128), F32)
    for p in range(3):
        hi, lo = split(jnp.where(p_lane == p, grads, 0.0))
        gfirst += mm(r_mix[p], hi) + mm(r_mix[p], lo)
    share = jnp.sum(gfirst * r_tab[...].reshape(128, 128), axis=0, keepdims=True)
    share = jnp.broadcast_to(share, (128, 128))
    share = pltpu.roll(share, 48, 1) + pltpu.roll(share, 32, 1) + pltpu.roll(share, 16, 1)
    s_gt[...] = jnp.where(
        lane128 < 48, gfirst, jnp.where(lane128 < 64, share, 0.0)
    ).reshape(NT, 8, 128)
    x_gt.start()
    r_gt[b] = s_gt[b]

    x_gt.recv()
    gt = r_gt[...].reshape(128, 128).T
    gnt = jnp.zeros((16, 128), F32)
    for p in range(3):
        hi, lo = split(gt[p * 16 : (p + 1) * 16, :])
        block = blk_ref[:, p * 128 : (p + 1) * 128]
        gnt += mm_nt(hi, block) + mm_nt(lo, block)
    cross = jnp.sum(gt[48:64, :], axis=1, keepdims=True) * 0.125
    emb = emb_ref[...].astype(F32)
    scal_col = jnp.sum(jnp.where(lane16 == row16, scal_row, 0.0), axis=1, keepdims=True)
    small[16:24, :] = jnp.broadcast_to(
        jnp.sum(gnt * emb * scal_col, axis=0, keepdims=True), (8, 128)
    )
    small[0:16, :] = (
        ctt
        + scal_col * gain_row * gnt
        - emb * (scal_col * scal_col * scal_col * cross * (1.0 / WIDTH))
    )

    x_out.recv()
    for n in range(4):
        x_fg(n).recv()

    for exchange in (
        x_filt, x_tok, x_gf, x_gg, x_seg, x_back, x_tab, x_out, x_gt,
        *[x_fl(n) for n in range(4)], *[x_fg(n) for n in range(4)],
    ):
        exchange.drain()


def finish(
    out_hbm, fg_hbm, w_hbm, emb_hbm, small_hbm,
    lay_ref, fgrad_ref, egrad_ref, ggrad_ref,
    out_ref, fg_ref, w_ref, emb_ref, small_ref, grid, sem,
):
    pairs = (
        (fg_hbm, fg_ref), (out_hbm, out_ref), (w_hbm, w_ref), (emb_hbm, emb_ref),
        (small_hbm, small_ref),
    )
    copies = [pltpu.make_async_copy(src, dst, sem.at[n]) for n, (src, dst) in enumerate(pairs)]
    for copy in copies:
        copy.start()
    copies[0].wait()
    grid[...] = fg_ref[...].reshape(2048, 128).astype(F32)
    for q in range(16):
        fgrad_ref[:, q * 128 : (q + 1) * 128] = grid[pl.ds(q, 128, stride=16), :]
    for copy in copies[1:]:
        copy.wait()
    mixture = mm_tn(w_ref[...], out_ref[...].reshape(256, 1024))
    for h in range(2):
        hrow = slice(h * 128, (h + 1) * 128)
        lay_ref[:, h * 1024 : (h + 1) * 1024] = (emb_ref[hrow].astype(F32) + mixture[hrow]).astype(BF)
    egrad_ref[...] = small_ref[0:16, :]
    ggrad_ref[...] = small_ref[16:17, :]


def local(token_ids, embedding, norm_gain, proj_blocks, proj_mixers, out_blocks, out_mixers, filters, cotangent):
    vmem = pl.BlockSpec(memory_space=pltpu.VMEM)
    V = pltpu.VMEM
    scratch = [
        V((16, 128), jnp.int32), V((16, 128), BF), V((1, 128), F32), V((128, 384), BF),
        V((384, 16), BF), V((128, 128), BF), V((128, 16), BF), V((128, 2048), BF),
        V((256, 128), BF), V((128, 256), F32), V((640, 256), BF),
        V((NC, 16, 2048), BF),
        V((NC, 16, 128), jnp.int32),
        V((NC, 16, 16, 128), BF), V((NC, 16, 16, 128), BF),
        V((NC, 16, 16, 128), BF), V((NC, 16, 16, 128), BF),
        V((NC, 16, 16, 128), BF),
        V((16, 128), F32), V((NC, 16, 128), F32),
        V((2, 16, 128), F32), V((NC, 2, 16, 128), F32),
        V((NT, 16, 1024), BF), V((NT, 16, 1024), BF),
        V((NT, 8, 128), F32), V((NT, 8, 128), F32),
        V((NT, 16, 1024), BF),
        V((NT, 8, 128), F32), V((NT, 8, 128), F32),
        V((256, 256), BF), V((3, 128, 128), BF),
        V((NC, 16, 2048), BF),
        V((128, 128), F32), V((128, 128), F32),
        V((2048, 128), F32), V((2048, 128), F32),
        V((2048, 256), F32), V((2048, 256), F32), V((2048, 128), F32),
        V((256, 1024), F32), V((256, 1024), F32),
        pltpu.SemaphoreType.DMA((13, NC)), pltpu.SemaphoreType.DMA((13, NC)),
        pltpu.SemaphoreType.DMA((4, NT)), pltpu.SemaphoreType.DMA((4, NT)), pltpu.SemaphoreType.DMA((12,)),
    ]
    received = pl.pallas_call(
        kernel,
        out_shape=(
            jax.ShapeDtypeStruct((NT, 16, 1024), BF),
            jax.ShapeDtypeStruct((NC, 16, 16, 128), BF),
            jax.ShapeDtypeStruct((256, 256), BF),
            jax.ShapeDtypeStruct((256, 1024), BF),
            jax.ShapeDtypeStruct((24, 128), F32),
        ),
        in_specs=[pl.BlockSpec(memory_space=pltpu.HBM)] * 12,
        out_specs=(vmem,) * 5,
        scratch_shapes=scratch,
        compiler_params=pltpu.CompilerParams(
            collective_id=0, has_side_effects=True, vmem_limit_bytes=56 * 1024 * 1024
        ),
    )(
        token_ids.reshape(16, 128),
        embedding,
        norm_gain.reshape(1, 128),
        proj_blocks.reshape(128, 384),
        proj_mixers.reshape(384, 16),
        out_blocks.reshape(128, 128),
        out_mixers.reshape(128, 16),
        filters,
        cotangent,
        *dft_tables(),
    )
    layer_out, filter_grad, embed_grad, gain_grad = pl.pallas_call(
        finish,
        out_shape=(
            jax.ShapeDtypeStruct((128, 2048), BF),
            jax.ShapeDtypeStruct((128, 2048), F32),
            jax.ShapeDtypeStruct((16, 128), F32),
            jax.ShapeDtypeStruct((1, 128), F32),
        ),
        in_specs=[pl.BlockSpec(memory_space=pltpu.HBM)] * 5,
        out_specs=(vmem,) * 4,
        scratch_shapes=[
            V((NT, 16, 1024), BF), V((NC, 16, 16, 128), BF), V((256, 256), BF), V((256, 1024), BF),
            V((24, 128), F32), V((2048, 128), F32), pltpu.SemaphoreType.DMA((5,)),
        ],
        compiler_params=pltpu.CompilerParams(vmem_limit_bytes=56 * 1024 * 1024),
    )(*received)
    return layer_out, filter_grad, embed_grad, gain_grad.reshape(128)


def solution(mesh):
    in_specs = (
        P("ctx"),
        P(None, "tp"),
        P("tp"),
        P("tp", None, None),
        P(None, "tp", None, None),
        P("tp", None, None),
        P("tp", None, None),
        P("tp", "ctx"),
        P("tp", "ctx"),
    )
    out_specs = (P("tp", "ctx"), P("tp", "ctx"), P(None, "tp"), P("tp"))
    return jax.shard_map(local, mesh=mesh, in_specs=in_specs, out_specs=out_specs, check_vma=False)
```

```python
import jax
import jax.numpy as jnp
import numpy as np
from jax import lax
from jax.experimental import pallas as pl
from jax.experimental.pallas import tpu as pltpu
from jax.sharding import PartitionSpec as P

WIDTH = 2048
EPS = 1e-06
SPAN = 32768
NC = 8
NT = 16
BF = jnp.bfloat16
F32 = jnp.float32
MESH = pl.DeviceIdType.MESH

FILT_IN, TOK, GF, FIN, FILT, FG = 0, 1, 2, 3, 4, 8
BACK, TAB, OUT, GT = range(4)


def dft_tables():
    idx = np.arange(128)
    half = idx + 0.5
    first = 2 * np.pi * np.outer(half, idx) / 256.0
    c1 = np.concatenate([np.cos(first), -np.sin(first)], 0)
    twist = 2 * np.pi * np.outer(half, idx) / SPAN
    second = 2 * np.pi * (np.outer(idx, idx) % 128) / 128.0
    co, si = np.cos(second), np.sin(second)
    c2 = np.block([[co, -si], [si, co]])
    i1 = np.block([[co, si], [-si, co]])
    i2 = np.concatenate([np.cos(first.T), -np.sin(first.T)], 1) * (2.0 / SPAN)
    cast = lambda a, d: jnp.asarray(a, F32).astype(d)
    return (
        cast(c1, BF),
        cast(np.concatenate([np.cos(twist), np.sin(twist)], 1), F32),
        cast(np.concatenate([c2, i1, i2], 0), BF),
    )


def mm(a, b):
    return jnp.dot(a, b, preferred_element_type=F32)


def mm_tn(a, b):
    return lax.dot_general(a, b, (((0,), (0,)), ((), ())), preferred_element_type=F32)


def mm_nt(a, b):
    return lax.dot_general(a, b, (((1,), (1,)), ((), ())), preferred_element_type=F32)


def iota2(rows, lanes):
    return (
        lax.broadcasted_iota(jnp.int32, (rows, lanes), 0),
        lax.broadcasted_iota(jnp.int32, (rows, lanes), 1),
    )


def ones_at(cond):
    return jnp.where(cond, 1.0, 0.0).astype(F32)


def split(x):
    hi = x.astype(BF)
    return hi, (x - hi.astype(F32)).astype(BF)


def kernel(
    tok_hbm, emb_hbm, gain_hbm, blk_hbm, mix_hbm, oblk_hbm, omix_hbm, filt_hbm, cot_hbm,
    c1_hbm, turn_hbm, dft_hbm,
    r_out, r_fg, w_back, embedded, small,
    tok_ref, emb_ref, gain_ref, blk_ref, mix_ref, oblk_ref, omix_ref, cot_ref, c1_ref, turn_ref, dft_ref,
    r_filt, r_tok, s_gf, r_gf, s_fl, r_fl, s_fg, own_gg, s_fin, r_fin,
    s_back, r_back, s_tab, r_tab, s_out, s_gt, r_gt,
    w_two, r_mix, hot, firsts, tall, gated_t, grid_a, grid_b, spec_x, spec_g, spec_s, outer, gbranch,
    ssem_c, rsem_c, ssem_t, rsem_t, lsem,
):
    a = lax.axis_index("ctx")
    b = lax.axis_index("tp")

    def peer_of(axis, k):
        if axis == "tp":
            return lax.rem(b + k, NT)
        return lax.rem(a // 4 + k // 4, 2) * 4 + lax.rem(a % 4 + k % 4, 4)

    class Exchange:
        def __init__(self, axis, msg, src, dst):
            self.me, self.n = (a, NC) if axis == "ctx" else (b, NT)
            sends, recvs = (ssem_c, rsem_c) if axis == "ctx" else (ssem_t, rsem_t)

            def copy(k):
                peer = peer_of(axis, k)
                return pltpu.make_async_remote_copy(
                    src_ref=src(peer),
                    dst_ref=dst(self.me),
                    send_sem=sends.at[msg, k],
                    recv_sem=recvs.at[msg, k],
                    device_id={axis: peer},
                    device_id_type=MESH,
                )

            self.copy = copy

        def each(self, act, low=1, high=None):
            def body(k, carry):
                act(self.copy(k))
                return carry

            lax.fori_loop(low, high or self.n, body, 0)

        def start(self, low=1, high=None):
            self.each(lambda c: c.start(), low, high)

        def recv(self):
            self.each(lambda c: c.wait_recv())

        def drain(self):
            self.each(lambda c: c.wait_send())

    rows16 = lambda ref: (lambda p: ref.at[pl.ds(pl.multiple_of(p * 16, 16), 16), :])
    slot = lambda ref: (lambda p: ref.at[p])
    whole = lambda ref: (lambda p: ref)

    x_filt = Exchange("ctx", FILT_IN, rows16(filt_hbm), slot(r_filt))
    x_tok = Exchange("ctx", TOK, whole(tok_ref), slot(r_tok))
    x_gf = Exchange("ctx", GF, slot(s_gf), slot(r_gf))
    quarter = lambda ref, n: (lambda p: ref.at[p, pl.ds(n * 4, 4)])
    x_fl = lambda n: Exchange("ctx", FILT + n, quarter(s_fl, n), quarter(r_fl, n))
    x_fg = lambda n: Exchange("ctx", FG + n, quarter(s_fg, n), quarter(r_fg, n))
    x_fin = Exchange("ctx", FIN, whole(s_fin), slot(r_fin))
    x_back = Exchange("tp", BACK, slot(s_back), slot(r_back))
    x_tab = Exchange("tp", TAB, slot(s_tab), slot(r_tab))
    x_out = Exchange("tp", OUT, slot(s_out), slot(r_out))
    x_gt = Exchange("tp", GT, slot(s_gt), slot(r_gt))

    barrier = pltpu.get_barrier_semaphore()

    def greet(axis, n):
        def body(k, carry):
            pl.semaphore_signal(
                barrier, inc=1, device_id={axis: peer_of(axis, k)}, device_id_type=MESH
            )
            return carry

        lax.fori_loop(1, n, body, 0)

    greet("ctx", NC)
    greet("tp", NT)

    own = pl.ds(pl.multiple_of(a * 16, 16), 16)
    loads = {}
    for n, (name, src, dst) in enumerate(
        (
            ("emb", emb_hbm, emb_ref),
            ("gain", gain_hbm, gain_ref),
            ("blk", blk_hbm, blk_ref),
            ("omix", omix_hbm, omix_ref),
            ("cot", cot_hbm, cot_ref),
            ("tok", tok_hbm, tok_ref),
            ("mix", mix_hbm, mix_ref),
            ("oblk", oblk_hbm, oblk_ref),
            ("c1", c1_hbm, c1_ref),
            ("turn", turn_hbm, turn_ref),
            ("dft", dft_hbm, dft_ref),
            ("filt", filt_hbm.at[own, :], r_filt.at[a]),
        )
    ):
        loads[name] = pltpu.make_async_copy(src, dst, lsem.at[n])
        loads[name].start()

    row128, lane128 = iota2(128, 128)
    p_lane = lane128 >> 4
    row16, lane16 = iota2(16, 128)

    eye = ones_at(row128 == lane128).astype(BF)
    for name in ("emb", "gain", "blk"):
        loads[name].wait()
    gain_row = gain_ref[...]
    hi = gain_row.astype(BF).astype(F32)
    mid = (gain_row - hi).astype(BF).astype(F32)
    row8 = lax.broadcasted_iota(jnp.int32, (8, 128), 0)
    gains = jnp.where(row8 == 0, hi, jnp.where(row8 == 1, mid, gain_row - hi - mid))
    gains = jnp.where(row8 < 3, gains, 0.0)
    turned = [
        mm_tn(blk_ref[:, p * 128 : (p + 1) * 128], eye).reshape(NT, 8, 128) for p in range(3)
    ]
    turned.append(jnp.broadcast_to(gains[None], (NT, 8, 128)))
    s_tab[:, 0:32, :] = jnp.concatenate(turned, axis=1).astype(BF)
    s_tab[:, 32:48, :] = jnp.broadcast_to(emb_ref[...][None], (NT, 16, 128))

    tile_m = ones_at((lane16 & 15) == row16).astype(BF)
    row, lane = iota2(256, 128)
    sel_row = ones_at(((row & 7) == (lane >> 4)) & ((row >> 4) == (lane & 15))).astype(BF)
    loads["omix"].wait()
    wide = mm(sel_row, mm(omix_ref[...], tile_m).astype(BF))
    row, lane = iota2(256, 256)
    keep = ((row & 7) == ((lane >> 4) & 7)) & (((row >> 3) & 1) == (lane >> 7))
    w_back[...] = jnp.where(keep, jnp.concatenate([wide, wide], axis=1), 0.0).astype(BF)
    loads["cot"].wait()
    cot2 = jnp.concatenate([cot_ref[:, :1024], cot_ref[:, 1024:]], axis=0)
    s_back[...] = mm(w_back[...], cot2).astype(BF).reshape(NT, 16, 1024)

    loads["tok"].wait()
    pl.semaphore_wait(barrier, NC - 1 + NT - 1)
    x_tab.start()
    x_tok.start()
    x_back.start()
    x_filt.start()
    r_tab[b] = s_tab[b]
    r_tok[a] = tok_ref[...]
    r_back[b] = s_back[b]

    sel_p = ones_at(((row128 & 7) == p_lane) & ((row128 >> 3) == (lane128 & 15))).astype(BF)
    for name in ("mix", "oblk", "c1", "turn", "dft", "filt"):
        loads[name].wait()
    for p in range(3):
        wide = mm(sel_p, mm(mix_ref[p * 128 : (p + 1) * 128, :], tile_m).astype(BF))
        r_mix[p] = jnp.where((row128 & 7) == p_lane, wide, 0.0).astype(BF)

    row, lane = iota2(128, 256)
    sel_col = ones_at(((lane >> 4) * 8 + (lane & 7)) == row).astype(BF)
    wide = mm(oblk_ref[...], sel_col)
    low = ((lane >> 3) & 1) == 0
    w_two[...] = jnp.concatenate(
        [jnp.where(low, wide, 0.0), jnp.where(low, 0.0, wide)], axis=0
    ).astype(BF)

    x_tok.recv()
    for src in range(NC):
        ids = r_tok[src]
        for q in range(16):
            hot[src, :, q * 128 : (q + 1) * 128] = ones_at(
                jnp.broadcast_to(ids[q : q + 1, :], (16, 128)) == row16
            ).astype(BF)

    x_tab.recv()
    squares = jnp.zeros((16, 128), F32)
    for g in range(NT):
        part = r_tab[g, 32:48, :].astype(F32)
        squares += part * part
    scal_col = lax.rsqrt(jnp.sum(squares, axis=1, keepdims=True) * (1.0 / WIDTH) + EPS)
    scal_row = jnp.sum(
        jnp.where((lane16 & 15) == row16, scal_col, 0.0), axis=0, keepdims=True
    )
    pieces = []
    for g in range(NT):
        top = r_tab[g, 16:32, :].astype(F32)
        gain_g = top[8:9, :] + top[9:10, :] + top[10:11, :]
        normed = (r_tab[g, 32:48, :].astype(F32) * scal_col * gain_g).astype(BF)
        pieces.append(mm_nt(r_tab[g, 0:32, :], jnp.concatenate([normed] * 8, axis=0)))
    first = jnp.zeros((128, 128), F32)
    for p in range(3):
        part = jnp.concatenate([piece[p * 8 : (p + 1) * 8] for piece in pieces], axis=0)
        first += jnp.where(p_lane == p, part, 0.0)
    firsts[...] = first
    table = jnp.zeros((128, 128), F32)
    for p in range(3):
        table += mm_tn(r_mix[p], jnp.where(p_lane == p, first, 0.0).astype(BF))
    tall[...] = table
    gated_t[...] = table * pltpu.roll(table, 112, 1)
    outer_hi, outer_lo = split(pltpu.roll(table, 96, 1)[:, :16])
    outer_w = jnp.concatenate([outer_hi, outer_lo], axis=1)
    for h in range(2):
        hot_h = hot[a, :, h * 1024 : (h + 1) * 1024]
        outer[h * 128 : (h + 1) * 128, :] = mm(outer_w, jnp.concatenate([hot_h, hot_h], axis=0))
        embedded[h * 128 : (h + 1) * 128, :] = mm_tn(emb_ref[...], hot_h).astype(BF)

    mine = gated_t[pl.ds(pl.multiple_of(a * 16, 16), 16), :][:, :16].astype(BF)
    for src in range(NC):
        vals = mm(mine, hot[src])
        for q in range(16):
            grid_a[pl.ds(src * 16 + q, 16, stride=128), :] = vals[:, q * 128 : (q + 1) * 128]

    tc = turn_ref[:, :128]
    ts = turn_ref[:, 128:]
    c2_ref = dft_ref.at[0:256, :]
    i1_ref = dft_ref.at[256:512, :]
    i2_ref = dft_ref.at[512:640, :]
    tc2 = jnp.concatenate([tc, tc], axis=1)
    ts2 = jnp.concatenate([ts, ts], axis=1)

    def forward(signals, second):
        turned = []
        for u in range(0, len(signals), 2):
            stage = mm(c1_ref[...], jnp.concatenate(signals[u : u + 2], axis=1))
            re, im = stage[:128], stage[128:]
            tr = re * tc2 + im * ts2
            ti = im * tc2 - re * ts2
            for v in range(2):
                cols = slice(v * 128, (v + 1) * 128)
                turned.append(jnp.concatenate([tr[:, cols], ti[:, cols]], axis=1).astype(BF))
        return mm(jnp.concatenate(turned, axis=0), second)

    def inverse(spectrum, weights):
        back = mm(spectrum.astype(BF), weights)
        results = []
        for u in range(0, spectrum.shape[0], 256):
            both = [
                jnp.concatenate(
                    [back[u + v : u + v + 128, :128], back[u + v : u + v + 128, 128:]], axis=0
                )
                for v in (0, 128)
            ]
            both = jnp.concatenate(both, axis=1)
            re, im = both[:128], both[128:]
            turned = jnp.concatenate([re * tc2 - im * ts2, im * tc2 + re * ts2], axis=0)
            pair = mm(i2_ref[...], turned.astype(BF))
            results += [pair[:, :128], pair[:, 128:]]
        return results

    def groups(body):
        def step(n, carry):
            body(n)
            return carry

        lax.fori_loop(0, 4, step, 0)

    def rows_of(n):
        return pl.ds(pl.multiple_of(n * 512, 512), 512)

    def signals(ref, n):
        block = ref[rows_of(n), :].astype(BF)
        return [block[u * 128 : (u + 1) * 128] for u in range(4)]

    def gated_spectrum(n):
        spec_x[rows_of(n), :] = forward(signals(grid_a, n), c2_ref[...])

    groups(gated_spectrum)

    x_back.recv()
    gbranch[...] = mm(w_two[...], r_back[...].reshape(256, 1024))
    for h in range(2):
        for s in range(8):
            part = slice(s * 128, (s + 1) * 128)
            hrow = slice(h * 128, (h + 1) * 128)
            grid_a[pl.ds(h * 8 + s, 128, stride=16), :] = gbranch[hrow, part] * outer[hrow, part]
    s_gf[...] = grid_a[...].astype(BF).reshape(NC, 16, 16, 128)
    x_gf.start()
    r_gf[a] = s_gf[a]

    x_filt.recv()
    for src in range(NC):
        for q in range(16):
            grid_b[pl.ds(src * 16 + q, 16, stride=128), :] = r_filt[
                src, :, q * 128 : (q + 1) * 128
            ].astype(F32)

    def filtered_group(n):
        even = 2.0 * forward(signals(grid_b, n), c2_ref[:, :128])
        spec_s[rows_of(n), :] = even
        spectrum = spec_x[rows_of(n), :] * jnp.concatenate([even, even], axis=1)
        for u, result in enumerate(inverse(spectrum, i1_ref[...])):
            s_fl[:, n * 4 + u] = result.astype(BF).reshape(NC, 16, 128)
        x_fl(n).start()

    groups(filtered_group)
    r_fl[a] = s_fl[a]

    x_gf.recv()

    def grad_group(n):
        spectrum = forward([r_gf[:, n * 4 + u].reshape(128, 128) for u in range(4)], c2_ref[...])
        spec_g[rows_of(n), :] = spectrum
        prod = spectrum * spec_x[rows_of(n), :]
        cross = 2.0 * (prod[:, :128] + prod[:, 128:])
        for u, result in enumerate(inverse(cross, i1_ref[:128, :])):
            s_fg[:, n * 4 + u] = result.astype(BF).reshape(NC, 16, 128)
        x_fg(n).start()

    groups(grad_group)
    r_fg[a] = s_fg[a]

    def gated_group(n):
        even = spec_s[rows_of(n), :]
        spectrum = spec_g[rows_of(n), :] * jnp.concatenate([even, even], axis=1)
        for u, result in enumerate(inverse(spectrum, i1_ref[...])):
            start = pl.multiple_of(n * 512 + u * 128, 128)
            grid_b[pl.ds(start, 128), :] = result

    groups(gated_group)
    sums = jnp.zeros((16, 32), F32)
    for src in range(NC):
        vals = jnp.concatenate(
            [grid_b[pl.ds(src * 16 + q, 16, stride=128), :] for q in range(16)], axis=1
        ).astype(BF)
        hot_s = hot[src]
        sums += mm_nt(vals, jnp.concatenate([hot_s, hot_s], axis=0))
    own_gg[...] = jnp.zeros((128, 128), F32)
    own_gg[own, :] = jnp.concatenate([sums, jnp.zeros((16, 96), F32)], axis=1)

    for n in range(4):
        x_fl(n).recv()
    grid_a[...] = r_fl[...].reshape(2048, 128).astype(F32)
    gp2 = jnp.zeros((16, 128), F32)
    ctt = jnp.zeros((16, 128), F32)
    branch = []
    for h in range(2):
        hrow = slice(h * 128, (h + 1) * 128)
        filtered = jnp.concatenate(
            [grid_a[pl.ds(h * 8 + s, 128, stride=16), :] for s in range(8)], axis=1
        )
        branch.append((outer[hrow, :] * filtered).astype(BF))
        hot_h = hot[a, :, h * 1024 : (h + 1) * 1024]
        hi, lo = split(gbranch[hrow, :] * filtered)
        gp2 += mm_nt(hot_h, hi) + mm_nt(hot_h, lo)
        ctt += mm_nt(hot_h, cot_ref[:, h * 1024 : (h + 1) * 1024])

    hi = gp2.astype(BF)
    rest = gp2 - hi.astype(F32)
    mid, low_part = split(rest)
    row48, lane48 = iota2(48, 128)
    place = ones_at(((row48 & 15) + 32) == lane48).astype(BF)
    gp2_t = mm_tn(jnp.concatenate([hi, mid, low_part], axis=0), place)
    table = tall[...]
    swapped = jnp.where(lane128 < 16, pltpu.roll(table, 112, 1), pltpu.roll(table, 16, 1))
    grads = jnp.where(lane128 < 32, own_gg[...] * swapped, gp2_t)
    gfirst = jnp.zeros((128, 128), F32)
    for p in range(3):
        hi, lo = split(jnp.where(p_lane == p, grads, 0.0))
        gfirst += mm(r_mix[p], hi) + mm(r_mix[p], lo)
    share = jnp.sum(gfirst * firsts[...], axis=0, keepdims=True) / scal_row
    share = jnp.broadcast_to(share, (128, 128))
    share = pltpu.roll(share, 48, 1) + pltpu.roll(share, 32, 1) + pltpu.roll(share, 16, 1)
    s_gt[...] = jnp.where(
        lane128 < 48, gfirst, jnp.where(lane128 < 64, share, 0.0)
    ).reshape(NT, 8, 128)
    x_gt.start()
    r_gt[b] = s_gt[b]

    s_out[...] = (
        mm_tn(w_two[...], jnp.concatenate(branch, axis=0)).astype(BF).reshape(NT, 16, 1024)
    )
    x_out.start()
    r_out[b] = s_out[b]

    x_gt.recv()
    gt = r_gt[...].reshape(128, 128).T
    gnt = jnp.zeros((16, 128), F32)
    for p in range(3):
        hi, lo = split(gt[p * 16 : (p + 1) * 16, :])
        block = blk_ref[:, p * 128 : (p + 1) * 128]
        gnt += mm_nt(hi, block) + mm_nt(lo, block)
    cross = jnp.sum(gt[48:64, :], axis=1, keepdims=True) * 0.125
    emb = emb_ref[...].astype(F32)
    s_fin[16:24, :] = jnp.broadcast_to(
        jnp.sum(gnt * emb * scal_col, axis=0, keepdims=True), (8, 128)
    )
    s_fin[0:16, :] = (
        ctt
        + scal_col * gain_row * gnt
        - emb * (scal_col * scal_col * scal_col * cross * (1.0 / WIDTH))
    )
    x_fin.start()
    r_fin[a] = s_fin[...]
    x_fin.recv()
    small[...] = jnp.sum(r_fin[...], axis=0)

    x_out.recv()
    for n in range(4):
        x_fg(n).recv()

    for exchange in (
        x_filt, x_tok, x_gf, x_fin, x_back, x_tab, x_out, x_gt,
        *[x_fl(n) for n in range(4)], *[x_fg(n) for n in range(4)],
    ):
        exchange.drain()


def finish(
    out_hbm, fg_hbm, w_hbm, emb_hbm, small_hbm,
    lay_ref, fgrad_ref, egrad_ref, ggrad_ref,
    out_ref, fg_ref, w_ref, emb_ref, small_ref, grid, sem,
):
    pairs = (
        (fg_hbm, fg_ref), (out_hbm, out_ref), (w_hbm, w_ref), (emb_hbm, emb_ref),
        (small_hbm, small_ref),
    )
    copies = [pltpu.make_async_copy(src, dst, sem.at[n]) for n, (src, dst) in enumerate(pairs)]
    for copy in copies:
        copy.start()
    copies[0].wait()
    grid[...] = fg_ref[...].reshape(2048, 128).astype(F32)
    for q in range(16):
        fgrad_ref[:, q * 128 : (q + 1) * 128] = grid[pl.ds(q, 128, stride=16), :]
    for copy in copies[1:]:
        copy.wait()
    mixture = mm_tn(w_ref[...], out_ref[...].reshape(256, 1024))
    for h in range(2):
        hrow = slice(h * 128, (h + 1) * 128)
        lay_ref[:, h * 1024 : (h + 1) * 1024] = (emb_ref[hrow].astype(F32) + mixture[hrow]).astype(BF)
    egrad_ref[...] = small_ref[0:16, :]
    ggrad_ref[...] = small_ref[16:17, :]


def local(token_ids, embedding, norm_gain, proj_blocks, proj_mixers, out_blocks, out_mixers, filters, cotangent):
    vmem = pl.BlockSpec(memory_space=pltpu.VMEM)
    V = pltpu.VMEM
    scratch = [
        V((16, 128), jnp.int32), V((16, 128), BF), V((1, 128), F32), V((128, 384), BF),
        V((384, 16), BF), V((128, 128), BF), V((128, 16), BF), V((128, 2048), BF),
        V((256, 128), BF), V((128, 256), F32), V((640, 256), BF),
        V((NC, 16, 2048), BF),
        V((NC, 16, 128), jnp.int32),
        V((NC, 16, 16, 128), BF), V((NC, 16, 16, 128), BF),
        V((NC, 16, 16, 128), BF), V((NC, 16, 16, 128), BF),
        V((NC, 16, 16, 128), BF),
        V((128, 128), F32), V((24, 128), F32), V((NC, 24, 128), F32),
        V((NT, 16, 1024), BF), V((NT, 16, 1024), BF),
        V((NT, 48, 128), BF), V((NT, 48, 128), BF),
        V((NT, 16, 1024), BF),
        V((NT, 8, 128), F32), V((NT, 8, 128), F32),
        V((256, 256), BF), V((3, 128, 128), BF),
        V((NC, 16, 2048), BF),
        V((128, 128), F32), V((128, 128), F32), V((128, 128), F32),
        V((2048, 128), F32), V((2048, 128), F32),
        V((2048, 256), F32), V((2048, 256), F32), V((2048, 128), F32),
        V((256, 1024), F32), V((256, 1024), F32),
        pltpu.SemaphoreType.DMA((12, NC)), pltpu.SemaphoreType.DMA((12, NC)),
        pltpu.SemaphoreType.DMA((4, NT)), pltpu.SemaphoreType.DMA((4, NT)), pltpu.SemaphoreType.DMA((12,)),
    ]
    received = pl.pallas_call(
        kernel,
        out_shape=(
            jax.ShapeDtypeStruct((NT, 16, 1024), BF),
            jax.ShapeDtypeStruct((NC, 16, 16, 128), BF),
            jax.ShapeDtypeStruct((256, 256), BF),
            jax.ShapeDtypeStruct((256, 1024), BF),
            jax.ShapeDtypeStruct((24, 128), F32),
        ),
        in_specs=[pl.BlockSpec(memory_space=pltpu.HBM)] * 12,
        out_specs=(vmem,) * 5,
        scratch_shapes=scratch,
        compiler_params=pltpu.CompilerParams(
            collective_id=0, has_side_effects=True, vmem_limit_bytes=56 * 1024 * 1024
        ),
    )(
        token_ids.reshape(16, 128),
        embedding,
        norm_gain.reshape(1, 128),
        proj_blocks.reshape(128, 384),
        proj_mixers.reshape(384, 16),
        out_blocks.reshape(128, 128),
        out_mixers.reshape(128, 16),
        filters,
        cotangent,
        *dft_tables(),
    )
    layer_out, filter_grad, embed_grad, gain_grad = pl.pallas_call(
        finish,
        out_shape=(
            jax.ShapeDtypeStruct((128, 2048), BF),
            jax.ShapeDtypeStruct((128, 2048), F32),
            jax.ShapeDtypeStruct((16, 128), F32),
            jax.ShapeDtypeStruct((1, 128), F32),
        ),
        in_specs=[pl.BlockSpec(memory_space=pltpu.HBM)] * 5,
        out_specs=(vmem,) * 4,
        scratch_shapes=[
            V((NT, 16, 1024), BF), V((NC, 16, 16, 128), BF), V((256, 256), BF), V((256, 1024), BF),
            V((24, 128), F32), V((2048, 128), F32), pltpu.SemaphoreType.DMA((5,)),
        ],
        compiler_params=pltpu.CompilerParams(vmem_limit_bytes=56 * 1024 * 1024),
    )(*received)
    return layer_out, filter_grad, embed_grad, gain_grad.reshape(128)


def solution(mesh):
    in_specs = (
        P("ctx"),
        P(None, "tp"),
        P("tp"),
        P("tp", None, None),
        P(None, "tp", None, None),
        P("tp", None, None),
        P("tp", None, None),
        P("tp", "ctx"),
        P("tp", "ctx"),
    )
    out_specs = (P("tp", "ctx"), P("tp", "ctx"), P(None, "tp"), P("tp"))
    return jax.shard_map(local, mesh=mesh, in_specs=in_specs, out_specs=out_specs, check_vma=False)
```

```python
import jax
import jax.numpy as jnp
import numpy as np
from jax import lax
from jax.experimental import pallas as pl
from jax.experimental.pallas import tpu as pltpu
from jax.sharding import PartitionSpec as P

WIDTH = 2048
EPS = 1e-06
SPAN = 32768
NC = 8
NT = 16
BF = jnp.bfloat16
F32 = jnp.float32
MESH = pl.DeviceIdType.MESH

FILT_IN, TOK, GF, FIN, FILT, FG = 0, 1, 2, 3, 4, 8
BACK, TAB, OUT, GT = range(4)


def dft_tables():
    idx = np.arange(128)
    half = idx + 0.5
    first = 2 * np.pi * np.outer(half, idx) / 256.0
    c1 = np.concatenate([np.cos(first), -np.sin(first)], 0)
    twist = 2 * np.pi * np.outer(half, idx) / SPAN
    second = 2 * np.pi * (np.outer(idx, idx) % 128) / 128.0
    co, si = np.cos(second), np.sin(second)
    c2 = np.block([[co, -si], [si, co]])
    i1 = np.block([[co, si], [-si, co]])
    i2 = np.concatenate([np.cos(first.T), -np.sin(first.T)], 1) * (2.0 / SPAN)
    cast = lambda a, d: jnp.asarray(a, F32).astype(d)
    return (
        cast(c1, BF),
        cast(np.concatenate([np.cos(twist), np.sin(twist)], 1), F32),
        cast(np.concatenate([c2, i1, i2], 0), BF),
    )


def mm(a, b):
    return jnp.dot(a, b, preferred_element_type=F32)


def mm_tn(a, b):
    return lax.dot_general(a, b, (((0,), (0,)), ((), ())), preferred_element_type=F32)


def mm_nt(a, b):
    return lax.dot_general(a, b, (((1,), (1,)), ((), ())), preferred_element_type=F32)


def iota2(rows, lanes):
    return (
        lax.broadcasted_iota(jnp.int32, (rows, lanes), 0),
        lax.broadcasted_iota(jnp.int32, (rows, lanes), 1),
    )


def ones_at(cond):
    return jnp.where(cond, 1.0, 0.0).astype(F32)


def split(x):
    hi = x.astype(BF)
    return hi, (x - hi.astype(F32)).astype(BF)


def kernel(
    tok_hbm, emb_hbm, gain_hbm, blk_hbm, mix_hbm, oblk_hbm, omix_hbm, filt_hbm, cot_hbm,
    c1_hbm, turn_hbm, dft_hbm,
    r_out, fgrad, w_back, embedded, small,
    tok_ref, emb_ref, gain_ref, blk_ref, mix_ref, oblk_ref, omix_ref, cot_ref, c1_ref, turn_ref, dft_ref,
    r_filt, r_tok, s_gf, r_gf, s_fl, r_fl, s_fg, r_fg, own_gg, s_fin, r_fin,
    s_back, r_back, s_tab, r_tab, s_out, s_gt, r_gt,
    w_two, r_mix, hot, firsts, tall, gated_t, grid_a, grid_b, spec_x, spec_g, spec_s, outer, gbranch,
    ssem_c, rsem_c, ssem_t, rsem_t, lsem,
):
    a = lax.axis_index("ctx")
    b = lax.axis_index("tp")

    def peer_of(axis, k):
        if axis == "tp":
            return lax.rem(b + k, NT)
        return lax.rem(a // 4 + k // 4, 2) * 4 + lax.rem(a % 4 + k % 4, 4)

    class Exchange:
        def __init__(self, axis, msg, src, dst):
            self.me, self.n = (a, NC) if axis == "ctx" else (b, NT)
            sends, recvs = (ssem_c, rsem_c) if axis == "ctx" else (ssem_t, rsem_t)

            def copy(k):
                peer = peer_of(axis, k)
                return pltpu.make_async_remote_copy(
                    src_ref=src(peer),
                    dst_ref=dst(self.me),
                    send_sem=sends.at[msg, k],
                    recv_sem=recvs.at[msg, k],
                    device_id={axis: peer},
                    device_id_type=MESH,
                )

            self.copy = copy

        def each(self, act, low=1, high=None):
            def body(k, carry):
                act(self.copy(k))
                return carry

            lax.fori_loop(low, high or self.n, body, 0)

        def start(self, low=1, high=None):
            self.each(lambda c: c.start(), low, high)

        def recv(self):
            self.each(lambda c: c.wait_recv())

        def drain(self):
            self.each(lambda c: c.wait_send())

    rows16 = lambda ref: (lambda p: ref.at[pl.ds(pl.multiple_of(p * 16, 16), 16), :])
    slot = lambda ref: (lambda p: ref.at[p])
    whole = lambda ref: (lambda p: ref)

    x_filt = Exchange("ctx", FILT_IN, rows16(filt_hbm), slot(r_filt))
    x_tok = Exchange("ctx", TOK, whole(tok_ref), slot(r_tok))
    x_gf = Exchange("ctx", GF, slot(s_gf), slot(r_gf))
    quarter = lambda ref, n: (lambda p: ref.at[p, pl.ds(n * 4, 4)])
    x_fl = lambda n: Exchange("ctx", FILT + n, quarter(s_fl, n), quarter(r_fl, n))
    x_fg = lambda n: Exchange("ctx", FG + n, quarter(s_fg, n), quarter(r_fg, n))
    x_fin = Exchange("ctx", FIN, whole(s_fin), slot(r_fin))
    x_back = Exchange("tp", BACK, slot(s_back), slot(r_back))
    x_tab = Exchange("tp", TAB, slot(s_tab), slot(r_tab))
    x_out = Exchange("tp", OUT, slot(s_out), slot(r_out))
    x_gt = Exchange("tp", GT, slot(s_gt), slot(r_gt))

    barrier = pltpu.get_barrier_semaphore()

    def greet(axis, n):
        def body(k, carry):
            pl.semaphore_signal(
                barrier, inc=1, device_id={axis: peer_of(axis, k)}, device_id_type=MESH
            )
            return carry

        lax.fori_loop(1, n, body, 0)

    greet("ctx", NC)
    greet("tp", NT)

    own = pl.ds(pl.multiple_of(a * 16, 16), 16)
    loads = {}
    for n, (name, src, dst) in enumerate(
        (
            ("emb", emb_hbm, emb_ref),
            ("gain", gain_hbm, gain_ref),
            ("blk", blk_hbm, blk_ref),
            ("omix", omix_hbm, omix_ref),
            ("cot", cot_hbm, cot_ref),
            ("tok", tok_hbm, tok_ref),
            ("mix", mix_hbm, mix_ref),
            ("oblk", oblk_hbm, oblk_ref),
            ("c1", c1_hbm, c1_ref),
            ("turn", turn_hbm, turn_ref),
            ("dft", dft_hbm, dft_ref),
            ("filt", filt_hbm.at[own, :], r_filt.at[a]),
        )
    ):
        loads[name] = pltpu.make_async_copy(src, dst, lsem.at[n])
        loads[name].start()

    row128, lane128 = iota2(128, 128)
    p_lane = lane128 >> 4
    row16, lane16 = iota2(16, 128)

    eye = ones_at(row128 == lane128).astype(BF)
    for name in ("emb", "gain", "blk"):
        loads[name].wait()
    gain_row = gain_ref[...]
    hi = gain_row.astype(BF).astype(F32)
    mid = (gain_row - hi).astype(BF).astype(F32)
    row8 = lax.broadcasted_iota(jnp.int32, (8, 128), 0)
    gains = jnp.where(row8 == 0, hi, jnp.where(row8 == 1, mid, gain_row - hi - mid))
    gains = jnp.where(row8 < 3, gains, 0.0)
    turned = [
        mm_tn(blk_ref[:, p * 128 : (p + 1) * 128], eye).reshape(NT, 8, 128) for p in range(3)
    ]
    turned.append(jnp.broadcast_to(gains[None], (NT, 8, 128)))
    s_tab[:, 0:32, :] = jnp.concatenate(turned, axis=1).astype(BF)
    s_tab[:, 32:48, :] = jnp.broadcast_to(emb_ref[...][None], (NT, 16, 128))

    tile_m = ones_at((lane16 & 15) == row16).astype(BF)
    row, lane = iota2(256, 128)
    sel_row = ones_at(((row & 7) == (lane >> 4)) & ((row >> 4) == (lane & 15))).astype(BF)
    loads["omix"].wait()
    wide = mm(sel_row, mm(omix_ref[...], tile_m).astype(BF))
    row, lane = iota2(256, 256)
    keep = ((row & 7) == ((lane >> 4) & 7)) & (((row >> 3) & 1) == (lane >> 7))
    w_back[...] = jnp.where(keep, jnp.concatenate([wide, wide], axis=1), 0.0).astype(BF)
    loads["cot"].wait()
    cot2 = jnp.concatenate([cot_ref[:, :1024], cot_ref[:, 1024:]], axis=0)
    s_back[...] = mm(w_back[...], cot2).astype(BF).reshape(NT, 16, 1024)

    loads["tok"].wait()
    pl.semaphore_wait(barrier, NC - 1 + NT - 1)
    x_tab.start()
    x_tok.start()
    x_back.start()
    x_filt.start()
    r_tab[b] = s_tab[b]
    r_tok[a] = tok_ref[...]
    r_back[b] = s_back[b]

    sel_p = ones_at(((row128 & 7) == p_lane) & ((row128 >> 3) == (lane128 & 15))).astype(BF)
    for name in ("mix", "oblk", "c1", "turn", "dft", "filt"):
        loads[name].wait()
    for p in range(3):
        wide = mm(sel_p, mm(mix_ref[p * 128 : (p + 1) * 128, :], tile_m).astype(BF))
        r_mix[p] = jnp.where((row128 & 7) == p_lane, wide, 0.0).astype(BF)

    row, lane = iota2(128, 256)
    sel_col = ones_at(((lane >> 4) * 8 + (lane & 7)) == row).astype(BF)
    wide = mm(oblk_ref[...], sel_col)
    low = ((lane >> 3) & 1) == 0
    w_two[...] = jnp.concatenate(
        [jnp.where(low, wide, 0.0), jnp.where(low, 0.0, wide)], axis=0
    ).astype(BF)

    x_tok.recv()
    for src in range(NC):
        ids = r_tok[src]
        for q in range(16):
            hot[src, :, q * 128 : (q + 1) * 128] = ones_at(
                jnp.broadcast_to(ids[q : q + 1, :], (16, 128)) == row16
            ).astype(BF)

    x_tab.recv()
    squares = jnp.zeros((16, 128), F32)
    for g in range(NT):
        part = r_tab[g, 32:48, :].astype(F32)
        squares += part * part
    scal_col = lax.rsqrt(jnp.sum(squares, axis=1, keepdims=True) * (1.0 / WIDTH) + EPS)
    scal_row = jnp.sum(
        jnp.where((lane16 & 15) == row16, scal_col, 0.0), axis=0, keepdims=True
    )
    pieces = []
    for g in range(NT):
        top = r_tab[g, 16:32, :].astype(F32)
        gain_g = top[8:9, :] + top[9:10, :] + top[10:11, :]
        normed = (r_tab[g, 32:48, :].astype(F32) * scal_col * gain_g).astype(BF)
        pieces.append(mm_nt(r_tab[g, 0:32, :], jnp.concatenate([normed] * 8, axis=0)))
    first = jnp.zeros((128, 128), F32)
    for p in range(3):
        part = jnp.concatenate([piece[p * 8 : (p + 1) * 8] for piece in pieces], axis=0)
        first += jnp.where(p_lane == p, part, 0.0)
    firsts[...] = first
    table = jnp.zeros((128, 128), F32)
    for p in range(3):
        table += mm_tn(r_mix[p], jnp.where(p_lane == p, first, 0.0).astype(BF))
    tall[...] = table
    gated_t[...] = table * pltpu.roll(table, 112, 1)
    outer_hi, outer_lo = split(pltpu.roll(table, 96, 1)[:, :16])
    outer_w = jnp.concatenate([outer_hi, outer_lo], axis=1)
    for h in range(2):
        hot_h = hot[a, :, h * 1024 : (h + 1) * 1024]
        outer[h * 128 : (h + 1) * 128, :] = mm(outer_w, jnp.concatenate([hot_h, hot_h], axis=0))
        embedded[h * 128 : (h + 1) * 128, :] = mm_tn(emb_ref[...], hot_h).astype(BF)

    mine = gated_t[pl.ds(pl.multiple_of(a * 16, 16), 16), :][:, :16].astype(BF)
    for src in range(NC):
        vals = mm(mine, hot[src])
        for q in range(16):
            grid_a[pl.ds(src * 16 + q, 16, stride=128), :] = vals[:, q * 128 : (q + 1) * 128]

    tc = turn_ref[:, :128]
    ts = turn_ref[:, 128:]
    c2_ref = dft_ref.at[0:256, :]
    i1_ref = dft_ref.at[256:512, :]
    i2_ref = dft_ref.at[512:640, :]
    tc2 = jnp.concatenate([tc, tc], axis=1)
    ts2 = jnp.concatenate([ts, ts], axis=1)

    def forward(signals, second):
        turned = []
        for u in range(0, len(signals), 2):
            stage = mm(c1_ref[...], jnp.concatenate(signals[u : u + 2], axis=1))
            re, im = stage[:128], stage[128:]
            tr = re * tc2 + im * ts2
            ti = im * tc2 - re * ts2
            for v in range(2):
                cols = slice(v * 128, (v + 1) * 128)
                turned.append(jnp.concatenate([tr[:, cols], ti[:, cols]], axis=1).astype(BF))
        return mm(jnp.concatenate(turned, axis=0), second)

    def inverse(spectrum, weights):
        back = mm(spectrum.astype(BF), weights)
        results = []
        for u in range(0, spectrum.shape[0], 256):
            both = [
                jnp.concatenate(
                    [back[u + v : u + v + 128, :128], back[u + v : u + v + 128, 128:]], axis=0
                )
                for v in (0, 128)
            ]
            both = jnp.concatenate(both, axis=1)
            re, im = both[:128], both[128:]
            turned = jnp.concatenate([re * tc2 - im * ts2, im * tc2 + re * ts2], axis=0)
            pair = mm(i2_ref[...], turned.astype(BF))
            results += [pair[:, :128], pair[:, 128:]]
        return results

    def groups(body):
        def step(n, carry):
            body(n)
            return carry

        lax.fori_loop(0, 4, step, 0)

    def rows_of(n):
        return pl.ds(pl.multiple_of(n * 512, 512), 512)

    def signals(ref, n):
        block = ref[rows_of(n), :].astype(BF)
        return [block[u * 128 : (u + 1) * 128] for u in range(4)]

    def gated_spectrum(n):
        spec_x[rows_of(n), :] = forward(signals(grid_a, n), c2_ref[...])

    groups(gated_spectrum)

    x_back.recv()
    gbranch[...] = mm(w_two[...], r_back[...].reshape(256, 1024))
    for h in range(2):
        for s in range(8):
            part = slice(s * 128, (s + 1) * 128)
            hrow = slice(h * 128, (h + 1) * 128)
            grid_a[pl.ds(h * 8 + s, 128, stride=16), :] = gbranch[hrow, part] * outer[hrow, part]
    s_gf[...] = grid_a[...].astype(BF).reshape(NC, 16, 16, 128)
    x_gf.start()
    r_gf[a] = s_gf[a]

    x_filt.recv()
    for src in range(NC):
        for q in range(16):
            grid_b[pl.ds(src * 16 + q, 16, stride=128), :] = r_filt[
                src, :, q * 128 : (q + 1) * 128
            ].astype(F32)

    def filtered_group(n):
        even = 2.0 * forward(signals(grid_b, n), c2_ref[:, :128])
        spec_s[rows_of(n), :] = even
        spectrum = spec_x[rows_of(n), :] * jnp.concatenate([even, even], axis=1)
        for u, result in enumerate(inverse(spectrum, i1_ref[...])):
            s_fl[:, n * 4 + u] = result.astype(BF).reshape(NC, 16, 128)
        x_fl(n).start()

    groups(filtered_group)
    r_fl[a] = s_fl[a]

    x_gf.recv()

    def grad_group(n):
        spectrum = forward([r_gf[:, n * 4 + u].reshape(128, 128) for u in range(4)], c2_ref[...])
        spec_g[rows_of(n), :] = spectrum
        prod = spectrum * spec_x[rows_of(n), :]
        cross = 2.0 * (prod[:, :128] + prod[:, 128:])
        for u, result in enumerate(inverse(cross, i1_ref[:128, :])):
            s_fg[:, n * 4 + u] = result.astype(BF).reshape(NC, 16, 128)
        x_fg(n).start()

    groups(grad_group)
    r_fg[a] = s_fg[a]

    def gated_group(n):
        even = spec_s[rows_of(n), :]
        spectrum = spec_g[rows_of(n), :] * jnp.concatenate([even, even], axis=1)
        for u, result in enumerate(inverse(spectrum, i1_ref[...])):
            start = pl.multiple_of(n * 512 + u * 128, 128)
            grid_b[pl.ds(start, 128), :] = result

    groups(gated_group)
    sums = jnp.zeros((16, 32), F32)
    for src in range(NC):
        vals = jnp.concatenate(
            [grid_b[pl.ds(src * 16 + q, 16, stride=128), :] for q in range(16)], axis=1
        ).astype(BF)
        hot_s = hot[src]
        sums += mm_nt(vals, jnp.concatenate([hot_s, hot_s], axis=0))
    own_gg[...] = jnp.zeros((128, 128), F32)
    own_gg[own, :] = jnp.concatenate([sums, jnp.zeros((16, 96), F32)], axis=1)

    for n in range(4):
        x_fl(n).recv()
    grid_a[...] = r_fl[...].reshape(2048, 128).astype(F32)
    gp2 = jnp.zeros((16, 128), F32)
    ctt = jnp.zeros((16, 128), F32)
    branch = []
    for h in range(2):
        hrow = slice(h * 128, (h + 1) * 128)
        filtered = jnp.concatenate(
            [grid_a[pl.ds(h * 8 + s, 128, stride=16), :] for s in range(8)], axis=1
        )
        branch.append((outer[hrow, :] * filtered).astype(BF))
        hot_h = hot[a, :, h * 1024 : (h + 1) * 1024]
        hi, lo = split(gbranch[hrow, :] * filtered)
        gp2 += mm_nt(hot_h, hi) + mm_nt(hot_h, lo)
        ctt += mm_nt(hot_h, cot_ref[:, h * 1024 : (h + 1) * 1024])

    hi = gp2.astype(BF)
    rest = gp2 - hi.astype(F32)
    mid, low_part = split(rest)
    row48, lane48 = iota2(48, 128)
    place = ones_at(((row48 & 15) + 32) == lane48).astype(BF)
    gp2_t = mm_tn(jnp.concatenate([hi, mid, low_part], axis=0), place)
    table = tall[...]
    swapped = jnp.where(lane128 < 16, pltpu.roll(table, 112, 1), pltpu.roll(table, 16, 1))
    grads = jnp.where(lane128 < 32, own_gg[...] * swapped, gp2_t)
    gfirst = jnp.zeros((128, 128), F32)
    for p in range(3):
        hi, lo = split(jnp.where(p_lane == p, grads, 0.0))
        gfirst += mm(r_mix[p], hi) + mm(r_mix[p], lo)
    share = jnp.sum(gfirst * firsts[...], axis=0, keepdims=True) / scal_row
    share = jnp.broadcast_to(share, (128, 128))
    share = pltpu.roll(share, 48, 1) + pltpu.roll(share, 32, 1) + pltpu.roll(share, 16, 1)
    s_gt[...] = jnp.where(
        lane128 < 48, gfirst, jnp.where(lane128 < 64, share, 0.0)
    ).reshape(NT, 8, 128)
    x_gt.start()
    r_gt[b] = s_gt[b]

    s_out[...] = (
        mm_tn(w_two[...], jnp.concatenate(branch, axis=0)).astype(BF).reshape(NT, 16, 1024)
    )
    x_out.start()
    r_out[b] = s_out[b]

    x_gt.recv()
    gt = r_gt[...].reshape(128, 128).T
    gnt = jnp.zeros((16, 128), F32)
    for p in range(3):
        hi, lo = split(gt[p * 16 : (p + 1) * 16, :])
        block = blk_ref[:, p * 128 : (p + 1) * 128]
        gnt += mm_nt(hi, block) + mm_nt(lo, block)
    cross = jnp.sum(gt[48:64, :], axis=1, keepdims=True) * 0.125
    emb = emb_ref[...].astype(F32)
    s_fin[16:24, :] = jnp.broadcast_to(
        jnp.sum(gnt * emb * scal_col, axis=0, keepdims=True), (8, 128)
    )
    s_fin[0:16, :] = (
        ctt
        + scal_col * gain_row * gnt
        - emb * (scal_col * scal_col * scal_col * cross * (1.0 / WIDTH))
    )
    x_fin.start()
    r_fin[a] = s_fin[...]
    for n in range(4):
        x_fg(n).recv()
    grid_a[...] = r_fg[...].reshape(2048, 128).astype(F32)
    for q in range(16):
        fgrad[:, q * 128 : (q + 1) * 128] = grid_a[pl.ds(q, 128, stride=16), :]
    x_fin.recv()
    small[...] = jnp.sum(r_fin[...], axis=0)
    x_out.recv()

    for exchange in (
        x_filt, x_tok, x_gf, x_fin, x_back, x_tab, x_out, x_gt,
        *[x_fl(n) for n in range(4)], *[x_fg(n) for n in range(4)],
    ):
        exchange.drain()


def finish(
    out_ref, fgrad_ref, w_ref, emb_ref, small_ref,
    lay_hbm, fgrad_hbm, egrad_ref, ggrad_ref,
    lay, sem,
):
    copies = [pltpu.make_async_copy(fgrad_ref, fgrad_hbm, sem.at[2])]
    copies[0].start()
    mixture = mm_tn(w_ref[...], out_ref[...].reshape(256, 1024))
    for h in range(2):
        hrow = slice(h * 128, (h + 1) * 128)
        cols = slice(h * 1024, (h + 1) * 1024)
        lay[:, cols] = (emb_ref[hrow].astype(F32) + mixture[hrow]).astype(BF)
        copies.append(pltpu.make_async_copy(lay.at[:, cols], lay_hbm.at[:, cols], sem.at[h]))
        copies[-1].start()
    egrad_ref[...] = small_ref[0:16, :]
    ggrad_ref[...] = small_ref[16:17, :]
    for copy in copies:
        copy.wait()


def local(token_ids, embedding, norm_gain, proj_blocks, proj_mixers, out_blocks, out_mixers, filters, cotangent):
    vmem = pl.BlockSpec(memory_space=pltpu.VMEM)
    hbm = pl.BlockSpec(memory_space=pltpu.HBM)
    V = pltpu.VMEM
    scratch = [
        V((16, 128), jnp.int32), V((16, 128), BF), V((1, 128), F32), V((128, 384), BF),
        V((384, 16), BF), V((128, 128), BF), V((128, 16), BF), V((128, 2048), BF),
        V((256, 128), BF), V((128, 256), F32), V((640, 256), BF),
        V((NC, 16, 2048), BF),
        V((NC, 16, 128), jnp.int32),
        V((NC, 16, 16, 128), BF), V((NC, 16, 16, 128), BF),
        V((NC, 16, 16, 128), BF), V((NC, 16, 16, 128), BF),
        V((NC, 16, 16, 128), BF), V((NC, 16, 16, 128), BF),
        V((128, 128), F32), V((24, 128), F32), V((NC, 24, 128), F32),
        V((NT, 16, 1024), BF), V((NT, 16, 1024), BF),
        V((NT, 48, 128), BF), V((NT, 48, 128), BF),
        V((NT, 16, 1024), BF),
        V((NT, 8, 128), F32), V((NT, 8, 128), F32),
        V((256, 256), BF), V((3, 128, 128), BF),
        V((NC, 16, 2048), BF),
        V((128, 128), F32), V((128, 128), F32), V((128, 128), F32),
        V((2048, 128), F32), V((2048, 128), F32),
        V((2048, 256), F32), V((2048, 256), F32), V((2048, 128), F32),
        V((256, 1024), F32), V((256, 1024), F32),
        pltpu.SemaphoreType.DMA((12, NC)), pltpu.SemaphoreType.DMA((12, NC)),
        pltpu.SemaphoreType.DMA((4, NT)), pltpu.SemaphoreType.DMA((4, NT)), pltpu.SemaphoreType.DMA((12,)),
    ]
    operands = (
        token_ids.reshape(16, 128),
        embedding,
        norm_gain.reshape(1, 128),
        proj_blocks.reshape(128, 384),
        proj_mixers.reshape(384, 16),
        out_blocks.reshape(128, 128),
        out_mixers.reshape(128, 16),
        filters,
        cotangent,
        *dft_tables(),
    )
    received = pl.pallas_call(
        kernel,
        out_shape=(
            jax.ShapeDtypeStruct((NT, 16, 1024), BF),
            jax.ShapeDtypeStruct((128, 2048), F32),
            jax.ShapeDtypeStruct((256, 256), BF),
            jax.ShapeDtypeStruct((256, 1024), BF),
            jax.ShapeDtypeStruct((24, 128), F32),
        ),
        in_specs=[hbm] * 12,
        out_specs=(vmem,) * 5,
        scratch_shapes=scratch,
        compiler_params=pltpu.CompilerParams(
            collective_id=0, has_side_effects=True, vmem_limit_bytes=40 * 1024 * 1024
        ),
    )(
        *[pltpu.with_memory_space_constraint(x, pltpu.HBM) for x in operands]
    )
    layer_out, filter_grad, embed_grad, gain_grad = pl.pallas_call(
        finish,
        out_shape=(
            jax.ShapeDtypeStruct((128, 2048), BF),
            jax.ShapeDtypeStruct((128, 2048), F32),
            jax.ShapeDtypeStruct((16, 128), F32),
            jax.ShapeDtypeStruct((1, 128), F32),
        ),
        in_specs=[vmem] * 5,
        out_specs=(hbm, hbm, vmem, vmem),
        scratch_shapes=[
            V((128, 2048), BF), pltpu.SemaphoreType.DMA((3,)),
        ],
        compiler_params=pltpu.CompilerParams(vmem_limit_bytes=16 * 1024 * 1024),
    )(*received)
    return layer_out, filter_grad, embed_grad, gain_grad.reshape(128)


def solution(mesh):
    in_specs = (
        P("ctx"),
        P(None, "tp"),
        P("tp"),
        P("tp", None, None),
        P(None, "tp", None, None),
        P("tp", None, None),
        P("tp", None, None),
        P("tp", "ctx"),
        P("tp", "ctx"),
    )
    out_specs = (P("tp", "ctx"), P("tp", "ctx"), P(None, "tp"), P("tp"))
    return jax.shard_map(local, mesh=mesh, in_specs=in_specs, out_specs=out_specs, check_vma=False)
```

```python
import jax
import jax.numpy as jnp
import numpy as np
from jax import lax
from jax.experimental import pallas as pl
from jax.experimental.pallas import tpu as pltpu
from jax.sharding import PartitionSpec as P

WIDTH = 2048
EPS = 1e-06
SPAN = 32768
NC = 8
NT = 16
BF = jnp.bfloat16
F32 = jnp.float32
MESH = pl.DeviceIdType.MESH

FILT_IN, TOK, GF, FIN, FILT, FG = 0, 1, 2, 3, 4, 6
BACK, TAB, OUT, GT = range(4)


def dft_tables():
    idx = np.arange(128)
    half = idx + 0.5
    first = 2 * np.pi * np.outer(half, idx) / 256.0
    c1 = np.concatenate([np.cos(first), -np.sin(first)], 0)
    twist = 2 * np.pi * np.outer(half, idx) / SPAN
    second = 2 * np.pi * (np.outer(idx, idx) % 128) / 128.0
    co, si = np.cos(second), np.sin(second)
    c2 = np.block([[co, -si], [si, co]])
    i1 = np.block([[co, si], [-si, co]])
    i2 = np.concatenate([np.cos(first.T), -np.sin(first.T)], 1) * (2.0 / SPAN)
    cast = lambda a, d: jnp.asarray(a, F32).astype(d)
    return (
        cast(c1, BF),
        cast(np.concatenate([np.cos(twist), np.sin(twist)], 1), F32),
        cast(np.concatenate([c2, i1, i2], 0), BF),
    )


def mm(a, b):
    return jnp.dot(a, b, preferred_element_type=F32)


def mm_tn(a, b):
    return lax.dot_general(a, b, (((0,), (0,)), ((), ())), preferred_element_type=F32)


def mm_nt(a, b):
    return lax.dot_general(a, b, (((1,), (1,)), ((), ())), preferred_element_type=F32)


def iota2(rows, lanes):
    return (
        lax.broadcasted_iota(jnp.int32, (rows, lanes), 0),
        lax.broadcasted_iota(jnp.int32, (rows, lanes), 1),
    )


def ones_at(cond):
    return jnp.where(cond, 1.0, 0.0).astype(F32)


def split(x):
    hi = x.astype(BF)
    return hi, (x - hi.astype(F32)).astype(BF)


def kernel(
    tok_hbm, emb_hbm, gain_hbm, blk_hbm, mix_hbm, oblk_hbm, omix_hbm, filt_hbm, cot_hbm,
    c1_hbm, turn_hbm, dft_hbm,
    r_out, fgrad, w_back, embedded, small,
    tok_ref, emb_ref, gain_ref, blk_ref, mix_ref, oblk_ref, omix_ref, cot_ref, c1_ref, turn_ref, dft_ref,
    r_filt, r_tok, s_gf, r_gf, s_fl, r_fl, s_fg, r_fg, own_gg, s_fin, r_fin,
    s_back, r_back, s_tab, r_tab, s_out, s_gt, r_gt,
    w_two, r_mix, hot, firsts, tall, gated_t, grid_a, grid_b, spec_x, spec_g, spec_s, outer, gbranch,
    ssem_c, rsem_c, ssem_t, rsem_t, lsem,
):
    a = lax.axis_index("ctx")
    b = lax.axis_index("tp")

    def peer_of(axis, k):
        if axis == "tp":
            return lax.rem(b + k, NT)
        return lax.rem(a // 4 + k // 4, 2) * 4 + lax.rem(a % 4 + k % 4, 4)

    class Exchange:
        def __init__(self, axis, msg, src, dst):
            self.me, self.n = (a, NC) if axis == "ctx" else (b, NT)
            sends, recvs = (ssem_c, rsem_c) if axis == "ctx" else (ssem_t, rsem_t)

            def copy(k):
                peer = peer_of(axis, k)
                return pltpu.make_async_remote_copy(
                    src_ref=src(peer),
                    dst_ref=dst(self.me),
                    send_sem=sends.at[msg, k],
                    recv_sem=recvs.at[msg, k],
                    device_id={axis: peer},
                    device_id_type=MESH,
                )

            self.copy = copy

        def each(self, act, low=1, high=None):
            def body(k, carry):
                act(self.copy(k))
                return carry

            lax.fori_loop(low, high or self.n, body, 0)

        def start(self, low=1, high=None):
            self.each(lambda c: c.start(), low, high)

        def recv(self):
            self.each(lambda c: c.wait_recv())

        def drain(self):
            self.each(lambda c: c.wait_send())

    rows16 = lambda ref: (lambda p: ref.at[pl.ds(pl.multiple_of(p * 16, 16), 16), :])
    slot = lambda ref: (lambda p: ref.at[p])
    whole = lambda ref: (lambda p: ref)

    x_filt = Exchange("ctx", FILT_IN, rows16(filt_hbm), slot(r_filt))
    x_tok = Exchange("ctx", TOK, whole(tok_ref), slot(r_tok))
    x_gf = Exchange("ctx", GF, slot(s_gf), slot(r_gf))
    quarter = lambda ref, n: (lambda p: ref.at[p, pl.ds(n * 8, 8)])
    x_fl = lambda n: Exchange("ctx", FILT + n, quarter(s_fl, n), quarter(r_fl, n))
    x_fg = lambda n: Exchange("ctx", FG + n, quarter(s_fg, n), quarter(r_fg, n))
    x_fin = Exchange("ctx", FIN, whole(s_fin), slot(r_fin))
    x_back = Exchange("tp", BACK, slot(s_back), slot(r_back))
    x_tab = Exchange("tp", TAB, slot(s_tab), slot(r_tab))
    x_out = Exchange("tp", OUT, slot(s_out), slot(r_out))
    x_gt = Exchange("tp", GT, slot(s_gt), slot(r_gt))

    barrier = pltpu.get_barrier_semaphore()

    def greet(axis, n):
        def body(k, carry):
            pl.semaphore_signal(
                barrier, inc=1, device_id={axis: peer_of(axis, k)}, device_id_type=MESH
            )
            return carry

        lax.fori_loop(1, n, body, 0)

    greet("ctx", NC)
    greet("tp", NT)

    own = pl.ds(pl.multiple_of(a * 16, 16), 16)
    loads = {}
    for n, (name, src, dst) in enumerate(
        (
            ("emb", emb_hbm, emb_ref),
            ("gain", gain_hbm, gain_ref),
            ("blk", blk_hbm, blk_ref),
            ("omix", omix_hbm, omix_ref),
            ("cot", cot_hbm, cot_ref),
            ("tok", tok_hbm, tok_ref),
            ("mix", mix_hbm, mix_ref),
            ("oblk", oblk_hbm, oblk_ref),
            ("c1", c1_hbm, c1_ref),
            ("turn", turn_hbm, turn_ref),
            ("dft", dft_hbm, dft_ref),
            ("filt", filt_hbm.at[own, :], r_filt.at[a]),
        )
    ):
        loads[name] = pltpu.make_async_copy(src, dst, lsem.at[n])
        loads[name].start()

    row128, lane128 = iota2(128, 128)
    p_lane = lane128 >> 4
    row16, lane16 = iota2(16, 128)

    eye = ones_at(row128 == lane128).astype(BF)
    for name in ("emb", "gain", "blk"):
        loads[name].wait()
    gain_row = gain_ref[...]
    hi = gain_row.astype(BF).astype(F32)
    mid = (gain_row - hi).astype(BF).astype(F32)
    row8 = lax.broadcasted_iota(jnp.int32, (8, 128), 0)
    gains = jnp.where(row8 == 0, hi, jnp.where(row8 == 1, mid, gain_row - hi - mid))
    gains = jnp.where(row8 < 3, gains, 0.0)
    turned = [
        mm_tn(blk_ref[:, p * 128 : (p + 1) * 128], eye).reshape(NT, 8, 128) for p in range(3)
    ]
    turned.append(jnp.broadcast_to(gains[None], (NT, 8, 128)))
    s_tab[:, 0:32, :] = jnp.concatenate(turned, axis=1).astype(BF)
    s_tab[:, 32:48, :] = jnp.broadcast_to(emb_ref[...][None], (NT, 16, 128))

    loads["tok"].wait()
    pl.semaphore_wait(barrier, NC - 1 + NT - 1)
    x_tab.start()
    x_tok.start()
    r_tab[b] = s_tab[b]
    r_tok[a] = tok_ref[...]

    tile_m = ones_at((lane16 & 15) == row16).astype(BF)
    row, lane = iota2(256, 128)
    sel_row = ones_at(((row & 7) == (lane >> 4)) & ((row >> 4) == (lane & 15))).astype(BF)
    loads["omix"].wait()
    wide = mm(sel_row, mm(omix_ref[...], tile_m).astype(BF))
    row, lane = iota2(256, 256)
    keep = ((row & 7) == ((lane >> 4) & 7)) & (((row >> 3) & 1) == (lane >> 7))
    w_back[...] = jnp.where(keep, jnp.concatenate([wide, wide], axis=1), 0.0).astype(BF)
    loads["cot"].wait()
    cot2 = jnp.concatenate([cot_ref[:, :1024], cot_ref[:, 1024:]], axis=0)
    s_back[...] = mm(w_back[...], cot2).astype(BF).reshape(NT, 16, 1024)
    x_back.start()
    x_filt.start()
    r_back[b] = s_back[b]

    sel_p = ones_at(((row128 & 7) == p_lane) & ((row128 >> 3) == (lane128 & 15))).astype(BF)
    for name in ("mix", "oblk", "c1", "turn", "dft", "filt"):
        loads[name].wait()
    for p in range(3):
        wide = mm(sel_p, mm(mix_ref[p * 128 : (p + 1) * 128, :], tile_m).astype(BF))
        r_mix[p] = jnp.where((row128 & 7) == p_lane, wide, 0.0).astype(BF)

    row, lane = iota2(128, 256)
    sel_col = ones_at(((lane >> 4) * 8 + (lane & 7)) == row).astype(BF)
    wide = mm(oblk_ref[...], sel_col)
    low = ((lane >> 3) & 1) == 0
    w_two[...] = jnp.concatenate(
        [jnp.where(low, wide, 0.0), jnp.where(low, 0.0, wide)], axis=0
    ).astype(BF)

    x_tok.recv()
    for src in range(NC):
        ids = r_tok[src]
        for q in range(16):
            hot[src, :, q * 128 : (q + 1) * 128] = ones_at(
                jnp.broadcast_to(ids[q : q + 1, :], (16, 128)) == row16
            ).astype(BF)

    x_tab.recv()
    squares = jnp.zeros((16, 128), F32)
    for g in range(NT):
        part = r_tab[g, 32:48, :].astype(F32)
        squares += part * part
    scal_col = lax.rsqrt(jnp.sum(squares, axis=1, keepdims=True) * (1.0 / WIDTH) + EPS)
    scal_row = jnp.sum(
        jnp.where((lane16 & 15) == row16, scal_col, 0.0), axis=0, keepdims=True
    )
    pieces = []
    for g in range(NT):
        top = r_tab[g, 16:32, :].astype(F32)
        gain_g = top[8:9, :] + top[9:10, :] + top[10:11, :]
        normed = (r_tab[g, 32:48, :].astype(F32) * scal_col * gain_g).astype(BF)
        pieces.append(mm_nt(r_tab[g, 0:32, :], jnp.concatenate([normed] * 8, axis=0)))
    first = jnp.zeros((128, 128), F32)
    for p in range(3):
        part = jnp.concatenate([piece[p * 8 : (p + 1) * 8] for piece in pieces], axis=0)
        first += jnp.where(p_lane == p, part, 0.0)
    firsts[...] = first
    table = jnp.zeros((128, 128), F32)
    for p in range(3):
        table += mm_tn(r_mix[p], jnp.where(p_lane == p, first, 0.0).astype(BF))
    tall[...] = table
    gated_t[...] = table * pltpu.roll(table, 112, 1)
    outer_hi, outer_lo = split(pltpu.roll(table, 96, 1)[:, :16])
    outer_w = jnp.concatenate([outer_hi, outer_lo], axis=1)
    for h in range(2):
        hot_h = hot[a, :, h * 1024 : (h + 1) * 1024]
        outer[h * 128 : (h + 1) * 128, :] = mm(outer_w, jnp.concatenate([hot_h, hot_h], axis=0))
        embedded[h * 128 : (h + 1) * 128, :] = mm_tn(emb_ref[...], hot_h).astype(BF)

    mine = gated_t[pl.ds(pl.multiple_of(a * 16, 16), 16), :][:, :16].astype(BF)
    for src in range(NC):
        vals = mm(mine, hot[src])
        for q in range(16):
            grid_a[pl.ds(src * 16 + q, 16, stride=128), :] = vals[:, q * 128 : (q + 1) * 128]

    tc = turn_ref[:, :128]
    ts = turn_ref[:, 128:]
    c2_ref = dft_ref.at[0:256, :]
    i1_ref = dft_ref.at[256:512, :]
    i2_ref = dft_ref.at[512:640, :]
    tc2 = jnp.concatenate([tc, tc], axis=1)
    ts2 = jnp.concatenate([ts, ts], axis=1)

    def forward(signals, second):
        turned = []
        for u in range(0, len(signals), 2):
            stage = mm(c1_ref[...], jnp.concatenate(signals[u : u + 2], axis=1))
            re, im = stage[:128], stage[128:]
            tr = re * tc2 + im * ts2
            ti = im * tc2 - re * ts2
            for v in range(2):
                cols = slice(v * 128, (v + 1) * 128)
                turned.append(jnp.concatenate([tr[:, cols], ti[:, cols]], axis=1).astype(BF))
        return mm(jnp.concatenate(turned, axis=0), second)

    def inverse(spectrum, weights):
        back = mm(spectrum.astype(BF), weights)
        results = []
        for u in range(0, spectrum.shape[0], 256):
            both = [
                jnp.concatenate(
                    [back[u + v : u + v + 128, :128], back[u + v : u + v + 128, 128:]], axis=0
                )
                for v in (0, 128)
            ]
            both = jnp.concatenate(both, axis=1)
            re, im = both[:128], both[128:]
            turned = jnp.concatenate([re * tc2 - im * ts2, im * tc2 + re * ts2], axis=0)
            pair = mm(i2_ref[...], turned.astype(BF))
            results += [pair[:, :128], pair[:, 128:]]
        return results

    def groups(body):
        for n in range(2):
            body(n)

    def rows_of(n):
        return pl.ds(pl.multiple_of(n * 1024, 1024), 1024)

    def signals(ref, n):
        block = ref[rows_of(n), :].astype(BF)
        return [block[u * 128 : (u + 1) * 128] for u in range(8)]

    def gated_spectrum(n):
        spec_x[rows_of(n), :] = forward(signals(grid_a, n), c2_ref[...])

    groups(gated_spectrum)

    x_back.recv()
    gbranch[...] = mm(w_two[...], r_back[...].reshape(256, 1024))
    for h in range(2):
        for s in range(8):
            part = slice(s * 128, (s + 1) * 128)
            hrow = slice(h * 128, (h + 1) * 128)
            grid_a[pl.ds(h * 8 + s, 128, stride=16), :] = gbranch[hrow, part] * outer[hrow, part]
    s_gf[...] = grid_a[...].astype(BF).reshape(NC, 16, 16, 128)
    x_gf.start()
    r_gf[a] = s_gf[a]

    x_filt.recv()
    for src in range(NC):
        for q in range(16):
            grid_b[pl.ds(src * 16 + q, 16, stride=128), :] = r_filt[
                src, :, q * 128 : (q + 1) * 128
            ].astype(F32)

    def filtered_group(n):
        even = 2.0 * forward(signals(grid_b, n), c2_ref[:, :128])
        spec_s[rows_of(n), :] = even
        spectrum = spec_x[rows_of(n), :] * jnp.concatenate([even, even], axis=1)
        for u, result in enumerate(inverse(spectrum, i1_ref[...])):
            s_fl[:, n * 8 + u] = result.astype(BF).reshape(NC, 16, 128)
        x_fl(n).start()

    groups(filtered_group)
    r_fl[a] = s_fl[a]

    x_gf.recv()

    def grad_group(n):
        spectrum = forward([r_gf[:, n * 8 + u].reshape(128, 128) for u in range(8)], c2_ref[...])
        spec_g[rows_of(n), :] = spectrum
        prod = spectrum * spec_x[rows_of(n), :]
        cross = 2.0 * (prod[:, :128] + prod[:, 128:])
        for u, result in enumerate(inverse(cross, i1_ref[:128, :])):
            s_fg[:, n * 8 + u] = result.astype(BF).reshape(NC, 16, 128)
        x_fg(n).start()

    groups(grad_group)
    r_fg[a] = s_fg[a]

    def gated_group(n):
        even = spec_s[rows_of(n), :]
        spectrum = spec_g[rows_of(n), :] * jnp.concatenate([even, even], axis=1)
        for u, result in enumerate(inverse(spectrum, i1_ref[...])):
            start = pl.multiple_of(n * 1024 + u * 128, 128)
            grid_b[pl.ds(start, 128), :] = result

    groups(gated_group)
    sums = jnp.zeros((16, 32), F32)
    for src in range(NC):
        vals = jnp.concatenate(
            [grid_b[pl.ds(src * 16 + q, 16, stride=128), :] for q in range(16)], axis=1
        ).astype(BF)
        hot_s = hot[src]
        sums += mm_nt(vals, jnp.concatenate([hot_s, hot_s], axis=0))
    own_gg[...] = jnp.zeros((128, 128), F32)
    own_gg[own, :] = jnp.concatenate([sums, jnp.zeros((16, 96), F32)], axis=1)

    table = tall[...]
    swapped = jnp.where(lane128 < 16, pltpu.roll(table, 112, 1), pltpu.roll(table, 16, 1))
    grads = own_gg[...] * swapped
    early = jnp.zeros((128, 128), F32)
    for p in range(2):
        hi, lo = split(jnp.where(p_lane == p, grads, 0.0))
        early += mm(r_mix[p], hi) + mm(r_mix[p], lo)
    ctt = jnp.zeros((16, 128), F32)
    for h in range(2):
        cols = slice(h * 1024, (h + 1) * 1024)
        ctt += mm_nt(hot[a, :, cols], cot_ref[:, cols])

    for n in range(2):
        x_fl(n).recv()
    grid_a[...] = r_fl[...].reshape(2048, 128).astype(F32)
    gp2 = jnp.zeros((16, 128), F32)
    branch = []
    for h in range(2):
        hrow = slice(h * 128, (h + 1) * 128)
        filtered = jnp.concatenate(
            [grid_a[pl.ds(h * 8 + s, 128, stride=16), :] for s in range(8)], axis=1
        )
        branch.append((outer[hrow, :] * filtered).astype(BF))
        hot_h = hot[a, :, h * 1024 : (h + 1) * 1024]
        hi, lo = split(gbranch[hrow, :] * filtered)
        gp2 += mm_nt(hot_h, hi) + mm_nt(hot_h, lo)

    hi = gp2.astype(BF)
    rest = gp2 - hi.astype(F32)
    mid, low_part = split(rest)
    row48, lane48 = iota2(48, 128)
    place = ones_at(((row48 & 15) + 32) == lane48).astype(BF)
    gp2_t = mm_tn(jnp.concatenate([hi, mid, low_part], axis=0), place)
    hi, lo = split(gp2_t)
    gfirst = early + mm(r_mix[2], hi) + mm(r_mix[2], lo)
    share = jnp.sum(gfirst * firsts[...], axis=0, keepdims=True) / scal_row
    share = jnp.broadcast_to(share, (128, 128))
    share = pltpu.roll(share, 48, 1) + pltpu.roll(share, 32, 1) + pltpu.roll(share, 16, 1)
    s_gt[...] = jnp.where(
        lane128 < 48, gfirst, jnp.where(lane128 < 64, share, 0.0)
    ).reshape(NT, 8, 128)
    x_gt.start()
    r_gt[b] = s_gt[b]

    s_out[...] = (
        mm_tn(w_two[...], jnp.concatenate(branch, axis=0)).astype(BF).reshape(NT, 16, 1024)
    )
    x_out.start()
    r_out[b] = s_out[b]

    x_gt.recv()
    gt = r_gt[...].reshape(128, 128).T
    gnt = jnp.zeros((16, 128), F32)
    for p in range(3):
        hi, lo = split(gt[p * 16 : (p + 1) * 16, :])
        block = blk_ref[:, p * 128 : (p + 1) * 128]
        gnt += mm_nt(hi, block) + mm_nt(lo, block)
    cross = jnp.sum(gt[48:64, :], axis=1, keepdims=True) * 0.125
    emb = emb_ref[...].astype(F32)
    s_fin[16:24, :] = jnp.broadcast_to(
        jnp.sum(gnt * emb * scal_col, axis=0, keepdims=True), (8, 128)
    )
    s_fin[0:16, :] = (
        ctt
        + scal_col * gain_row * gnt
        - emb * (scal_col * scal_col * scal_col * cross * (1.0 / WIDTH))
    )
    x_fin.start()
    r_fin[a] = s_fin[...]
    for n in range(2):
        x_fg(n).recv()
    grid_a[...] = r_fg[...].reshape(2048, 128).astype(F32)
    for q in range(16):
        fgrad[:, q * 128 : (q + 1) * 128] = grid_a[pl.ds(q, 128, stride=16), :]
    x_fin.recv()
    small[...] = jnp.sum(r_fin[...], axis=0)
    x_out.recv()

    for exchange in (
        x_filt, x_tok, x_gf, x_fin, x_back, x_tab, x_out, x_gt,
        *[x_fl(n) for n in range(2)], *[x_fg(n) for n in range(2)],
    ):
        exchange.drain()


def finish(
    out_ref, fgrad_ref, w_ref, emb_ref, small_ref,
    lay_hbm, fgrad_hbm, egrad_ref, ggrad_ref,
    lay, sem,
):
    copies = [pltpu.make_async_copy(fgrad_ref, fgrad_hbm, sem.at[2])]
    copies[0].start()
    mixture = mm_tn(w_ref[...], out_ref[...].reshape(256, 1024))
    for h in range(2):
        hrow = slice(h * 128, (h + 1) * 128)
        cols = slice(h * 1024, (h + 1) * 1024)
        lay[:, cols] = (emb_ref[hrow].astype(F32) + mixture[hrow]).astype(BF)
        copies.append(pltpu.make_async_copy(lay.at[:, cols], lay_hbm.at[:, cols], sem.at[h]))
        copies[-1].start()
    egrad_ref[...] = small_ref[0:16, :]
    ggrad_ref[...] = small_ref[16:17, :]
    for copy in copies:
        copy.wait()


def local(token_ids, embedding, norm_gain, proj_blocks, proj_mixers, out_blocks, out_mixers, filters, cotangent):
    vmem = pl.BlockSpec(memory_space=pltpu.VMEM)
    hbm = pl.BlockSpec(memory_space=pltpu.HBM)
    V = pltpu.VMEM
    scratch = [
        V((16, 128), jnp.int32), V((16, 128), BF), V((1, 128), F32), V((128, 384), BF),
        V((384, 16), BF), V((128, 128), BF), V((128, 16), BF), V((128, 2048), BF),
        V((256, 128), BF), V((128, 256), F32), V((640, 256), BF),
        V((NC, 16, 2048), BF),
        V((NC, 16, 128), jnp.int32),
        V((NC, 16, 16, 128), BF), V((NC, 16, 16, 128), BF),
        V((NC, 16, 16, 128), BF), V((NC, 16, 16, 128), BF),
        V((NC, 16, 16, 128), BF), V((NC, 16, 16, 128), BF),
        V((128, 128), F32), V((24, 128), F32), V((NC, 24, 128), F32),
        V((NT, 16, 1024), BF), V((NT, 16, 1024), BF),
        V((NT, 48, 128), BF), V((NT, 48, 128), BF),
        V((NT, 16, 1024), BF),
        V((NT, 8, 128), F32), V((NT, 8, 128), F32),
        V((256, 256), BF), V((3, 128, 128), BF),
        V((NC, 16, 2048), BF),
        V((128, 128), F32), V((128, 128), F32), V((128, 128), F32),
        V((2048, 128), F32), V((2048, 128), F32),
        V((2048, 256), F32), V((2048, 256), F32), V((2048, 128), F32),
        V((256, 1024), F32), V((256, 1024), F32),
        pltpu.SemaphoreType.DMA((8, NC)), pltpu.SemaphoreType.DMA((8, NC)),
        pltpu.SemaphoreType.DMA((4, NT)), pltpu.SemaphoreType.DMA((4, NT)), pltpu.SemaphoreType.DMA((12,)),
    ]
    operands = (
        token_ids.reshape(16, 128),
        embedding,
        norm_gain.reshape(1, 128),
        proj_blocks.reshape(128, 384),
        proj_mixers.reshape(384, 16),
        out_blocks.reshape(128, 128),
        out_mixers.reshape(128, 16),
        filters,
        cotangent,
        *dft_tables(),
    )
    received = pl.pallas_call(
        kernel,
        out_shape=(
            jax.ShapeDtypeStruct((NT, 16, 1024), BF),
            jax.ShapeDtypeStruct((128, 2048), F32),
            jax.ShapeDtypeStruct((256, 256), BF),
            jax.ShapeDtypeStruct((256, 1024), BF),
            jax.ShapeDtypeStruct((24, 128), F32),
        ),
        in_specs=[hbm] * 12,
        out_specs=(vmem,) * 5,
        scratch_shapes=scratch,
        compiler_params=pltpu.CompilerParams(
            collective_id=0, has_side_effects=True, vmem_limit_bytes=40 * 1024 * 1024
        ),
    )(
        *[pltpu.with_memory_space_constraint(x, pltpu.HBM) for x in operands]
    )
    layer_out, filter_grad, embed_grad, gain_grad = pl.pallas_call(
        finish,
        out_shape=(
            jax.ShapeDtypeStruct((128, 2048), BF),
            jax.ShapeDtypeStruct((128, 2048), F32),
            jax.ShapeDtypeStruct((16, 128), F32),
            jax.ShapeDtypeStruct((1, 128), F32),
        ),
        in_specs=[vmem] * 5,
        out_specs=(hbm, hbm, vmem, vmem),
        scratch_shapes=[
            V((128, 2048), BF), pltpu.SemaphoreType.DMA((3,)),
        ],
        compiler_params=pltpu.CompilerParams(vmem_limit_bytes=16 * 1024 * 1024),
    )(*received)
    return layer_out, filter_grad, embed_grad, gain_grad.reshape(128)


def solution(mesh):
    in_specs = (
        P("ctx"),
        P(None, "tp"),
        P("tp"),
        P("tp", None, None),
        P(None, "tp", None, None),
        P("tp", None, None),
        P("tp", None, None),
        P("tp", "ctx"),
        P("tp", "ctx"),
    )
    out_specs = (P("tp", "ctx"), P("tp", "ctx"), P(None, "tp"), P("tp"))
    return jax.shard_map(local, mesh=mesh, in_specs=in_specs, out_specs=out_specs, check_vma=False)
```

```python
import jax
import jax.numpy as jnp
import numpy as np
from jax import lax
from jax.experimental import pallas as pl
from jax.experimental.pallas import tpu as pltpu
from jax.sharding import PartitionSpec as P

WIDTH = 2048
EPS = 1e-06
SPAN = 32768
NC = 8
NT = 16
BF = jnp.bfloat16
F32 = jnp.float32
MESH = pl.DeviceIdType.MESH

FILT_IN, TOK, GF, FIN, FILT, FG = 0, 1, 2, 3, 4, 6
BACK, TAB, OUT, GT = range(4)


def dft_tables():
    idx = np.arange(128)
    half = idx + 0.5
    first = 2 * np.pi * np.outer(half, idx) / 256.0
    c1 = np.concatenate([np.cos(first), -np.sin(first)], 0)
    twist = 2 * np.pi * np.outer(half, idx) / SPAN
    second = 2 * np.pi * (np.outer(idx, idx) % 128) / 128.0
    co, si = np.cos(second), np.sin(second)
    c2 = np.block([[co, -si], [si, co]])
    i1 = np.block([[co, si], [-si, co]])
    i2 = np.concatenate([np.cos(first.T), -np.sin(first.T)], 1) * (2.0 / SPAN)
    cast = lambda a, d: jnp.asarray(a, F32).astype(d)
    return (
        cast(c1, BF),
        cast(np.concatenate([np.cos(twist), np.sin(twist)], 1), F32),
        cast(np.concatenate([c2, i1, i2], 0), BF),
    )


def mm(a, b):
    return jnp.dot(a, b, preferred_element_type=F32)


def mm_tn(a, b):
    return lax.dot_general(a, b, (((0,), (0,)), ((), ())), preferred_element_type=F32)


def mm_nt(a, b):
    return lax.dot_general(a, b, (((1,), (1,)), ((), ())), preferred_element_type=F32)


def iota2(rows, lanes):
    return (
        lax.broadcasted_iota(jnp.int32, (rows, lanes), 0),
        lax.broadcasted_iota(jnp.int32, (rows, lanes), 1),
    )


def ones_at(cond):
    return jnp.where(cond, 1.0, 0.0).astype(F32)


def split(x):
    hi = x.astype(BF)
    return hi, (x - hi.astype(F32)).astype(BF)


def kernel(
    tok_hbm, emb_hbm, gain_hbm, blk_hbm, mix_hbm, oblk_hbm, omix_hbm, filt_hbm, cot_hbm,
    c1_hbm, turn_hbm, dft_hbm,
    r_out, fgrad, w_back, embedded, small,
    tok_ref, emb_ref, gain_ref, blk_ref, mix_ref, oblk_ref, omix_ref, cot_ref, c1_ref, turn_ref, dft_ref,
    r_filt, r_tok, s_gf, r_gf, s_fl, r_fl, s_fg, r_fg, own_gg, s_fin, r_fin,
    s_back, r_back, s_tab, r_tab, s_out, s_gt, r_gt,
    w_two, r_mix, hot, firsts, tall, gated_t, grid_a, grid_b, spec_x, spec_s, outer, gbranch,
    ssem_c, rsem_c, ssem_t, rsem_t, lsem,
):
    a = lax.axis_index("ctx")
    b = lax.axis_index("tp")

    def peer_of(axis, k):
        if axis == "tp":
            return lax.rem(b + k, NT)
        return lax.rem(a // 4 + k // 4, 2) * 4 + lax.rem(a % 4 + k % 4, 4)

    class Exchange:
        def __init__(self, axis, msg, src, dst):
            self.me, self.n = (a, NC) if axis == "ctx" else (b, NT)
            sends, recvs = (ssem_c, rsem_c) if axis == "ctx" else (ssem_t, rsem_t)

            def copy(k):
                peer = peer_of(axis, k)
                return pltpu.make_async_remote_copy(
                    src_ref=src(peer),
                    dst_ref=dst(self.me),
                    send_sem=sends.at[msg, k],
                    recv_sem=recvs.at[msg, k],
                    device_id={axis: peer},
                    device_id_type=MESH,
                )

            self.copy = copy

        def each(self, act, low=1, high=None):
            def body(k, carry):
                act(self.copy(k))
                return carry

            lax.fori_loop(low, high or self.n, body, 0)

        def start(self, low=1, high=None):
            self.each(lambda c: c.start(), low, high)

        def recv(self):
            self.each(lambda c: c.wait_recv())

        def drain(self):
            self.each(lambda c: c.wait_send())

    rows16 = lambda ref: (lambda p: ref.at[pl.ds(pl.multiple_of(p * 16, 16), 16), :])
    slot = lambda ref: (lambda p: ref.at[p])
    whole = lambda ref: (lambda p: ref)

    x_filt = Exchange("ctx", FILT_IN, rows16(filt_hbm), slot(r_filt))
    x_tok = Exchange("ctx", TOK, whole(tok_ref), slot(r_tok))
    x_gf = Exchange("ctx", GF, slot(s_gf), slot(r_gf))
    quarter = lambda ref, n: (lambda p: ref.at[p, pl.ds(n * 8, 8)])
    x_fl = lambda n: Exchange("ctx", FILT + n, quarter(s_fl, n), quarter(r_fl, n))
    x_fg = lambda n: Exchange("ctx", FG + n, quarter(s_fg, n), quarter(r_fg, n))
    x_fin = Exchange("ctx", FIN, whole(s_fin), slot(r_fin))
    x_back = Exchange("tp", BACK, slot(s_back), slot(r_back))
    x_tab = Exchange("tp", TAB, slot(s_tab), slot(r_tab))
    x_out = Exchange("tp", OUT, slot(s_out), slot(r_out))
    x_gt = Exchange("tp", GT, slot(s_gt), slot(r_gt))

    barrier = pltpu.get_barrier_semaphore()

    def greet(axis, n):
        def body(k, carry):
            pl.semaphore_signal(
                barrier, inc=1, device_id={axis: peer_of(axis, k)}, device_id_type=MESH
            )
            return carry

        lax.fori_loop(1, n, body, 0)

    greet("ctx", NC)
    greet("tp", NT)

    own = pl.ds(pl.multiple_of(a * 16, 16), 16)
    loads = {}
    for n, (name, src, dst) in enumerate(
        (
            ("emb", emb_hbm, emb_ref),
            ("gain", gain_hbm, gain_ref),
            ("blk", blk_hbm, blk_ref),
            ("omix", omix_hbm, omix_ref),
            ("cot", cot_hbm, cot_ref),
            ("tok", tok_hbm, tok_ref),
            ("mix", mix_hbm, mix_ref),
            ("oblk", oblk_hbm, oblk_ref),
            ("c1", c1_hbm, c1_ref),
            ("turn", turn_hbm, turn_ref),
            ("dft", dft_hbm, dft_ref),
            ("filt", filt_hbm.at[own, :], r_filt.at[a]),
        )
    ):
        loads[name] = pltpu.make_async_copy(src, dst, lsem.at[n])
        loads[name].start()

    row128, lane128 = iota2(128, 128)
    p_lane = lane128 >> 4
    row16, lane16 = iota2(16, 128)

    eye = ones_at(row128 == lane128).astype(BF)
    for name in ("emb", "gain", "blk"):
        loads[name].wait()
    gain_row = gain_ref[...]
    hi = gain_row.astype(BF).astype(F32)
    mid = (gain_row - hi).astype(BF).astype(F32)
    row8 = lax.broadcasted_iota(jnp.int32, (8, 128), 0)
    gains = jnp.where(row8 == 0, hi, jnp.where(row8 == 1, mid, gain_row - hi - mid))
    gains = jnp.where(row8 < 3, gains, 0.0)
    turned = [
        mm_tn(blk_ref[:, p * 128 : (p + 1) * 128], eye).reshape(NT, 8, 128) for p in range(3)
    ]
    turned.append(jnp.broadcast_to(gains[None], (NT, 8, 128)))
    s_tab[:, 0:32, :] = jnp.concatenate(turned, axis=1).astype(BF)
    s_tab[:, 32:48, :] = jnp.broadcast_to(emb_ref[...][None], (NT, 16, 128))

    loads["tok"].wait()
    pl.semaphore_wait(barrier, NC - 1 + NT - 1)
    x_tab.start()
    x_tok.start()
    r_tab[b] = s_tab[b]
    r_tok[a] = tok_ref[...]

    tile_m = ones_at((lane16 & 15) == row16).astype(BF)
    row, lane = iota2(256, 128)
    sel_row = ones_at(((row & 7) == (lane >> 4)) & ((row >> 4) == (lane & 15))).astype(BF)
    loads["omix"].wait()
    wide = mm(sel_row, mm(omix_ref[...], tile_m).astype(BF))
    row, lane = iota2(256, 256)
    keep = ((row & 7) == ((lane >> 4) & 7)) & (((row >> 3) & 1) == (lane >> 7))
    w_back[...] = jnp.where(keep, jnp.concatenate([wide, wide], axis=1), 0.0).astype(BF)
    loads["cot"].wait()
    cot2 = jnp.concatenate([cot_ref[:, :1024], cot_ref[:, 1024:]], axis=0)
    s_back[...] = mm(w_back[...], cot2).astype(BF).reshape(NT, 16, 1024)
    x_back.start()
    x_filt.start()
    r_back[b] = s_back[b]

    sel_p = ones_at(((row128 & 7) == p_lane) & ((row128 >> 3) == (lane128 & 15))).astype(BF)
    for name in ("mix", "oblk", "c1", "turn", "dft", "filt"):
        loads[name].wait()
    for p in range(3):
        wide = mm(sel_p, mm(mix_ref[p * 128 : (p + 1) * 128, :], tile_m).astype(BF))
        r_mix[p] = jnp.where((row128 & 7) == p_lane, wide, 0.0).astype(BF)

    row, lane = iota2(128, 256)
    sel_col = ones_at(((lane >> 4) * 8 + (lane & 7)) == row).astype(BF)
    wide = mm(oblk_ref[...], sel_col)
    low = ((lane >> 3) & 1) == 0
    w_two[...] = jnp.concatenate(
        [jnp.where(low, wide, 0.0), jnp.where(low, 0.0, wide)], axis=0
    ).astype(BF)

    x_tok.recv()
    for src in range(NC):
        ids = r_tok[src]
        for q in range(16):
            hot[src, :, q * 128 : (q + 1) * 128] = ones_at(
                jnp.broadcast_to(ids[q : q + 1, :], (16, 128)) == row16
            ).astype(BF)

    x_tab.recv()
    squares = jnp.zeros((16, 128), F32)
    for g in range(NT):
        part = r_tab[g, 32:48, :].astype(F32)
        squares += part * part
    scal_col = lax.rsqrt(jnp.sum(squares, axis=1, keepdims=True) * (1.0 / WIDTH) + EPS)
    scal_row = jnp.sum(
        jnp.where((lane16 & 15) == row16, scal_col, 0.0), axis=0, keepdims=True
    )
    pieces = []
    for g in range(NT):
        top = r_tab[g, 16:32, :].astype(F32)
        gain_g = top[8:9, :] + top[9:10, :] + top[10:11, :]
        normed = (r_tab[g, 32:48, :].astype(F32) * scal_col * gain_g).astype(BF)
        pieces.append(mm_nt(r_tab[g, 0:32, :], jnp.concatenate([normed] * 8, axis=0)))
    first = jnp.zeros((128, 128), F32)
    for p in range(3):
        part = jnp.concatenate([piece[p * 8 : (p + 1) * 8] for piece in pieces], axis=0)
        first += jnp.where(p_lane == p, part, 0.0)
    firsts[...] = first
    table = jnp.zeros((128, 128), F32)
    for p in range(3):
        table += mm_tn(r_mix[p], jnp.where(p_lane == p, first, 0.0).astype(BF))
    tall[...] = table
    gated_t[...] = table * pltpu.roll(table, 112, 1)
    outer_hi, outer_lo = split(pltpu.roll(table, 96, 1)[:, :16])
    outer_w = jnp.concatenate([outer_hi, outer_lo], axis=1)
    for h in range(2):
        hot_h = hot[a, :, h * 1024 : (h + 1) * 1024]
        outer[h * 128 : (h + 1) * 128, :] = mm(outer_w, jnp.concatenate([hot_h, hot_h], axis=0))
        embedded[h * 128 : (h + 1) * 128, :] = mm_tn(emb_ref[...], hot_h).astype(BF)

    mine = gated_t[pl.ds(pl.multiple_of(a * 16, 16), 16), :][:, :16].astype(BF)
    for src in range(NC):
        vals = mm(mine, hot[src])
        for q in range(16):
            grid_a[pl.ds(src * 16 + q, 16, stride=128), :] = vals[:, q * 128 : (q + 1) * 128]

    tc = turn_ref[:, :128]
    ts = turn_ref[:, 128:]
    c2_ref = dft_ref.at[0:256, :]
    i1_ref = dft_ref.at[256:512, :]
    i2_ref = dft_ref.at[512:640, :]
    tc2 = jnp.concatenate([tc, tc], axis=1)
    ts2 = jnp.concatenate([ts, ts], axis=1)

    def forward(signals, second):
        turned = []
        for u in range(0, len(signals), 2):
            stage = mm(c1_ref[...], jnp.concatenate(signals[u : u + 2], axis=1))
            re, im = stage[:128], stage[128:]
            tr = re * tc2 + im * ts2
            ti = im * tc2 - re * ts2
            for v in range(2):
                cols = slice(v * 128, (v + 1) * 128)
                turned.append(jnp.concatenate([tr[:, cols], ti[:, cols]], axis=1).astype(BF))
        return mm(jnp.concatenate(turned, axis=0), second)

    def inverse(spectrum, weights):
        back = mm(spectrum.astype(BF), weights)
        results = []
        for u in range(0, spectrum.shape[0], 256):
            both = [
                jnp.concatenate(
                    [back[u + v : u + v + 128, :128], back[u + v : u + v + 128, 128:]], axis=0
                )
                for v in (0, 128)
            ]
            both = jnp.concatenate(both, axis=1)
            re, im = both[:128], both[128:]
            turned = jnp.concatenate([re * tc2 - im * ts2, im * tc2 + re * ts2], axis=0)
            pair = mm(i2_ref[...], turned.astype(BF))
            results += [pair[:, :128], pair[:, 128:]]
        return results

    def groups(body):
        for n in range(2):
            body(n)

    def rows_of(n):
        return pl.ds(pl.multiple_of(n * 1024, 1024), 1024)

    def signals(ref, n):
        block = ref[rows_of(n), :].astype(BF)
        return [block[u * 128 : (u + 1) * 128] for u in range(8)]

    def gated_spectrum(n):
        spec_x[rows_of(n), :] = forward(signals(grid_a, n), c2_ref[...])

    groups(gated_spectrum)

    x_back.recv()
    gbranch[...] = mm(w_two[...], r_back[...].reshape(256, 1024))
    for h in range(2):
        for s in range(8):
            part = slice(s * 128, (s + 1) * 128)
            hrow = slice(h * 128, (h + 1) * 128)
            grid_a[pl.ds(h * 8 + s, 128, stride=16), :] = gbranch[hrow, part] * outer[hrow, part]
    s_gf[...] = grid_a[...].astype(BF).reshape(NC, 16, 16, 128)
    x_gf.start()
    r_gf[a] = s_gf[a]

    ctt = jnp.zeros((16, 128), F32)
    for h in range(2):
        cols = slice(h * 1024, (h + 1) * 1024)
        ctt += mm_nt(hot[a, :, cols], cot_ref[:, cols])

    x_filt.recv()
    for src in range(NC):
        for q in range(16):
            grid_b[pl.ds(src * 16 + q, 16, stride=128), :] = r_filt[
                src, :, q * 128 : (q + 1) * 128
            ].astype(F32)

    def filtered_group(n):
        even = 2.0 * forward(signals(grid_b, n), c2_ref[:, :128])
        spec_s[rows_of(n), :] = even
        spectrum = spec_x[rows_of(n), :] * jnp.concatenate([even, even], axis=1)
        for u, result in enumerate(inverse(spectrum, i1_ref[...])):
            s_fl[:, n * 8 + u] = result.astype(BF).reshape(NC, 16, 128)
        x_fl(n).start()

    groups(filtered_group)
    r_fl[a] = s_fl[a]

    x_gf.recv()

    def grad_group(n):
        spectrum = forward([r_gf[:, n * 8 + u].reshape(128, 128) for u in range(8)], c2_ref[...])
        prod = spectrum * spec_x[rows_of(n), :]
        cross = 2.0 * (prod[:, :128] + prod[:, 128:])
        for u, result in enumerate(inverse(cross, i1_ref[:128, :])):
            s_fg[:, n * 8 + u] = result.astype(BF).reshape(NC, 16, 128)
        x_fg(n).start()
        even = spec_s[rows_of(n), :]
        spectrum = spectrum * jnp.concatenate([even, even], axis=1)
        for u, result in enumerate(inverse(spectrum, i1_ref[...])):
            start = pl.multiple_of(n * 1024 + u * 128, 128)
            grid_b[pl.ds(start, 128), :] = result

    groups(grad_group)
    r_fg[a] = s_fg[a]

    sums = jnp.zeros((16, 32), F32)
    for src in range(NC):
        vals = jnp.concatenate(
            [grid_b[pl.ds(src * 16 + q, 16, stride=128), :] for q in range(16)], axis=1
        ).astype(BF)
        hot_s = hot[src]
        sums += mm_nt(vals, jnp.concatenate([hot_s, hot_s], axis=0))
    own_gg[...] = jnp.zeros((128, 128), F32)
    own_gg[own, :] = jnp.concatenate([sums, jnp.zeros((16, 96), F32)], axis=1)

    table = tall[...]
    swapped = jnp.where(lane128 < 16, pltpu.roll(table, 112, 1), pltpu.roll(table, 16, 1))
    grads = own_gg[...] * swapped
    early = jnp.zeros((128, 128), F32)
    for p in range(2):
        hi, lo = split(jnp.where(p_lane == p, grads, 0.0))
        early += mm(r_mix[p], hi) + mm(r_mix[p], lo)

    for n in range(2):
        x_fl(n).recv()
    grid_a[...] = r_fl[...].reshape(2048, 128).astype(F32)
    gp2 = jnp.zeros((16, 128), F32)
    branch = []
    for h in range(2):
        hrow = slice(h * 128, (h + 1) * 128)
        filtered = jnp.concatenate(
            [grid_a[pl.ds(h * 8 + s, 128, stride=16), :] for s in range(8)], axis=1
        )
        branch.append((outer[hrow, :] * filtered).astype(BF))
        hot_h = hot[a, :, h * 1024 : (h + 1) * 1024]
        hi, lo = split(gbranch[hrow, :] * filtered)
        gp2 += mm_nt(hot_h, hi) + mm_nt(hot_h, lo)

    hi = gp2.astype(BF)
    rest = gp2 - hi.astype(F32)
    mid, low_part = split(rest)
    row48, lane48 = iota2(48, 128)
    place = ones_at(((row48 & 15) + 32) == lane48).astype(BF)
    gp2_t = mm_tn(jnp.concatenate([hi, mid, low_part], axis=0), place)
    hi, lo = split(gp2_t)
    gfirst = early + mm(r_mix[2], hi) + mm(r_mix[2], lo)
    share = jnp.sum(gfirst * firsts[...], axis=0, keepdims=True) / scal_row
    share = jnp.broadcast_to(share, (128, 128))
    share = pltpu.roll(share, 48, 1) + pltpu.roll(share, 32, 1) + pltpu.roll(share, 16, 1)
    s_gt[...] = jnp.where(
        lane128 < 48, gfirst, jnp.where(lane128 < 64, share, 0.0)
    ).reshape(NT, 8, 128)
    x_gt.start()
    r_gt[b] = s_gt[b]

    s_out[...] = (
        mm_tn(w_two[...], jnp.concatenate(branch, axis=0)).astype(BF).reshape(NT, 16, 1024)
    )
    x_out.start()
    r_out[b] = s_out[b]

    x_gt.recv()
    gt = r_gt[...].reshape(128, 128).T
    gnt = jnp.zeros((16, 128), F32)
    for p in range(3):
        hi, lo = split(gt[p * 16 : (p + 1) * 16, :])
        block = blk_ref[:, p * 128 : (p + 1) * 128]
        gnt += mm_nt(hi, block) + mm_nt(lo, block)
    cross = jnp.sum(gt[48:64, :], axis=1, keepdims=True) * 0.125
    emb = emb_ref[...].astype(F32)
    s_fin[16:24, :] = jnp.broadcast_to(
        jnp.sum(gnt * emb * scal_col, axis=0, keepdims=True), (8, 128)
    )
    s_fin[0:16, :] = (
        ctt
        + scal_col * gain_row * gnt
        - emb * (scal_col * scal_col * scal_col * cross * (1.0 / WIDTH))
    )
    x_fin.start()
    r_fin[a] = s_fin[...]
    for n in range(2):
        x_fg(n).recv()
    grid_a[...] = r_fg[...].reshape(2048, 128).astype(F32)
    for q in range(16):
        fgrad[:, q * 128 : (q + 1) * 128] = grid_a[pl.ds(q, 128, stride=16), :]
    x_fin.recv()
    small[...] = jnp.sum(r_fin[...], axis=0)
    x_out.recv()

    for exchange in (
        x_filt, x_tok, x_gf, x_fin, x_back, x_tab, x_out, x_gt,
        *[x_fl(n) for n in range(2)], *[x_fg(n) for n in range(2)],
    ):
        exchange.drain()


def finish(
    out_ref, fgrad_ref, w_ref, emb_ref, small_ref,
    lay_hbm, fgrad_hbm, egrad_ref, ggrad_ref,
    lay, sem,
):
    copies = [pltpu.make_async_copy(fgrad_ref, fgrad_hbm, sem.at[2])]
    copies[0].start()
    mixture = mm_tn(w_ref[...], out_ref[...].reshape(256, 1024))
    for h in range(2):
        hrow = slice(h * 128, (h + 1) * 128)
        cols = slice(h * 1024, (h + 1) * 1024)
        lay[:, cols] = (emb_ref[hrow].astype(F32) + mixture[hrow]).astype(BF)
        copies.append(pltpu.make_async_copy(lay.at[:, cols], lay_hbm.at[:, cols], sem.at[h]))
        copies[-1].start()
    egrad_ref[...] = small_ref[0:16, :]
    ggrad_ref[...] = small_ref[16:17, :]
    for copy in copies:
        copy.wait()


def local(token_ids, embedding, norm_gain, proj_blocks, proj_mixers, out_blocks, out_mixers, filters, cotangent):
    vmem = pl.BlockSpec(memory_space=pltpu.VMEM)
    hbm = pl.BlockSpec(memory_space=pltpu.HBM)
    V = pltpu.VMEM
    scratch = [
        V((16, 128), jnp.int32), V((16, 128), BF), V((1, 128), F32), V((128, 384), BF),
        V((384, 16), BF), V((128, 128), BF), V((128, 16), BF), V((128, 2048), BF),
        V((256, 128), BF), V((128, 256), F32), V((640, 256), BF),
        V((NC, 16, 2048), BF),
        V((NC, 16, 128), jnp.int32),
        V((NC, 16, 16, 128), BF), V((NC, 16, 16, 128), BF),
        V((NC, 16, 16, 128), BF), V((NC, 16, 16, 128), BF),
        V((NC, 16, 16, 128), BF), V((NC, 16, 16, 128), BF),
        V((128, 128), F32), V((24, 128), F32), V((NC, 24, 128), F32),
        V((NT, 16, 1024), BF), V((NT, 16, 1024), BF),
        V((NT, 48, 128), BF), V((NT, 48, 128), BF),
        V((NT, 16, 1024), BF),
        V((NT, 8, 128), F32), V((NT, 8, 128), F32),
        V((256, 256), BF), V((3, 128, 128), BF),
        V((NC, 16, 2048), BF),
        V((128, 128), F32), V((128, 128), F32), V((128, 128), F32),
        V((2048, 128), F32), V((2048, 128), F32),
        V((2048, 256), F32), V((2048, 128), F32),
        V((256, 1024), F32), V((256, 1024), F32),
        pltpu.SemaphoreType.DMA((8, NC)), pltpu.SemaphoreType.DMA((8, NC)),
        pltpu.SemaphoreType.DMA((4, NT)), pltpu.SemaphoreType.DMA((4, NT)), pltpu.SemaphoreType.DMA((12,)),
    ]
    operands = (
        token_ids.reshape(16, 128),
        embedding,
        norm_gain.reshape(1, 128),
        proj_blocks.reshape(128, 384),
        proj_mixers.reshape(384, 16),
        out_blocks.reshape(128, 128),
        out_mixers.reshape(128, 16),
        filters,
        cotangent,
        *dft_tables(),
    )
    received = pl.pallas_call(
        kernel,
        out_shape=(
            jax.ShapeDtypeStruct((NT, 16, 1024), BF),
            jax.ShapeDtypeStruct((128, 2048), F32),
            jax.ShapeDtypeStruct((256, 256), BF),
            jax.ShapeDtypeStruct((256, 1024), BF),
            jax.ShapeDtypeStruct((24, 128), F32),
        ),
        in_specs=[hbm] * 12,
        out_specs=(vmem,) * 5,
        scratch_shapes=scratch,
        compiler_params=pltpu.CompilerParams(
            collective_id=0, has_side_effects=True, vmem_limit_bytes=40 * 1024 * 1024
        ),
    )(
        *[pltpu.with_memory_space_constraint(x, pltpu.HBM) for x in operands]
    )
    layer_out, filter_grad, embed_grad, gain_grad = pl.pallas_call(
        finish,
        out_shape=(
            jax.ShapeDtypeStruct((128, 2048), BF),
            jax.ShapeDtypeStruct((128, 2048), F32),
            jax.ShapeDtypeStruct((16, 128), F32),
            jax.ShapeDtypeStruct((1, 128), F32),
        ),
        in_specs=[vmem] * 5,
        out_specs=(hbm, hbm, vmem, vmem),
        scratch_shapes=[
            V((128, 2048), BF), pltpu.SemaphoreType.DMA((3,)),
        ],
        compiler_params=pltpu.CompilerParams(vmem_limit_bytes=16 * 1024 * 1024),
    )(*received)
    return layer_out, filter_grad, embed_grad, gain_grad.reshape(128)


def solution(mesh):
    in_specs = (
        P("ctx"),
        P(None, "tp"),
        P("tp"),
        P("tp", None, None),
        P(None, "tp", None, None),
        P("tp", None, None),
        P("tp", None, None),
        P("tp", "ctx"),
        P("tp", "ctx"),
    )
    out_specs = (P("tp", "ctx"), P("tp", "ctx"), P(None, "tp"), P("tp"))
    return jax.shard_map(local, mesh=mesh, in_specs=in_specs, out_specs=out_specs, check_vma=False)
```
